512 devices in a mesh: net: 128 (over z, y, core), scen: 4 (over x).
Axes of the slice: x: 4, y: 8, z: 8, core: 2. Of those that a mesh axis runs over, the one named last changes fastest.
Arguments:
- volt_mag: float32 [30720, 128], P('net', 'scen'), parts along dimension 1, may hold values from 0.94 to 1.06
- volt_ang: float32 [30720, 128], P('net', 'scen'), parts along dimension 1, may hold values from -0.5 to 0.5
- gradient: float32 [30720, 2, 128], P('net', None, 'scen'), parts along dimension 2, may hold values from -40 to 40
- branch_from: int32 [40960], P('net'), may hold values from 0 to 239, as said below
- branch_to: int32 [40960], P('net'), may hold values from 0 to 479, as said below
- branch_count: int32 [128], P('net'), may hold values from 160 to 320, as said below
- boundary: int32 [30720], P('net'), may hold values from 0 to 239, as said below
- conductance: float32 [40960], P('net'), may hold values from 0.2 to 2
- susceptance: float32 [40960], P('net'), may hold values from 1 to 10
- duals: float32 [2, 40960, 128], P(None, 'net', 'scen'), parts along dimension 2, may hold values from 0.02 to 0.2
- slacks: float32 [2, 40960, 128], P(None, 'net', 'scen'), parts along dimension 2, may hold values from 0.2 to 2
- gen_bus: int32 [5120], P('net'), may hold values from 0 to 239
- gen_curvature: float32 [5120], P('net'), may hold values from 1 to 10
Outputs:
- search_step: float32 [30720, 2, 128], P('net', None, 'scen'), parts along dimension 2
- residual: float32 [30720, 2, 128], P('net', None, 'scen'), parts along dimension 2
The draws below stay inside these ranges and needn't reach their ends.
There are 4 independent parts, one for each index of `scen`. The reference program is written for one: setup_inputs(seed, part) draws one part's arguments, and reference() takes and returns one part's arrays. A program takes and returns all parts, laid end to end along the dimension named above; an argument that names none is the same for every part. Nothing has to cross between parts.
Inputs may be any that keep to these rules, and one draw needn't show every extreme that they name: `branch_from`: A bus index within the branch's own device. A branch whose branch_to is 240 + e with e >= 0 starts at boundary entry e of its own device. `branch_to`: below 240: a bus of the same device other than the from-bus. 240 + e for e < 120: entry e of the previous device's list toward this device; 360 + e: entry e of the next device's list toward this device. Only the first 240 slots of a device end at a neighbour, each such value at most once a device; the first device has no ends of the first kind, the last none of the second. `branch_count`: slots at or past a device's count contribute nothing. Some device is full in every draw. `boundary`: per device 2 * 120 distinct local buses: the first 120 face the previous device, the rest the next device.
All inputs are finite; a program needn't handle non-finite values.
Results may differ from the reference program's by a relative error of at most 0.0003.
Values sent between devices are 32-bit elements; how exact they have to be, the bound alone decides.
A program may use at most 64 MiB of HBM per device.

```python
import math
import jax
import jax.numpy as jnp

B_DEV = 240
S = 32
ITERS = 4
BR_DEV = 320
GH = 120
GEN_DEV = 40
BUSES = 30720
BRANCHES = 40960
GENS = 5120
N_NET = 128


def network_layout(key):
    devices = BUSES // B_DEV
    key_lists = jax.random.fold_in(key, 101)
    key_order = jax.random.fold_in(key, 202)
    key_from = jax.random.fold_in(key, 303)
    key_to = jax.random.fold_in(key, 404)
    key_count = jax.random.fold_in(key, 505)
    key_full = jax.random.fold_in(key, 606)
    key_low = jax.random.fold_in(key, 707)
    lists = jax.vmap(lambda single: jax.random.permutation(single, B_DEV)[:2 * GH])(jax.random.split(key_lists, devices)).astype(jnp.int32)
    ghost_order = jax.vmap(lambda single: jax.random.permutation(single, 2 * GH))(jax.random.split(key_order, devices)).astype(jnp.int32)
    local_from = jax.random.randint(key_from, (devices, BR_DEV), 0, B_DEV).astype(jnp.int32)
    local_to = ((local_from + 1 + jax.random.randint(key_to, (devices, BR_DEV), 0, B_DEV - 1)) % B_DEV).astype(jnp.int32)
    slot_ids = jnp.arange(BR_DEV, dtype=jnp.int32)[None, :]
    device_ids = jnp.arange(devices, dtype=jnp.int32)[:, None]
    order_padded = jnp.concatenate([ghost_order, jnp.zeros((devices, BR_DEV - 2 * GH), jnp.int32)], axis=1)
    crossing = slot_ids < 2 * GH
    bad_first = (device_ids == 0) & (order_padded < GH)
    bad_last = (device_ids == devices - 1) & (order_padded >= GH)
    valid = crossing & jnp.logical_not(bad_first) & jnp.logical_not(bad_last)
    cross_from = jnp.take_along_axis(lists, order_padded, axis=1)
    from_all = jnp.where(valid, cross_from, local_from).astype(jnp.int32)
    to_all = jnp.where(valid, B_DEV + order_padded, local_to).astype(jnp.int32)
    counts = jax.random.randint(key_count, (devices,), BR_DEV // 2, BR_DEV + 1).astype(jnp.int32)
    full_dev = jax.random.randint(key_full, (), 0, devices)
    low_dev = (full_dev + 1 + jax.random.randint(key_low, (), 0, devices - 1)) % devices
    flat_ids = jnp.arange(devices, dtype=jnp.int32)
    counts = jnp.where(flat_ids == full_dev, BR_DEV, jnp.where(flat_ids == low_dev, BR_DEV // 2, counts)).astype(jnp.int32)
    return (from_all.reshape(-1), to_all.reshape(-1), counts, lists.reshape(-1))


def draw_branch_from(key, part):
    return network_layout(key)[0]


def draw_branch_to(key, part):
    return network_layout(key)[1]


def draw_branch_count(key, part):
    return network_layout(key)[2]


def draw_boundary(key, part):
    return network_layout(key)[3]


def draw_gradient(key, part):
    devices = BUSES // B_DEV
    key_bus = jax.random.fold_in(key, 11)
    key_scen = jax.random.fold_in(key, 12)
    key_rough = jax.random.fold_in(key, 13)
    position = (jnp.arange(BUSES) // B_DEV).astype(jnp.float32)
    ramp = (1.0 + 2.0 * position / max(devices - 1, 1))[:, None, None]
    scen_scale = jnp.exp(jax.random.uniform(key_scen, (1, 1, S), minval=0.0, maxval=math.log(4.0)))
    bus_scale = jnp.exp(jax.random.uniform(key_bus, (BUSES, 1, 1), minval=0.0, maxval=math.log(10.0)))
    values = 0.3 * ramp * bus_scale * scen_scale * jax.random.normal(key_rough, (BUSES, 2, S))
    return jnp.clip(values, -40.0, 40.0).astype(jnp.float32)


def place_ends(entries, own_key, least, high):
    spot = [jax.random.randint(jax.random.fold_in(own_key, axis), (), 0, length) for axis, length in enumerate(entries.shape)]
    main_axis = entries.shape.index(max(entries.shape))
    next_to = spot[:main_axis] + [(spot[main_axis] + 1) % entries.shape[main_axis]] + spot[main_axis + 1:]
    return entries.at[tuple(spot)].set(least).at[tuple(next_to)].set(high)


def block_scale(own_key, extent, shards, smallest, largest):
    gain, own = 1.0, jax.random.fold_in(own_key, 6)
    for dim, shards_of in shards:
        draws = jnp.exp(jax.random.uniform(jax.random.fold_in(own, dim), (shards_of,), jnp.float32, smallest / len(shards), largest / len(shards)))
        gain = gain * jnp.repeat(draws, extent[dim] // shards_of).reshape([-1 if axis == dim else 1 for axis in range(len(extent))])
    return gain


def setup_inputs(seed: int = 0, part: int = 0) -> dict:
    streams_of = jax.random.split(jax.random.key(seed), 14)
    own_keys = jax.random.split(jax.random.fold_in(streams_of[13], part), 14)
    volt_mag = jnp.clip(0.94 + 0.119999945 * jax.random.uniform(own_keys[0], (BUSES, S), jnp.float32) ** block_scale(own_keys[0], (BUSES, S), ((0, 128),), -0.2, 0.2), 0.94, 1.06)
    volt_ang = jnp.clip(jax.random.uniform(own_keys[1], (BUSES, S), jnp.float32, -0.5, 0.5) * block_scale(own_keys[1], (BUSES, S), ((0, 128),), -0.4, 0.0), -0.5, 0.5)
    gradient = draw_gradient(jax.random.fold_in(jax.random.fold_in(streams_of[13], part), 71), part)
    branch_from = draw_branch_from(jax.random.fold_in(streams_of[13], 71), part)
    branch_to = draw_branch_to(jax.random.fold_in(streams_of[13], 71), part)
    branch_count = draw_branch_count(jax.random.fold_in(streams_of[13], 71), part)
    boundary = draw_boundary(jax.random.fold_in(streams_of[13], 71), part)
    conductance = jnp.clip(jnp.exp(math.log(2.0) - 2.3025851 * jax.random.uniform(streams_of[7], (BRANCHES,), jnp.float32) ** block_scale(streams_of[7], (BRANCHES,), ((0, 128),), -0.2, 0.2)), 0.2, 2.0)
    susceptance = jnp.clip(jnp.exp(math.log(10.0) - 2.3025851 * jax.random.uniform(streams_of[8], (BRANCHES,), jnp.float32) ** block_scale(streams_of[8], (BRANCHES,), ((0, 128),), -0.2, 0.2)), 1.0, 10.0)
    duals = jnp.clip(jnp.exp(math.log(0.2) - 2.3025851 * jax.random.uniform(own_keys[9], (2, BRANCHES, S), jnp.float32) ** block_scale(own_keys[9], (2, BRANCHES, S), ((1, 128),), -0.2, 0.2)), 0.02, 0.2)
    slacks = jnp.clip(jnp.exp(math.log(2.0) - 2.3025851 * jax.random.uniform(own_keys[10], (2, BRANCHES, S), jnp.float32) ** block_scale(own_keys[10], (2, BRANCHES, S), ((1, 128),), -0.2, 0.2)), 0.2, 2.0)
    gen_bus = place_ends(jax.random.randint(streams_of[11], (GENS,), 0, B_DEV), jax.random.fold_in(streams_of[11], 1), 0, B_DEV - 1).astype(jnp.int32)
    gen_curvature = jnp.clip(jnp.exp(math.log(10.0) - 2.3025851 * jax.random.uniform(streams_of[12], (GENS,), jnp.float32) ** block_scale(streams_of[12], (GENS,), ((0, 128),), -0.2, 0.2)), 1.0, 10.0)
    return {"volt_mag": volt_mag, "volt_ang": volt_ang, "gradient": gradient, "branch_from": branch_from, "branch_to": branch_to, "branch_count": branch_count, "boundary": boundary, "conductance": conductance, "susceptance": susceptance, "duals": duals, "slacks": slacks, "gen_bus": gen_bus, "gen_curvature": gen_curvature}


barrier_weight = 0.01
volt_low = 0.9
volt_high = 1.1
angle_reg = 0.5


def branch_blocks(magnitude_from, angle_from, magnitude_to, angle_to, conduct, suscept, weight_active, weight_reactive):
    angle_diff = angle_from - angle_to
    cosine_diff = jnp.cos(angle_diff)
    sine_diff = jnp.sin(angle_diff)
    flow_along = conduct * cosine_diff + suscept * sine_diff
    flow_across = conduct * sine_diff - suscept * cosine_diff
    cross_term = magnitude_from * magnitude_to
    active_rows = (2.0 * conduct * magnitude_from - magnitude_to * flow_along, cross_term * flow_across,
                   -magnitude_from * flow_along, -cross_term * flow_across)
    reactive_rows = (-2.0 * suscept * magnitude_from - magnitude_to * flow_across, -cross_term * flow_along,
                     -magnitude_from * flow_across, cross_term * flow_along)

    def block_entry(left_index, right_index):
        return (weight_active * active_rows[left_index] * active_rows[right_index]
                + weight_reactive * reactive_rows[left_index] * reactive_rows[right_index])

    from_block = jnp.stack([block_entry(0, 0), block_entry(0, 1), block_entry(1, 1)], axis=1)
    to_block = jnp.stack([block_entry(2, 2), block_entry(2, 3), block_entry(3, 3)], axis=1)
    cross_block = jnp.stack([block_entry(0, 2), block_entry(0, 3), block_entry(1, 2), block_entry(1, 3)], axis=1)
    return from_block, to_block, cross_block


def apply_cross(matrix_block, vector):
    return jnp.stack([matrix_block[:, 0] * vector[:, 0] + matrix_block[:, 1] * vector[:, 1],
                      matrix_block[:, 2] * vector[:, 0] + matrix_block[:, 3] * vector[:, 1]], axis=1)


def apply_cross_transposed(matrix_block, vector):
    return jnp.stack([matrix_block[:, 0] * vector[:, 0] + matrix_block[:, 2] * vector[:, 1],
                      matrix_block[:, 1] * vector[:, 0] + matrix_block[:, 3] * vector[:, 1]], axis=1)


def reference(volt_mag, volt_ang, gradient, branch_from, branch_to, branch_count, boundary, conductance, susceptance, duals, slacks, gen_bus, gen_curvature):
    slot_ids = jnp.arange(BRANCHES, dtype=jnp.int32)
    owner_dev = slot_ids // BR_DEV
    from_bus = (owner_dev * B_DEV + branch_from).astype(jnp.int32)
    bound_table = boundary.reshape(N_NET, 2 * GH)
    offset = branch_to - B_DEV
    prev_owner = jnp.clip(owner_dev - 1, 0, N_NET - 1)
    next_owner = jnp.clip(owner_dev + 1, 0, N_NET - 1)
    prev_bus = prev_owner * B_DEV + bound_table[prev_owner, jnp.clip(offset + GH, 0, 2 * GH - 1)]
    next_bus = next_owner * B_DEV + bound_table[next_owner, jnp.clip(offset - GH, 0, 2 * GH - 1)]
    to_bus = jnp.where(branch_to < B_DEV, owner_dev * B_DEV + branch_to,
                       jnp.where(offset < GH, prev_bus, next_bus)).astype(jnp.int32)
    live_mask = ((slot_ids % BR_DEV) < branch_count[owner_dev]).astype(jnp.float32)[:, None]
    weight_active = live_mask * duals[0] / slacks[0]
    weight_reactive = live_mask * duals[1] / slacks[1]
    from_block, to_block, cross_block = branch_blocks(
        volt_mag[from_bus], volt_ang[from_bus], volt_mag[to_bus], volt_ang[to_bus],
        conductance[:, None], susceptance[:, None], weight_active, weight_reactive)
    diag_sum = (jax.ops.segment_sum(from_block, from_bus, num_segments=BUSES)
                + jax.ops.segment_sum(to_block, to_bus, num_segments=BUSES))
    gen_owner = jnp.arange(GENS, dtype=jnp.int32) // GEN_DEV
    gen_sum = jax.ops.segment_sum(gen_curvature, (gen_owner * B_DEV + gen_bus).astype(jnp.int32), num_segments=BUSES)[:, None]
    barrier = barrier_weight / jnp.square(volt_mag - volt_low) + barrier_weight / jnp.square(volt_high - volt_mag)
    diag_vv = diag_sum[:, 0] + barrier + gen_sum
    diag_va = diag_sum[:, 1]
    diag_aa = diag_sum[:, 2] + angle_reg + gen_sum
    determinant = diag_vv * diag_aa - diag_va * diag_va
    inverse_vv = diag_aa / determinant
    inverse_va = -diag_va / determinant
    inverse_aa = diag_vv / determinant

    def precondition(vector):
        return jnp.stack([inverse_vv * vector[:, 0] + inverse_va * vector[:, 1],
                          inverse_va * vector[:, 0] + inverse_aa * vector[:, 1]], axis=1)

    def apply_matrix(vector):
        result = jnp.stack([diag_vv * vector[:, 0] + diag_va * vector[:, 1],
                            diag_va * vector[:, 0] + diag_aa * vector[:, 1]], axis=1)
        from_terms = apply_cross(cross_block, vector[to_bus])
        to_terms = apply_cross_transposed(cross_block, vector[from_bus])
        return (result + jax.ops.segment_sum(from_terms, from_bus, num_segments=BUSES)
                + jax.ops.segment_sum(to_terms, to_bus, num_segments=BUSES))

    def scenario_sum(left_vec, right_vec):
        return jnp.sum(left_vec * right_vec, axis=(0, 1))

    update_field = jnp.zeros_like(gradient)
    residual = gradient
    scaled = precondition(residual)
    search = scaled
    energy = scenario_sum(residual, scaled)
    for iteration in range(ITERS):
        matrix_image = apply_matrix(search)
        step_size = energy / scenario_sum(search, matrix_image)
        update_field = update_field + step_size[None, None, :] * search
        residual = residual - step_size[None, None, :] * matrix_image
        if iteration + 1 < ITERS:
            scaled = precondition(residual)
            energy_next = scenario_sum(residual, scaled)
            search = scaled + (energy_next / energy)[None, None, :] * search
            energy = energy_next
    return update_field, residual
```

```python
import functools

import jax
import jax.numpy as jnp
from jax import lax
from jax.experimental import pallas as pl
from jax.experimental.pallas import tpu as pltpu
from jax.sharding import PartitionSpec as P

MESH = pl.DeviceIdType.MESH
F32, BF16 = jnp.float32, jnp.bfloat16
ITERS = 4
LANES = 128

barrier_weight = 0.01
volt_low = 0.9
volt_high = 1.1
angle_reg = 0.5


def sine_cosine(angle):
    square = angle * angle
    sine = 1.0 / 6227020800.0
    for term in (-1.0 / 39916800.0, 1.0 / 362880.0, -1.0 / 5040.0, 1.0 / 120.0, -1.0 / 6.0, 1.0):
        sine = sine * square + term
    cosine = -1.0 / 87178291200.0
    for term in (1.0 / 479001600.0, -1.0 / 3628800.0, 1.0 / 40320.0, -1.0 / 720.0, 1.0 / 24.0, -0.5, 1.0):
        cosine = cosine * square + term
    return sine * angle, cosine


def branch_blocks(mag_from, mag_to, sine, cosine, conduct, suscept, weight_p, weight_q):
    along = conduct * cosine + suscept * sine
    across = conduct * sine - suscept * cosine
    cross = mag_from * mag_to
    jp = (2.0 * conduct * mag_from - mag_to * along, cross * across, -mag_from * along, -cross * across)
    jq = (-2.0 * suscept * mag_from - mag_to * across, -cross * along, -mag_from * across, cross * along)
    wp = [weight_p * j for j in jp]
    wq = [weight_q * j for j in jq]

    def entry(i, j):
        return wp[i] * jp[j] + wq[i] * jq[j]

    return (
        (entry(0, 0), entry(0, 1), entry(1, 1)),
        (entry(2, 2), entry(2, 3), entry(3, 3)),
        (entry(0, 2), entry(0, 3), entry(1, 2), entry(1, 3)),
    )


def pieces(values, terms):
    out = []
    for _ in range(terms - 1):
        head = values.astype(BF16)
        out.append(head)
        values = values - head.astype(F32)
    return jnp.concatenate(out + [values.astype(BF16)], axis=0)


def select_dot(values, table, terms):
    rows = values.shape[0]
    out = jnp.dot(pieces(values, terms), table, preferred_element_type=F32)
    total = out[(terms - 1) * rows :]
    for k in range(terms - 2, -1, -1):
        total = total + out[k * rows : (k + 1) * rows]
    return total


def inner(left, right):
    product = left * right
    half = product.shape[0] // 2
    product = product[:half] + product[half:]
    product = product[:, :LANES] + product[:, LANES:]
    return jnp.sum(product, axis=1, keepdims=True)


def pack(sums):
    lane = lax.broadcasted_iota(jnp.int32, (8, LANES), 1)
    tile = jnp.zeros((8, LANES), F32)
    for m, column in enumerate(sums):
        for g in range(4):
            tile = jnp.where(lane == 4 * m + g, column[8 * g : 8 * g + 8], tile)
    return tile


def unpack(tile):
    return jnp.concatenate([tile[:, g : g + 1] for g in range(4)], axis=0)


def galerkin(gram, rhs, n):
    a = {(i, j): gram[(min(i, j), max(i, j))] for i in range(n) for j in range(n)}
    rhs = list(rhs)
    low, inv = {}, {}
    for k in range(n):
        live = a[(k, k)] > 1e-7 * gram[(k, k)]
        inv[k] = jnp.where(live, 1.0 / jnp.where(live, a[(k, k)], 1.0), 0.0)
        for i in range(k + 1, n):
            low[(i, k)] = a[(i, k)] * inv[k]
            for j in range(k + 1, i + 1):
                a[(i, j)] = a[(i, j)] - low[(i, k)] * a[(j, k)]
                a[(j, i)] = a[(i, j)]
            rhs[i] = rhs[i] - low[(i, k)] * rhs[k]
    out = [None] * n
    for k in reversed(range(n)):
        value = rhs[k] * inv[k]
        for i in range(k + 1, n):
            value = value - low[(i, k)] * out[i]
        out[k] = value
    return out


def kernel(
    n,
    group,
    vm_ref,
    va_ref,
    grad_ref,
    from_ref,
    to_ref,
    count_ref,
    bound_ref,
    g_ref,
    b_ref,
    dual_ref,
    slack_ref,
    gbus_ref,
    gcur_ref,
    x_ref,
    r_ref,
    irow,
    frow,
    vin,
    gather_tab,
    scatter_tab,
    pay_out,
    pay_in,
    halo_out,
    halo_in,
    red_a,
    red_b,
    pay_send,
    pay_recv,
    halo_send,
    halo_recv,
    a_send,
    a_recv,
    b_send,
    b_recv,
):
    scen, buses = vm_ref.shape
    slots = from_ref.shape[1]
    ghost = buses // 2
    wide = 2 * LANES
    span = gather_tab.shape[1] // 2
    gens = gbus_ref.shape[1]
    outer = n // group
    me = lax.axis_index("net")
    prev, nxt = lax.rem(me + n - 1, n), lax.rem(me + 1, n)
    inside = lax.rem(me, group)
    block = lax.div(me, group)
    peers_a = [block * group + lax.rem(inside + d, group) for d in range(1, group)]
    peers_b = [lax.rem(block + d, outer) * group + inside for d in range(1, outer)]

    barrier = pltpu.get_barrier_semaphore()
    for peer in (prev, nxt, *peers_a, *peers_b):
        pl.semaphore_signal(barrier, inc=1, device_id={"net": peer}, device_id_type=MESH)

    def exchange(source, target, send, recv):
        out = []
        for half, peer in ((0, prev), (1, nxt)):
            copy = pltpu.make_async_remote_copy(
                src_ref=source.at[half],
                dst_ref=target.at[1 - half],
                send_sem=send.at[half],
                recv_sem=recv.at[half],
                device_id={"net": peer},
                device_id_type=MESH,
            )
            copy.start()
            out.append(copy)
        return out

    irow[...] = jnp.full(irow.shape, -1.0, F32)
    irow[0:1, :slots] = from_ref[...].astype(F32)
    irow[1:2, :slots] = to_ref[...].astype(F32)
    irow[2:3, :buses] = bound_ref[...].astype(F32)
    irow[3:4, :gens] = gbus_ref[...].astype(F32)
    frow[...] = jnp.zeros(frow.shape, F32)
    frow[0:1, :slots] = g_ref[...]
    frow[1:2, :slots] = b_ref[...]
    frow[2:3, :gens] = gcur_ref[...]
    from_row, to_row = irow[0:1, :], irow[1:2, :]
    lane_i = lax.broadcasted_iota(jnp.int32, (8, wide), 1)
    lane = lane_i.astype(F32)
    plain = irow[0:8, :wide]
    rolled = pltpu.roll(plain, LANES - ghost, 1)
    upper = (lane_i >= LANES) & (lane_i < LANES + ghost)
    place = jnp.where(lane_i < ghost, plain, jnp.where(upper, rolled, -2.0))[2:3]
    entry = jnp.where(lane_i < ghost, lane, jnp.where(upper, lane - (LANES - ghost), -1e6))[0:1]

    def column(row):
        return jnp.transpose(jnp.broadcast_to(row, (LANES, row.shape[1])))

    def hot(mask):
        return jnp.where(mask, 1.0, 0.0).astype(BF16)

    place_col, from_col, to_col = column(place), column(from_row), column(to_row)
    lanes_of = lambda row, t: row[:, t * LANES : (t + 1) * LANES]
    for t in range(span // LANES):
        gather_tab[:, t * LANES : (t + 1) * LANES] = hot(place_col == lanes_of(from_row, t))
        gather_tab[:, span + t * LANES : span + (t + 1) * LANES] = hot(place_col == lanes_of(to_row, t))
    for t in range(2):
        cols = slice(t * LANES, (t + 1) * LANES)
        scatter_tab[0:span, cols] = hot(from_col == lanes_of(place, t))
        scatter_tab[span:, cols] = hot(to_col == lanes_of(place, t))
    cross_tab = jnp.concatenate([hot(to_col == lanes_of(entry, t) + buses) for t in range(2)], axis=1)
    bus_row = lane[0:1]
    bus_col = lax.broadcasted_iota(jnp.int32, (wide, LANES), 0).astype(F32)
    to_place = jnp.concatenate([hot(bus_col == lanes_of(place, t)) for t in range(2)], axis=1)
    to_bus = jnp.concatenate([hot(place_col == lanes_of(bus_row, t)) for t in range(2)], axis=1)

    vin[...] = jnp.zeros(vin.shape, F32)
    vin[0:scen, :buses] = vm_ref[...]
    vin[scen : 2 * scen, :buses] = va_ref[...]
    vin[2 * scen : 3 * scen, :buses] = grad_ref[0]
    vin[3 * scen : 4 * scen, :buses] = grad_ref[1]
    placed = select_dot(vin[...], to_place, 3)
    vm, va, start = placed[0:scen], placed[scen : 2 * scen], placed[2 * scen :]

    slot = lax.broadcasted_iota(jnp.int32, (1, slots), 1)
    live = jnp.where(slot < count_ref[...], 1.0, 0.0)
    pad = jnp.zeros((scen, span - slots), F32)
    weight_p = jnp.concatenate([live * dual_ref[0] / slack_ref[0], pad], axis=1)
    weight_q = jnp.concatenate([live * dual_ref[1] / slack_ref[1], pad], axis=1)
    conduct, suscept = frow[0:1, :], frow[1:2, :]
    stacked = jnp.concatenate([weight_p, weight_q, frow[0:8, :]], axis=0)
    crossing = select_dot(stacked, cross_tab, 3)
    payload = jnp.concatenate([vm, va, crossing], axis=0)
    for half in range(2):
        pay_out[half] = payload[:, half * LANES : (half + 1) * LANES]

    pl.semaphore_wait(barrier, 2 + (group - 1) + (outer - 1))
    pay_copies = exchange(pay_out, pay_in, pay_send, pay_recv)

    ends = select_dot(placed[0 : 2 * scen], gather_tab[...], 3)
    local = jnp.where((to_row >= 0.0) & (to_row < float(buses)), 1.0, 0.0)
    sine, cosine = sine_cosine(ends[scen:, :span] - ends[scen:, span:])
    hff, htt, (h00, h01, h10, h11) = branch_blocks(
        ends[:scen, :span], ends[:scen, span:], sine, cosine, conduct, suscept, weight_p * local, weight_q * local
    )
    both = jnp.concatenate([jnp.concatenate([a, b], axis=1) for a, b in zip(hff, htt)], axis=0)
    diag = select_dot(both, scatter_tab[...], 3)
    gen = column(irow[3:4, :LANES])
    curve = column(frow[2:3, :LANES])
    gen_sum = jnp.concatenate(
        [jnp.sum(jnp.where(gen == lanes_of(place, t), curve, 0.0), axis=0, keepdims=True) for t in range(2)], axis=1
    )
    low, high = vm - volt_low, volt_high - vm
    base_vv = barrier_weight / (low * low) + barrier_weight / (high * high) + gen_sum
    base_aa = angle_reg + gen_sum

    for copy in pay_copies:
        copy.wait()
    arrived = jnp.concatenate([pay_in[0], pay_in[1]], axis=1)
    there_vm, there_va = arrived[0:scen], arrived[scen : 2 * scen]
    there_p, there_q = arrived[2 * scen : 3 * scen], arrived[3 * scen : 4 * scen]
    there_g, there_b = arrived[4 * scen : 4 * scen + 1], arrived[4 * scen + 1 : 4 * scen + 2]
    here_p, here_q = crossing[0:scen], crossing[scen : 2 * scen]
    here_g, here_b = crossing[2 * scen : 2 * scen + 1], crossing[2 * scen + 1 : 2 * scen + 2]
    sine, cosine = sine_cosine(va - there_va)
    off, _, (o00, o01, o10, o11) = branch_blocks(vm, there_vm, sine, cosine, here_g, here_b, here_p, here_q)
    _, on, (i00, i01, i10, i11) = branch_blocks(there_vm, vm, -sine, cosine, there_g, there_b, there_p, there_q)
    c00, c01, c10, c11 = o00 + i00, o01 + i10, o10 + i01, o11 + i11
    d00 = diag[0:scen] + off[0] + on[0] + base_vv
    d01 = diag[scen : 2 * scen] + off[1] + on[1]
    d11 = diag[2 * scen :] + off[2] + on[2] + base_aa
    inverse = 1.0 / (d00 * d11 - d01 * d01)
    p00, p01, p11 = d11 * inverse, -d01 * inverse, d00 * inverse

    def precondition(v):
        return jnp.concatenate([p00 * v[:scen] + p01 * v[scen:], p01 * v[:scen] + p11 * v[scen:]], axis=0)

    s, u = [start], [precondition(start)]
    for j in range(ITERS):
        v = u[j]
        halo_out[j, 0] = v[:, :LANES]
        halo_out[j, 1] = v[:, LANES:]
        copies = exchange(halo_out.at[j], halo_in.at[j], halo_send.at[j], halo_recv.at[j])
        ends = select_dot(v, gather_tab[...], 2)
        f0, f1, t0, t1 = ends[:scen, :span], ends[scen:, :span], ends[:scen, span:], ends[scen:, span:]
        terms = jnp.concatenate(
            [
                jnp.concatenate([h00 * t0 + h01 * t1, h00 * f0 + h10 * f1], axis=1),
                jnp.concatenate([h10 * t0 + h11 * t1, h01 * f0 + h11 * f1], axis=1),
            ],
            axis=0,
        )
        inside_sum = select_dot(terms, scatter_tab[...], 2)
        for copy in copies:
            copy.wait()
        n0 = jnp.concatenate([halo_in[j, 0, :scen], halo_in[j, 1, :scen]], axis=1)
        n1 = jnp.concatenate([halo_in[j, 0, scen:], halo_in[j, 1, scen:]], axis=1)
        s.append(inside_sum + jnp.concatenate([c00 * n0 + c01 * n1, c10 * n0 + c11 * n1], axis=0))
        if j + 1 < ITERS:
            u.append(precondition(s[-1]))

    def all_sum(tile):
        red_a[pl.ds(inside, 1)] = tile[None]
        copies = []
        for d, peer in enumerate(peers_a):
            copy = pltpu.make_async_remote_copy(
                src_ref=red_a.at[inside],
                dst_ref=red_a.at[inside],
                send_sem=a_send.at[d],
                recv_sem=a_recv.at[d],
                device_id={"net": peer},
                device_id_type=MESH,
            )
            copy.start()
            copies.append(copy)
        for copy in copies:
            copy.wait()
        total = red_a[0]
        for k in range(1, group):
            total = total + red_a[k]
        red_b[pl.ds(block, 1)] = total[None]
        copies = []
        for d, peer in enumerate(peers_b):
            copy = pltpu.make_async_remote_copy(
                src_ref=red_b.at[block],
                dst_ref=red_b.at[block],
                send_sem=b_send.at[d],
                recv_sem=b_recv.at[d],
                device_id={"net": peer},
                device_id_type=MESH,
            )
            copy.start()
            copies.append(copy)
        for copy in copies:
            copy.wait()
        total = red_b[0]
        for k in range(1, outer):
            total = total + red_b[k]
        return total

    total = all_sum(pack([inner(u[k // 2], s[k - k // 2]) for k in range(2 * ITERS)]))
    moments = [total] + [pltpu.roll(total, LANES - 4 * m, 1) for m in range(1, 2 * ITERS)]
    gram = {(i, j): moments[i + j] + moments[i + j + 1] for i in range(ITERS) for j in range(i, ITERS)}
    weights = galerkin(gram, moments[:ITERS], ITERS)
    weights = [unpack(w) for w in weights]
    weights = [jnp.concatenate([w, w], axis=0) for w in weights]
    step = weights[0] * u[0]
    residual = s[0] - weights[0] * (s[0] + s[1])
    for j in range(1, ITERS):
        step = step + weights[j] * u[j]
        residual = residual - weights[j] * (s[j] + s[j + 1])
    out = select_dot(jnp.concatenate([step, residual], axis=0), to_bus, 3)
    for c in range(2):
        x_ref[c] = out[c * scen : (c + 1) * scen, :buses]
        r_ref[c] = out[(2 + c) * scen : (3 + c) * scen, :buses]


def body(
    n,
    volt_mag,
    volt_ang,
    gradient,
    branch_from,
    branch_to,
    branch_count,
    boundary,
    conductance,
    susceptance,
    duals,
    slacks,
    gen_bus,
    gen_curvature,
):
    buses, scen = volt_mag.shape
    slots = branch_from.shape[0]
    span = -(-slots // LANES) * LANES
    group = 16 if n % 16 == 0 and n > 16 else 4 if n % 4 == 0 else 1
    outer = n // group
    row = lambda a: a.reshape(1, -1)
    rows = 4 * scen + 8
    dma = lambda *shape: pltpu.SemaphoreType.DMA(shape)
    step, residual = pl.pallas_call(
        functools.partial(kernel, n, group),
        out_shape=[jax.ShapeDtypeStruct((2, scen, buses), F32)] * 2,
        in_specs=[pl.BlockSpec(memory_space=pltpu.VMEM)] * 13,
        out_specs=[pl.BlockSpec(memory_space=pltpu.VMEM)] * 2,
        scratch_shapes=[
            pltpu.VMEM((8, span), F32),
            pltpu.VMEM((8, span), F32),
            pltpu.VMEM((4 * scen, 2 * LANES), F32),
            pltpu.VMEM((2 * LANES, 2 * span), BF16),
            pltpu.VMEM((2 * span, 2 * LANES), BF16),
            pltpu.VMEM((2, rows, LANES), F32),
            pltpu.VMEM((2, rows, LANES), F32),
            pltpu.VMEM((ITERS, 2, 2 * scen, LANES), F32),
            pltpu.VMEM((ITERS, 2, 2 * scen, LANES), F32),
            pltpu.VMEM((group, 8, LANES), F32),
            pltpu.VMEM((outer, 8, LANES), F32),
            dma(2),
            dma(2),
            dma(ITERS, 2),
            dma(ITERS, 2),
            dma(group),
            dma(group),
            dma(outer),
            dma(outer),
        ],
        compiler_params=pltpu.CompilerParams(
            collective_id=0, has_side_effects=True, vmem_limit_bytes=32 * 1024 * 1024
        ),
        name="newton",
    )(
        volt_mag.T,
        volt_ang.T,
        gradient.transpose(1, 2, 0),
        row(branch_from),
        row(branch_to),
        row(branch_count),
        row(boundary),
        row(conductance),
        row(susceptance),
        duals.transpose(0, 2, 1),
        slacks.transpose(0, 2, 1),
        row(gen_bus),
        row(gen_curvature),
    )
    return step.transpose(2, 0, 1), residual.transpose(2, 0, 1)


def solution(mesh):
    placed = (
        P("net", "scen"),
        P("net", "scen"),
        P("net", None, "scen"),
        P("net"),
        P("net"),
        P("net"),
        P("net"),
        P("net"),
        P("net"),
        P(None, "net", "scen"),
        P(None, "net", "scen"),
        P("net"),
        P("net"),
    )
    return jax.shard_map(
        functools.partial(body, mesh.shape["net"]),
        mesh=mesh,
        in_specs=placed,
        out_specs=(P("net", None, "scen"), P("net", None, "scen")),
        check_vma=False,
    )
```

```python
import functools

import jax
import jax.numpy as jnp
from jax import lax
from jax.experimental import pallas as pl
from jax.experimental.pallas import tpu as pltpu
from jax.sharding import PartitionSpec as P

MESH = pl.DeviceIdType.MESH
F32, BF16 = jnp.float32, jnp.bfloat16
ITERS = 4
LANES = 128

barrier_weight = 0.01
volt_low = 0.9
volt_high = 1.1
angle_reg = 0.5


def sine_cosine(angle):
    square = angle * angle
    sine = 1.0 / 6227020800.0
    for term in (-1.0 / 39916800.0, 1.0 / 362880.0, -1.0 / 5040.0, 1.0 / 120.0, -1.0 / 6.0, 1.0):
        sine = sine * square + term
    cosine = -1.0 / 87178291200.0
    for term in (1.0 / 479001600.0, -1.0 / 3628800.0, 1.0 / 40320.0, -1.0 / 720.0, 1.0 / 24.0, -0.5, 1.0):
        cosine = cosine * square + term
    return sine * angle, cosine


def branch_blocks(mag_from, mag_to, sine, cosine, conduct, suscept, weight_p, weight_q):
    along = conduct * cosine + suscept * sine
    across = conduct * sine - suscept * cosine
    cross = mag_from * mag_to
    jp = (2.0 * conduct * mag_from - mag_to * along, cross * across, -mag_from * along, -cross * across)
    jq = (-2.0 * suscept * mag_from - mag_to * across, -cross * along, -mag_from * across, cross * along)
    wp = [weight_p * j for j in jp]
    wq = [weight_q * j for j in jq]

    def entry(i, j):
        return wp[i] * jp[j] + wq[i] * jq[j]

    return (
        (entry(0, 0), entry(0, 1), entry(1, 1)),
        (entry(2, 2), entry(2, 3), entry(3, 3)),
        (entry(0, 2), entry(0, 3), entry(1, 2), entry(1, 3)),
    )


def pieces(values, terms):
    out = []
    for _ in range(terms - 1):
        head = values.astype(BF16)
        out.append(head)
        values = values - head.astype(F32)
    return jnp.concatenate(out + [values.astype(BF16)], axis=0)


def select_dot(values, table, terms):
    rows = values.shape[0]
    out = jnp.dot(pieces(values, terms), table, preferred_element_type=F32)
    total = out[(terms - 1) * rows :]
    for k in range(terms - 2, -1, -1):
        total = total + out[k * rows : (k + 1) * rows]
    return total


def inner(left, right):
    product = left * right
    half = product.shape[0] // 2
    product = product[:half] + product[half:]
    product = product[:, :LANES] + product[:, LANES:]
    return jnp.sum(product, axis=1, keepdims=True)


def pack(sums):
    lane = lax.broadcasted_iota(jnp.int32, (8, LANES), 1)
    tile = jnp.zeros((8, LANES), F32)
    for m, column in enumerate(sums):
        for g in range(4):
            tile = jnp.where(lane == 4 * m + g, column[8 * g : 8 * g + 8], tile)
    return tile


def unpack(tile):
    return jnp.concatenate([tile[:, g : g + 1] for g in range(4)], axis=0)


def galerkin(gram, rhs, n):
    a = {(i, j): gram[(min(i, j), max(i, j))] for i in range(n) for j in range(n)}
    rhs = list(rhs)
    low, inv = {}, {}
    for k in range(n):
        live = a[(k, k)] > 1e-7 * gram[(k, k)]
        inv[k] = jnp.where(live, 1.0 / jnp.where(live, a[(k, k)], 1.0), 0.0)
        for i in range(k + 1, n):
            low[(i, k)] = a[(i, k)] * inv[k]
            for j in range(k + 1, i + 1):
                a[(i, j)] = a[(i, j)] - low[(i, k)] * a[(j, k)]
                a[(j, i)] = a[(i, j)]
            rhs[i] = rhs[i] - low[(i, k)] * rhs[k]
    out = [None] * n
    for k in reversed(range(n)):
        value = rhs[k] * inv[k]
        for i in range(k + 1, n):
            value = value - low[(i, k)] * out[i]
        out[k] = value
    return out


def kernel(
    n,
    group,
    *refs,
):
    inputs, (x_ref, r_ref), loaded, rest = refs[:13], refs[13:15], refs[15:28], refs[28:]
    load_sem = rest[0]
    loads = []
    for k, (source, target) in enumerate(zip(inputs, loaded)):
        copy = pltpu.make_async_copy(source, target, load_sem.at[k])
        copy.start()
        loads.append(copy)
    solve(n, group, loads, *loaded, x_ref, r_ref, *rest[1:])


def solve(
    n,
    group,
    loads,
    vm_ref,
    va_ref,
    grad_ref,
    from_ref,
    to_ref,
    count_ref,
    bound_ref,
    g_ref,
    b_ref,
    dual_ref,
    slack_ref,
    gbus_ref,
    gcur_ref,
    x_ref,
    r_ref,
    irow,
    frow,
    vin,
    gather_tab,
    scatter_tab,
    pay_out,
    pay_in,
    halo_out,
    halo_in,
    red_a,
    red_b,
    pay_send,
    pay_recv,
    halo_send,
    halo_recv,
    a_send,
    a_recv,
    b_send,
    b_recv,
):
    scen, buses = vm_ref.shape
    slots = from_ref.shape[-1]
    ghost = buses // 2
    wide = 2 * LANES
    span = gather_tab.shape[1] // 2
    gens = gbus_ref.shape[1]
    outer = n // group
    me = lax.axis_index("net")
    prev, nxt = lax.rem(me + n - 1, n), lax.rem(me + 1, n)
    inside = lax.rem(me, group)
    block = lax.div(me, group)
    peers_a = [block * group + lax.rem(inside + d, group) for d in range(1, group)]
    peers_b = [lax.rem(block + d, outer) * group + inside for d in range(1, outer)]

    barrier = pltpu.get_barrier_semaphore()
    for peer in (prev, nxt, *peers_a, *peers_b):
        pl.semaphore_signal(barrier, inc=1, device_id={"net": peer}, device_id_type=MESH)

    def exchange(source, target, send, recv):
        out = []
        for half, peer in ((0, prev), (1, nxt)):
            copy = pltpu.make_async_remote_copy(
                src_ref=source.at[half],
                dst_ref=target.at[1 - half],
                send_sem=send.at[half],
                recv_sem=recv.at[half],
                device_id={"net": peer},
                device_id_type=MESH,
            )
            copy.start()
            out.append(copy)
        return out

    for copy in loads:
        copy.wait()

    irow[...] = jnp.full(irow.shape, -1.0, F32)
    irow[0:1, :slots] = from_ref[...].reshape(1, slots).astype(F32)
    irow[1:2, :slots] = to_ref[...].reshape(1, slots).astype(F32)
    irow[2:3, :buses] = bound_ref[...].astype(F32)
    irow[3:4, :gens] = gbus_ref[...].astype(F32)
    frow[...] = jnp.zeros(frow.shape, F32)
    frow[0:1, :slots] = g_ref[...].reshape(1, slots)
    frow[1:2, :slots] = b_ref[...].reshape(1, slots)
    frow[2:3, :gens] = gcur_ref[...]
    from_row, to_row = irow[0:1, :], irow[1:2, :]
    lane_i = lax.broadcasted_iota(jnp.int32, (8, wide), 1)
    lane = lane_i.astype(F32)
    plain = irow[0:8, :wide]
    rolled = pltpu.roll(plain, LANES - ghost, 1)
    upper = (lane_i >= LANES) & (lane_i < LANES + ghost)
    place = jnp.where(lane_i < ghost, plain, jnp.where(upper, rolled, -2.0))[2:3]
    entry = jnp.where(lane_i < ghost, lane, jnp.where(upper, lane - (LANES - ghost), -1e6))[0:1]

    def column(row):
        return jnp.transpose(jnp.broadcast_to(row, (LANES, row.shape[1])))

    def hot(mask):
        return jnp.where(mask, 1.0, 0.0).astype(BF16)

    place_col, from_col, to_col = column(place), column(from_row), column(to_row)
    lanes_of = lambda row, t: row[:, t * LANES : (t + 1) * LANES]
    for t in range(span // LANES):
        gather_tab[:, t * LANES : (t + 1) * LANES] = hot(place_col == lanes_of(from_row, t))
        gather_tab[:, span + t * LANES : span + (t + 1) * LANES] = hot(place_col == lanes_of(to_row, t))
    for t in range(2):
        cols = slice(t * LANES, (t + 1) * LANES)
        scatter_tab[0:span, cols] = hot(from_col == lanes_of(place, t))
        scatter_tab[span:, cols] = hot(to_col == lanes_of(place, t))
    cross_tab = jnp.concatenate([hot(to_col == lanes_of(entry, t) + buses) for t in range(2)], axis=1)
    bus_row = lane[0:1]
    bus_col = lax.broadcasted_iota(jnp.int32, (wide, LANES), 0).astype(F32)
    to_place = jnp.concatenate([hot(bus_col == lanes_of(place, t)) for t in range(2)], axis=1)
    to_bus = jnp.concatenate([hot(place_col == lanes_of(bus_row, t)) for t in range(2)], axis=1)

    vin[...] = jnp.zeros(vin.shape, F32)
    vin[0:scen, :buses] = vm_ref[...]
    vin[scen : 2 * scen, :buses] = va_ref[...]
    vin[2 * scen : 3 * scen, :buses] = grad_ref[0]
    vin[3 * scen : 4 * scen, :buses] = grad_ref[1]
    placed = select_dot(vin[...], to_place, 3)
    vm, va, start = placed[0:scen], placed[scen : 2 * scen], placed[2 * scen :]

    slot = lax.broadcasted_iota(jnp.int32, (1, slots), 1)
    live = jnp.where(slot < count_ref[...].reshape(1, 1), 1.0, 0.0)
    pad = jnp.zeros((scen, span - slots), F32)
    weight_p = jnp.concatenate([live * dual_ref[0] / slack_ref[0], pad], axis=1)
    weight_q = jnp.concatenate([live * dual_ref[1] / slack_ref[1], pad], axis=1)
    conduct, suscept = frow[0:1, :], frow[1:2, :]
    stacked = jnp.concatenate([weight_p, weight_q, frow[0:8, :]], axis=0)
    crossing = select_dot(stacked, cross_tab, 3)
    payload = jnp.concatenate([vm, va, crossing], axis=0)
    for half in range(2):
        pay_out[half] = payload[:, half * LANES : (half + 1) * LANES]

    pl.semaphore_wait(barrier, 2 + (group - 1) + (outer - 1))
    pay_copies = exchange(pay_out, pay_in, pay_send, pay_recv)

    ends = select_dot(placed[0 : 2 * scen], gather_tab[...], 3)
    local = jnp.where((to_row >= 0.0) & (to_row < float(buses)), 1.0, 0.0)
    sine, cosine = sine_cosine(ends[scen:, :span] - ends[scen:, span:])
    hff, htt, (h00, h01, h10, h11) = branch_blocks(
        ends[:scen, :span], ends[:scen, span:], sine, cosine, conduct, suscept, weight_p * local, weight_q * local
    )
    both = jnp.concatenate([jnp.concatenate([a, b], axis=1) for a, b in zip(hff, htt)], axis=0)
    diag = select_dot(both, scatter_tab[...], 3)
    gen = column(irow[3:4, :LANES])
    curve = column(frow[2:3, :LANES])
    gen_sum = jnp.concatenate(
        [jnp.sum(jnp.where(gen == lanes_of(place, t), curve, 0.0), axis=0, keepdims=True) for t in range(2)], axis=1
    )
    low, high = vm - volt_low, volt_high - vm
    base_vv = barrier_weight / (low * low) + barrier_weight / (high * high) + gen_sum
    base_aa = angle_reg + gen_sum

    for copy in pay_copies:
        copy.wait()
    arrived = jnp.concatenate([pay_in[0], pay_in[1]], axis=1)
    there_vm, there_va = arrived[0:scen], arrived[scen : 2 * scen]
    there_p, there_q = arrived[2 * scen : 3 * scen], arrived[3 * scen : 4 * scen]
    there_g, there_b = arrived[4 * scen : 4 * scen + 1], arrived[4 * scen + 1 : 4 * scen + 2]
    here_p, here_q = crossing[0:scen], crossing[scen : 2 * scen]
    here_g, here_b = crossing[2 * scen : 2 * scen + 1], crossing[2 * scen + 1 : 2 * scen + 2]
    sine, cosine = sine_cosine(va - there_va)
    off, _, (o00, o01, o10, o11) = branch_blocks(vm, there_vm, sine, cosine, here_g, here_b, here_p, here_q)
    _, on, (i00, i01, i10, i11) = branch_blocks(there_vm, vm, -sine, cosine, there_g, there_b, there_p, there_q)
    c00, c01, c10, c11 = o00 + i00, o01 + i10, o10 + i01, o11 + i11
    d00 = diag[0:scen] + off[0] + on[0] + base_vv
    d01 = diag[scen : 2 * scen] + off[1] + on[1]
    d11 = diag[2 * scen :] + off[2] + on[2] + base_aa
    inverse = 1.0 / (d00 * d11 - d01 * d01)
    p00, p01, p11 = d11 * inverse, -d01 * inverse, d00 * inverse

    def precondition(v):
        return jnp.concatenate([p00 * v[:scen] + p01 * v[scen:], p01 * v[:scen] + p11 * v[scen:]], axis=0)

    s, u = [start], [precondition(start)]
    for j in range(ITERS):
        v = u[j]
        halo_out[j, 0] = v[:, :LANES]
        halo_out[j, 1] = v[:, LANES:]
        copies = exchange(halo_out.at[j], halo_in.at[j], halo_send.at[j], halo_recv.at[j])
        ends = select_dot(v, gather_tab[...], 2)
        f0, f1, t0, t1 = ends[:scen, :span], ends[scen:, :span], ends[:scen, span:], ends[scen:, span:]
        terms = jnp.concatenate(
            [
                jnp.concatenate([h00 * t0 + h01 * t1, h00 * f0 + h10 * f1], axis=1),
                jnp.concatenate([h10 * t0 + h11 * t1, h01 * f0 + h11 * f1], axis=1),
            ],
            axis=0,
        )
        inside_sum = select_dot(terms, scatter_tab[...], 2)
        for copy in copies:
            copy.wait()
        n0 = jnp.concatenate([halo_in[j, 0, :scen], halo_in[j, 1, :scen]], axis=1)
        n1 = jnp.concatenate([halo_in[j, 0, scen:], halo_in[j, 1, scen:]], axis=1)
        s.append(inside_sum + jnp.concatenate([c00 * n0 + c01 * n1, c10 * n0 + c11 * n1], axis=0))
        if j + 1 < ITERS:
            u.append(precondition(s[-1]))

    def all_sum(tile):
        red_a[pl.ds(inside, 1)] = tile[None]
        copies = []
        for d, peer in enumerate(peers_a):
            copy = pltpu.make_async_remote_copy(
                src_ref=red_a.at[inside],
                dst_ref=red_a.at[inside],
                send_sem=a_send.at[d],
                recv_sem=a_recv.at[d],
                device_id={"net": peer},
                device_id_type=MESH,
            )
            copy.start()
            copies.append(copy)
        for copy in copies:
            copy.wait()
        total = red_a[0]
        for k in range(1, group):
            total = total + red_a[k]
        red_b[pl.ds(block, 1)] = total[None]
        copies = []
        for d, peer in enumerate(peers_b):
            copy = pltpu.make_async_remote_copy(
                src_ref=red_b.at[block],
                dst_ref=red_b.at[block],
                send_sem=b_send.at[d],
                recv_sem=b_recv.at[d],
                device_id={"net": peer},
                device_id_type=MESH,
            )
            copy.start()
            copies.append(copy)
        for copy in copies:
            copy.wait()
        total = red_b[0]
        for k in range(1, outer):
            total = total + red_b[k]
        return total

    total = all_sum(pack([inner(u[k // 2], s[k - k // 2]) for k in range(2 * ITERS)]))
    moments = [total] + [pltpu.roll(total, LANES - 4 * m, 1) for m in range(1, 2 * ITERS)]
    gram = {(i, j): moments[i + j] + moments[i + j + 1] for i in range(ITERS) for j in range(i, ITERS)}
    weights = galerkin(gram, moments[:ITERS], ITERS)
    weights = [unpack(w) for w in weights]
    weights = [jnp.concatenate([w, w], axis=0) for w in weights]
    step = weights[0] * u[0]
    residual = s[0] - weights[0] * (s[0] + s[1])
    for j in range(1, ITERS):
        step = step + weights[j] * u[j]
        residual = residual - weights[j] * (s[j] + s[j + 1])
    out = select_dot(jnp.concatenate([step, residual], axis=0), to_bus, 3)
    for c in range(2):
        x_ref[c] = out[c * scen : (c + 1) * scen, :buses]
        r_ref[c] = out[(2 + c) * scen : (3 + c) * scen, :buses]


def body(
    n,
    volt_mag,
    volt_ang,
    gradient,
    branch_from,
    branch_to,
    branch_count,
    boundary,
    conductance,
    susceptance,
    duals,
    slacks,
    gen_bus,
    gen_curvature,
):
    buses, scen = volt_mag.shape
    slots = branch_from.shape[0]
    span = -(-slots // LANES) * LANES
    group = 16 if n % 16 == 0 and n > 16 else 4 if n % 4 == 0 else 1
    outer = n // group
    row = lambda a: a.reshape(1, -1)
    rows = 4 * scen + 8
    dma = lambda *shape: pltpu.SemaphoreType.DMA(shape)
    operands = (
        volt_mag.T,
        volt_ang.T,
        gradient.transpose(1, 2, 0),
        branch_from,
        branch_to,
        branch_count,
        row(boundary),
        conductance,
        susceptance,
        duals.transpose(0, 2, 1),
        slacks.transpose(0, 2, 1),
        row(gen_bus),
        row(gen_curvature),
    )
    step, residual = pl.pallas_call(
        functools.partial(kernel, n, group),
        out_shape=[jax.ShapeDtypeStruct((2, scen, buses), F32)] * 2,
        in_specs=[pl.BlockSpec(memory_space=pltpu.HBM)] * 13,
        out_specs=[pl.BlockSpec(memory_space=pltpu.VMEM)] * 2,
        scratch_shapes=[
            *(pltpu.VMEM(a.shape, a.dtype) for a in operands),
            dma(13),
            pltpu.VMEM((8, span), F32),
            pltpu.VMEM((8, span), F32),
            pltpu.VMEM((4 * scen, 2 * LANES), F32),
            pltpu.VMEM((2 * LANES, 2 * span), BF16),
            pltpu.VMEM((2 * span, 2 * LANES), BF16),
            pltpu.VMEM((2, rows, LANES), F32),
            pltpu.VMEM((2, rows, LANES), F32),
            pltpu.VMEM((ITERS, 2, 2 * scen, LANES), F32),
            pltpu.VMEM((ITERS, 2, 2 * scen, LANES), F32),
            pltpu.VMEM((group, 8, LANES), F32),
            pltpu.VMEM((outer, 8, LANES), F32),
            dma(2),
            dma(2),
            dma(ITERS, 2),
            dma(ITERS, 2),
            dma(group),
            dma(group),
            dma(outer),
            dma(outer),
        ],
        compiler_params=pltpu.CompilerParams(
            collective_id=0, has_side_effects=True, vmem_limit_bytes=62 * 1024 * 1024
        ),
        name="newton",
    )(*operands)
    return step.transpose(2, 0, 1), residual.transpose(2, 0, 1)


def solution(mesh):
    placed = (
        P("net", "scen"),
        P("net", "scen"),
        P("net", None, "scen"),
        P("net"),
        P("net"),
        P("net"),
        P("net"),
        P("net"),
        P("net"),
        P(None, "net", "scen"),
        P(None, "net", "scen"),
        P("net"),
        P("net"),
    )
    return jax.shard_map(
        functools.partial(body, mesh.shape["net"]),
        mesh=mesh,
        in_specs=placed,
        out_specs=(P("net", None, "scen"), P("net", None, "scen")),
        check_vma=False,
    )
```

```python
import functools

import jax
import jax.numpy as jnp
from jax import lax
from jax.experimental import pallas as pl
from jax.experimental.pallas import tpu as pltpu
from jax.sharding import PartitionSpec as P

MESH = pl.DeviceIdType.MESH
F32, BF16 = jnp.float32, jnp.bfloat16
ITERS = 4
LANES = 128

barrier_weight = 0.01
volt_low = 0.9
volt_high = 1.1
angle_reg = 0.5


def sine_cosine(angle):
    square = angle * angle
    sine = 1.0 / 6227020800.0
    for term in (-1.0 / 39916800.0, 1.0 / 362880.0, -1.0 / 5040.0, 1.0 / 120.0, -1.0 / 6.0, 1.0):
        sine = sine * square + term
    cosine = -1.0 / 87178291200.0
    for term in (1.0 / 479001600.0, -1.0 / 3628800.0, 1.0 / 40320.0, -1.0 / 720.0, 1.0 / 24.0, -0.5, 1.0):
        cosine = cosine * square + term
    return sine * angle, cosine


def branch_blocks(mag_from, mag_to, sine, cosine, conduct, suscept, weight_p, weight_q):
    along = conduct * cosine + suscept * sine
    across = conduct * sine - suscept * cosine
    cross = mag_from * mag_to
    jp = (2.0 * conduct * mag_from - mag_to * along, cross * across, -mag_from * along, -cross * across)
    jq = (-2.0 * suscept * mag_from - mag_to * across, -cross * along, -mag_from * across, cross * along)
    wp = [weight_p * j for j in jp]
    wq = [weight_q * j for j in jq]

    def entry(i, j):
        return wp[i] * jp[j] + wq[i] * jq[j]

    return (
        (entry(0, 0), entry(0, 1), entry(1, 1)),
        (entry(2, 2), entry(2, 3), entry(3, 3)),
        (entry(0, 2), entry(0, 3), entry(1, 2), entry(1, 3)),
    )


def pieces(values, terms):
    out = []
    for _ in range(terms - 1):
        head = values.astype(BF16)
        out.append(head)
        values = values - head.astype(F32)
    return jnp.concatenate(out + [values.astype(BF16)], axis=0)


def select_dot(values, table, terms):
    rows = values.shape[0]
    out = jnp.dot(pieces(values, terms), table, preferred_element_type=F32)
    total = out[(terms - 1) * rows :]
    for k in range(terms - 2, -1, -1):
        total = total + out[k * rows : (k + 1) * rows]
    return total


def inner(left, right):
    product = left * right
    half = product.shape[0] // 2
    product = product[:half] + product[half:]
    return product[:, :LANES] + product[:, LANES:]


def pack(parts):
    return jnp.sum(jnp.transpose(jnp.concatenate(parts, axis=0)), axis=0, keepdims=True)


def unpack(rows):
    lane = lax.broadcasted_iota(jnp.int32, (1, LANES), 1)
    joined = rows[0]
    for k in range(1, len(rows)):
        joined = jnp.where(lane < 32 * k, joined, pltpu.roll(rows[k], 32 * k, 1))
    columns = jnp.transpose(jnp.broadcast_to(joined, (LANES, LANES)))
    return [columns[32 * k : 32 * k + 32] for k in range(len(rows))]


def galerkin(gram, rhs, n):
    a = {(i, j): gram[(min(i, j), max(i, j))] for i in range(n) for j in range(n)}
    rhs = list(rhs)
    low, inv = {}, {}
    for k in range(n):
        live = a[(k, k)] > 1e-7 * gram[(k, k)]
        inv[k] = jnp.where(live, 1.0 / jnp.where(live, a[(k, k)], 1.0), 0.0)
        for i in range(k + 1, n):
            low[(i, k)] = a[(i, k)] * inv[k]
            for j in range(k + 1, i + 1):
                a[(i, j)] = a[(i, j)] - low[(i, k)] * a[(j, k)]
                a[(j, i)] = a[(i, j)]
            rhs[i] = rhs[i] - low[(i, k)] * rhs[k]
    out = [None] * n
    for k in reversed(range(n)):
        value = rhs[k] * inv[k]
        for i in range(k + 1, n):
            value = value - low[(i, k)] * out[i]
        out[k] = value
    return out


def kernel(
    n,
    group,
    *refs,
):
    inputs, o_ref, loaded, rest = refs[:13], refs[13], refs[14:27], refs[27:]
    x_ref, r_ref = o_ref.at[0], o_ref.at[1]
    load_sem = rest[0]
    me = lax.axis_index("net")
    neighbours = (lax.rem(me + n - 1, n), lax.rem(me + 1, n))
    for peer in neighbours:
        pl.semaphore_signal(pltpu.get_barrier_semaphore(), inc=1, device_id={"net": peer}, device_id_type=MESH)
    loads = []
    for k, (source, target) in enumerate(zip(inputs, loaded)):
        copy = pltpu.make_async_copy(source, target, load_sem.at[k])
        copy.start()
        loads.append(copy)
    solve(n, group, loads, *loaded, x_ref, r_ref, *rest[1:])


def solve(
    n,
    group,
    loads,
    vm_ref,
    va_ref,
    grad_ref,
    from_ref,
    to_ref,
    count_ref,
    bound_ref,
    g_ref,
    b_ref,
    dual_ref,
    slack_ref,
    gbus_ref,
    gcur_ref,
    x_ref,
    r_ref,
    irow,
    frow,
    vin,
    gather_tab,
    scatter_tab,
    pay_out,
    pay_in,
    diag_out,
    diag_in,
    halo_out,
    halo_in,
    red_a,
    red_b,
    pay_send,
    pay_recv,
    diag_send,
    diag_recv,
    halo_send,
    halo_recv,
    a_send,
    a_recv,
    b_send,
    b_recv,
):
    scen, buses = vm_ref.shape
    slots = from_ref.shape[-1]
    ghost = buses // 2
    wide = 2 * LANES
    span = gather_tab.shape[1] // 2
    gens = gbus_ref.shape[1]
    outer = n // group
    me = lax.axis_index("net")
    prev, nxt = lax.rem(me + n - 1, n), lax.rem(me + 1, n)
    inside = lax.rem(me, group)
    block = lax.div(me, group)
    peers_a = [block * group + lax.rem(inside + d, group) for d in range(1, group)]
    peers_b = [lax.rem(block + d, outer) * group + inside for d in range(1, outer)]

    barrier = pltpu.get_barrier_semaphore()
    for peer in (*peers_a, *peers_b):
        pl.semaphore_signal(barrier, inc=1, device_id={"net": peer}, device_id_type=MESH)

    def exchange(source, target, send, recv):
        out = []
        for half, peer in ((0, prev), (1, nxt)):
            copy = pltpu.make_async_remote_copy(
                src_ref=source.at[half],
                dst_ref=target.at[1 - half],
                send_sem=send.at[half],
                recv_sem=recv.at[half],
                device_id={"net": peer},
                device_id_type=MESH,
            )
            copy.start()
            out.append(copy)
        return out

    for copy in loads:
        copy.wait()

    irow[...] = jnp.full(irow.shape, -1.0, F32)
    irow[0:1, :slots] = from_ref[...].reshape(1, slots).astype(F32)
    irow[1:2, :slots] = to_ref[...].reshape(1, slots).astype(F32)
    irow[2:3, :buses] = bound_ref[...].astype(F32)
    irow[3:4, :gens] = gbus_ref[...].astype(F32)
    frow[...] = jnp.zeros(frow.shape, F32)
    frow[0:1, :slots] = g_ref[...].reshape(1, slots)
    frow[1:2, :slots] = b_ref[...].reshape(1, slots)
    frow[2:3, :gens] = gcur_ref[...]
    from_row, to_row = irow[0:1, :], irow[1:2, :]
    lane_i = lax.broadcasted_iota(jnp.int32, (8, wide), 1)
    lane = lane_i.astype(F32)
    plain = irow[0:8, :wide]
    rolled = pltpu.roll(plain, LANES - ghost, 1)
    upper = (lane_i >= LANES) & (lane_i < LANES + ghost)
    place = jnp.where(lane_i < ghost, plain, jnp.where(upper, rolled, -2.0))[2:3]
    entry = jnp.where(lane_i < ghost, lane, jnp.where(upper, lane - (LANES - ghost), -1e6))[0:1]

    def column(row):
        return jnp.transpose(jnp.broadcast_to(row, (LANES, row.shape[1])))

    def hot(mask):
        return jnp.where(mask, 1.0, 0.0).astype(BF16)

    place_col, from_col, to_col = column(place), column(from_row), column(to_row)
    lanes_of = lambda row, t: row[:, t * LANES : (t + 1) * LANES]
    for t in range(span // LANES):
        gather_tab[:, t * LANES : (t + 1) * LANES] = hot(place_col == lanes_of(from_row, t))
        gather_tab[:, span + t * LANES : span + (t + 1) * LANES] = hot(place_col == lanes_of(to_row, t))
    for t in range(2):
        cols = slice(t * LANES, (t + 1) * LANES)
        scatter_tab[0:span, cols] = hot(from_col == lanes_of(place, t))
        scatter_tab[span:, cols] = hot(to_col == lanes_of(place, t))
    cross_tab = jnp.concatenate([hot(to_col == lanes_of(entry, t) + buses) for t in range(2)], axis=1)
    bus_row = lane[0:1]
    bus_col = lax.broadcasted_iota(jnp.int32, (wide, LANES), 0).astype(F32)
    to_place = jnp.concatenate([hot(bus_col == lanes_of(place, t)) for t in range(2)], axis=1)
    to_bus = jnp.concatenate([hot(place_col == lanes_of(bus_row, t)) for t in range(2)], axis=1)

    vin[...] = jnp.zeros(vin.shape, F32)
    vin[0:scen, :buses] = vm_ref[...]
    vin[scen : 2 * scen, :buses] = va_ref[...]
    vin[2 * scen : 3 * scen, :buses] = grad_ref[0]
    vin[3 * scen : 4 * scen, :buses] = grad_ref[1]
    placed = select_dot(vin[...], to_place, 3)
    vm, va, start = placed[0:scen], placed[scen : 2 * scen], placed[2 * scen :]

    slot = lax.broadcasted_iota(jnp.int32, (1, slots), 1)
    live = jnp.where(slot < count_ref[...].reshape(1, 1), 1.0, 0.0)
    pad = jnp.zeros((scen, span - slots), F32)
    weight_p = jnp.concatenate([live * dual_ref[0] / slack_ref[0], pad], axis=1)
    weight_q = jnp.concatenate([live * dual_ref[1] / slack_ref[1], pad], axis=1)
    conduct, suscept = frow[0:1, :], frow[1:2, :]
    stacked = jnp.concatenate([weight_p, weight_q, frow[0:8, :]], axis=0)
    crossing = select_dot(stacked, cross_tab, 3)
    payload = jnp.concatenate([vm, va, crossing], axis=0)
    for half in range(2):
        pay_out[half] = payload[:, half * LANES : (half + 1) * LANES]

    pl.semaphore_wait(barrier, 2 + (group - 1) + (outer - 1))
    pay_copies = exchange(pay_out, pay_in, pay_send, pay_recv)

    ends = select_dot(placed[0 : 2 * scen], gather_tab[...], 3)
    local = jnp.where((to_row >= 0.0) & (to_row < float(buses)), 1.0, 0.0)
    sine, cosine = sine_cosine(ends[scen:, :span] - ends[scen:, span:])
    hff, htt, (h00, h01, h10, h11) = branch_blocks(
        ends[:scen, :span], ends[:scen, span:], sine, cosine, conduct, suscept, weight_p * local, weight_q * local
    )
    both = jnp.concatenate([jnp.concatenate([a, b], axis=1) for a, b in zip(hff, htt)], axis=0)
    diag = select_dot(both, scatter_tab[...], 3)
    gen = column(irow[3:4, :LANES])
    curve = column(frow[2:3, :LANES])
    gen_sum = jnp.concatenate(
        [jnp.sum(jnp.where(gen == lanes_of(place, t), curve, 0.0), axis=0, keepdims=True) for t in range(2)], axis=1
    )
    low, high = vm - volt_low, volt_high - vm
    base_vv = barrier_weight / (low * low) + barrier_weight / (high * high) + gen_sum
    base_aa = angle_reg + gen_sum

    own = jnp.concatenate(
        [diag[0:scen] + base_vv, diag[scen : 2 * scen], diag[2 * scen :] + base_aa, start], axis=0
    )
    for half in range(2):
        diag_out[half] = own[:, half * LANES : (half + 1) * LANES]
    diag_copies = exchange(diag_out, diag_in, diag_send, diag_recv)
    pending = [*pay_copies, *diag_copies]

    for copy in pay_copies:
        copy.wait_recv()
    arrived = jnp.concatenate([pay_in[0], pay_in[1]], axis=1)
    there_vm, there_va = arrived[0:scen], arrived[scen : 2 * scen]
    there_p, there_q = arrived[2 * scen : 3 * scen], arrived[3 * scen : 4 * scen]
    there_g, there_b = arrived[4 * scen : 4 * scen + 1], arrived[4 * scen + 1 : 4 * scen + 2]
    here_p, here_q = crossing[0:scen], crossing[scen : 2 * scen]
    here_g, here_b = crossing[2 * scen : 2 * scen + 1], crossing[2 * scen + 1 : 2 * scen + 2]
    sine, cosine = sine_cosine(va - there_va)
    off, reach, (o00, o01, o10, o11) = branch_blocks(vm, there_vm, sine, cosine, here_g, here_b, here_p, here_q)
    root, on, (i00, i01, i10, i11) = branch_blocks(there_vm, vm, -sine, cosine, there_g, there_b, there_p, there_q)
    c00, c01, c10, c11 = o00 + i00, o01 + i10, o10 + i01, o11 + i11

    def inverse_of(fields, first, second):
        d00, d01, d11 = (fields[k * scen : (k + 1) * scen] + first[k] + second[k] for k in range(3))
        inverse = 1.0 / (d00 * d11 - d01 * d01)
        return d11 * inverse, -d01 * inverse, d00 * inverse

    def applied(blocks, v):
        b00, b01, b11 = blocks
        return jnp.concatenate([b00 * v[:scen] + b01 * v[scen:], b01 * v[:scen] + b11 * v[scen:]], axis=0)

    diag_inverse = inverse_of(own, off, on)
    def precondition(v):
        return applied(diag_inverse, v)

    for copy in diag_copies:
        copy.wait_recv()
    beyond = jnp.concatenate([diag_in[0], diag_in[1]], axis=1)
    facing = applied(inverse_of(beyond, reach, root), beyond[3 * scen :])

    s, u = [start], [precondition(start)]
    for j in range(ITERS):
        v = u[j]
        copies = []
        if j:
            halo_out[j - 1, 0] = v[:, :LANES]
            halo_out[j - 1, 1] = v[:, LANES:]
            copies = exchange(
                halo_out.at[j - 1], halo_in.at[j - 1], halo_send.at[j - 1], halo_recv.at[j - 1]
            )
        ends = select_dot(v, gather_tab[...], 2)
        f0, f1, t0, t1 = ends[:scen, :span], ends[scen:, :span], ends[:scen, span:], ends[scen:, span:]
        terms = jnp.concatenate(
            [
                jnp.concatenate([h00 * t0 + h01 * t1, h00 * f0 + h10 * f1], axis=1),
                jnp.concatenate([h10 * t0 + h11 * t1, h01 * f0 + h11 * f1], axis=1),
            ],
            axis=0,
        )
        inside_sum = select_dot(terms, scatter_tab[...], 2)
        for copy in copies:
            copy.wait_recv()
        pending.extend(copies)
        if j:
            facing = jnp.concatenate([halo_in[j - 1, 0], halo_in[j - 1, 1]], axis=1)
        n0, n1 = facing[:scen], facing[scen:]
        s.append(inside_sum + jnp.concatenate([c00 * n0 + c01 * n1, c10 * n0 + c11 * n1], axis=0))
        if j + 1 < ITERS:
            u.append(precondition(s[-1]))

    def all_sum(tile):
        red_a[pl.ds(inside, 1)] = tile[None]
        copies = []
        for d, peer in enumerate(peers_a):
            copy = pltpu.make_async_remote_copy(
                src_ref=red_a.at[inside],
                dst_ref=red_a.at[inside],
                send_sem=a_send.at[d],
                recv_sem=a_recv.at[d],
                device_id={"net": peer},
                device_id_type=MESH,
            )
            copy.start()
            copies.append(copy)
        for copy in copies:
            copy.wait_recv()
        pending.extend(copies)
        total = red_a[0]
        for k in range(1, group):
            total = total + red_a[k]
        red_b[pl.ds(block, 1)] = total[None]
        copies = []
        for d, peer in enumerate(peers_b):
            copy = pltpu.make_async_remote_copy(
                src_ref=red_b.at[block],
                dst_ref=red_b.at[block],
                send_sem=b_send.at[d],
                recv_sem=b_recv.at[d],
                device_id={"net": peer},
                device_id_type=MESH,
            )
            copy.start()
            copies.append(copy)
        for copy in copies:
            copy.wait_recv()
        pending.extend(copies)
        total = red_b[0]
        for k in range(1, outer):
            total = total + red_b[k]
        return total

    parts = [inner(u[k // 2], s[k - k // 2]) for k in range(2 * ITERS)]
    total = all_sum(jnp.concatenate([pack(parts[:4]), pack(parts[4:])], axis=0))
    moments = [total[k // 4 : k // 4 + 1] for k in range(2 * ITERS)]
    moments = [pltpu.roll(m, LANES - 32 * (k % 4), 1) if k % 4 else m for k, m in enumerate(moments)]
    gram = {(i, j): moments[i + j] + moments[i + j + 1] for i in range(ITERS) for j in range(i, ITERS)}
    w = unpack(galerkin(gram, moments[ITERS:], ITERS))
    w = [jnp.concatenate([jnp.concatenate([c, c], axis=1)] * 2, axis=0) for c in w]
    step = (1.0 + w[0]) * u[0] + (w[1] - 1.0) * u[1] + (1.0 + w[2]) * u[2] + (w[3] - 1.0) * u[3]
    residual = (1.0 - w[3]) * s[4] - (w[2] + w[3]) * s[3] - (w[1] + w[2]) * s[2] - (w[0] + w[1]) * s[1] - w[0] * s[0]
    out = select_dot(jnp.concatenate([step, residual], axis=0), to_bus, 3)
    for c in range(2):
        x_ref[c] = out[c * scen : (c + 1) * scen, :buses]
        r_ref[c] = out[(2 + c) * scen : (3 + c) * scen, :buses]

    for copy in pending:
        copy.wait_send()


def body(
    n,
    volt_mag,
    volt_ang,
    gradient,
    branch_from,
    branch_to,
    branch_count,
    boundary,
    conductance,
    susceptance,
    duals,
    slacks,
    gen_bus,
    gen_curvature,
):
    buses, scen = volt_mag.shape
    slots = branch_from.shape[0]
    span = -(-slots // LANES) * LANES
    group = 16 if n % 16 == 0 and n > 16 else 4 if n % 4 == 0 else 1
    outer = n // group
    row = lambda a: a.reshape(1, -1)
    rows = 4 * scen + 8
    dma = lambda *shape: pltpu.SemaphoreType.DMA(shape)
    operands = (
        volt_mag.T,
        volt_ang.T,
        gradient.transpose(1, 2, 0),
        branch_from,
        branch_to,
        branch_count,
        row(boundary),
        conductance,
        susceptance,
        duals.transpose(0, 2, 1),
        slacks.transpose(0, 2, 1),
        row(gen_bus),
        row(gen_curvature),
    )
    both = pl.pallas_call(
        functools.partial(kernel, n, group),
        out_shape=pltpu.VMEM((2, 2, scen, buses), F32),
        in_specs=[pl.BlockSpec(memory_space=pltpu.HBM)] * 13,
        out_specs=pl.BlockSpec(memory_space=pltpu.VMEM),
        scratch_shapes=[
            *(pltpu.VMEM(a.shape, a.dtype) for a in operands),
            dma(13),
            pltpu.VMEM((8, span), F32),
            pltpu.VMEM((8, span), F32),
            pltpu.VMEM((4 * scen, 2 * LANES), F32),
            pltpu.VMEM((2 * LANES, 2 * span), BF16),
            pltpu.VMEM((2 * span, 2 * LANES), BF16),
            pltpu.VMEM((2, rows, LANES), F32),
            pltpu.VMEM((2, rows, LANES), F32),
            pltpu.VMEM((2, 5 * scen, LANES), F32),
            pltpu.VMEM((2, 5 * scen, LANES), F32),
            pltpu.VMEM((ITERS - 1, 2, 2 * scen, LANES), F32),
            pltpu.VMEM((ITERS - 1, 2, 2 * scen, LANES), F32),
            pltpu.VMEM((group, 2, LANES), F32),
            pltpu.VMEM((outer, 2, LANES), F32),
            dma(2),
            dma(2),
            dma(2),
            dma(2),
            dma(ITERS - 1, 2),
            dma(ITERS - 1, 2),
            dma(group),
            dma(group),
            dma(outer),
            dma(outer),
        ],
        compiler_params=pltpu.CompilerParams(
            collective_id=0, has_side_effects=True, vmem_limit_bytes=62 * 1024 * 1024
        ),
        name="newton",
    )(*operands)
    return both[0].transpose(2, 0, 1), both[1].transpose(2, 0, 1)


def solution(mesh):
    placed = (
        P("net", "scen"),
        P("net", "scen"),
        P("net", None, "scen"),
        P("net"),
        P("net"),
        P("net"),
        P("net"),
        P("net"),
        P("net"),
        P(None, "net", "scen"),
        P(None, "net", "scen"),
        P("net"),
        P("net"),
    )
    return jax.shard_map(
        functools.partial(body, mesh.shape["net"]),
        mesh=mesh,
        in_specs=placed,
        out_specs=(P("net", None, "scen"), P("net", None, "scen")),
        check_vma=False,
    )
```

```python
import functools

import jax
import jax.numpy as jnp
from jax import lax
from jax.experimental import pallas as pl
from jax.experimental.pallas import tpu as pltpu
from jax.sharding import PartitionSpec as P

MESH = pl.DeviceIdType.MESH
F32, BF16 = jnp.float32, jnp.bfloat16
ITERS = 4
LANES = 128
OWN = 2

barrier_weight = 0.01
volt_low = 0.9
volt_high = 1.1
angle_reg = 0.5


def sine_cosine(angle):
    square = angle * angle
    sine = 1.0 / 6227020800.0
    for term in (-1.0 / 39916800.0, 1.0 / 362880.0, -1.0 / 5040.0, 1.0 / 120.0, -1.0 / 6.0, 1.0):
        sine = sine * square + term
    cosine = -1.0 / 87178291200.0
    for term in (1.0 / 479001600.0, -1.0 / 3628800.0, 1.0 / 40320.0, -1.0 / 720.0, 1.0 / 24.0, -0.5, 1.0):
        cosine = cosine * square + term
    return sine * angle, cosine


def branch_blocks(mag_from, mag_to, sine, cosine, conduct, suscept, weight_p, weight_q):
    along = conduct * cosine + suscept * sine
    across = conduct * sine - suscept * cosine
    cross = mag_from * mag_to
    jp = (2.0 * conduct * mag_from - mag_to * along, cross * across, -mag_from * along, -cross * across)
    jq = (-2.0 * suscept * mag_from - mag_to * across, -cross * along, -mag_from * across, cross * along)
    wp = [weight_p * j for j in jp]
    wq = [weight_q * j for j in jq]

    def entry(i, j):
        return wp[i] * jp[j] + wq[i] * jq[j]

    return (
        (entry(0, 0), entry(0, 1), entry(1, 1)),
        (entry(2, 2), entry(2, 3), entry(3, 3)),
        (entry(0, 2), entry(0, 3), entry(1, 2), entry(1, 3)),
    )


def pieces(values, terms):
    out = []
    for _ in range(terms - 1):
        head = values.astype(BF16)
        out.append(head)
        values = values - head.astype(F32)
    return jnp.concatenate(out + [values.astype(BF16)], axis=0)


def select_dot(values, table, terms):
    rows = values.shape[0]
    out = jnp.dot(pieces(values, terms), table, preferred_element_type=F32)
    total = out[(terms - 1) * rows :]
    for k in range(terms - 2, -1, -1):
        total = total + out[k * rows : (k + 1) * rows]
    return total


def inner(left, right):
    product = left * right
    half = product.shape[0] // 2
    product = product[:half] + product[half:]
    return product[:, :LANES] + product[:, LANES:]


def pack(parts):
    return jnp.sum(jnp.transpose(jnp.concatenate(parts, axis=0)), axis=0, keepdims=True)


def unpack(rows):
    lane = lax.broadcasted_iota(jnp.int32, (1, LANES), 1)
    joined = rows[0]
    for k in range(1, len(rows)):
        joined = jnp.where(lane < 32 * k, joined, pltpu.roll(rows[k], 32 * k, 1))
    columns = jnp.transpose(jnp.broadcast_to(joined, (LANES, LANES)))
    return [columns[32 * k : 32 * k + 32] for k in range(len(rows))]


def galerkin(gram, rhs, n):
    a = {(i, j): gram[(min(i, j), max(i, j))] for i in range(n) for j in range(n)}
    rhs = list(rhs)
    low, inv = {}, {}
    for k in range(n):
        live = a[(k, k)] > 1e-7 * gram[(k, k)]
        inv[k] = jnp.where(live, 1.0 / jnp.where(live, a[(k, k)], 1.0), 0.0)
        for i in range(k + 1, n):
            low[(i, k)] = a[(i, k)] * inv[k]
            for j in range(k + 1, i + 1):
                a[(i, j)] = a[(i, j)] - low[(i, k)] * a[(j, k)]
                a[(j, i)] = a[(i, j)]
            rhs[i] = rhs[i] - low[(i, k)] * rhs[k]
    out = [None] * n
    for k in reversed(range(n)):
        value = rhs[k] * inv[k]
        for i in range(k + 1, n):
            value = value - low[(i, k)] * out[i]
        out[k] = value
    return out


def kernel(
    n,
    group,
    *refs,
):
    inputs, o_ref, loaded, rest = refs[:13], refs[13], refs[14:27], refs[27:]
    x_ref, r_ref = o_ref.at[0], o_ref.at[1]
    load_sem = rest[0]
    me = lax.axis_index("net")
    neighbours = [lax.rem(me + n + d, n) for d in (-1, 1, -2, 2)]
    for peer in neighbours:
        pl.semaphore_signal(pltpu.get_barrier_semaphore(), inc=1, device_id={"net": peer}, device_id_type=MESH)
    loads = []
    for k, (source, target) in enumerate(zip(inputs, loaded)):
        copy = pltpu.make_async_copy(source, target, load_sem.at[k])
        copy.start()
        loads.append(copy)
    solve(n, group, loads, *loaded, x_ref, r_ref, *rest[1:])


def solve(
    n,
    group,
    loads,
    vm_ref,
    va_ref,
    grad_ref,
    from_ref,
    to_ref,
    count_ref,
    bound_ref,
    g_ref,
    b_ref,
    dual_ref,
    slack_ref,
    gbus_ref,
    gcur_ref,
    x_ref,
    r_ref,
    irow,
    frow,
    vin,
    gather_tab,
    scatter_tab,
    blocks,
    a_out,
    a_in,
    f_in,
    b_out,
    b_in,
    w_out,
    w_in,
    x_out,
    x_in,
    y_in,
    red_a,
    red_b,
    send_sem,
    recv_sem,
    a_send,
    a_recv,
    b_send,
    b_recv,
):
    scen, buses = vm_ref.shape
    slots = from_ref.shape[-1]
    ghost = buses // 2
    wide = 2 * LANES
    span = gather_tab.shape[2] // 2
    gens = gbus_ref.shape[1]
    outer = n // group
    me = lax.axis_index("net")
    prev, nxt, prev2, nxt2 = [lax.rem(me + n + d, n) for d in (-1, 1, -2, 2)]
    member = lax.rem(me, group)
    block = lax.div(me, group)
    peers_a = [block * group + lax.rem(member + d, group) for d in range(1, group)]
    peers_b = [lax.rem(block + d, outer) * group + member for d in range(1, outer)]

    barrier = pltpu.get_barrier_semaphore()
    for peer in (*peers_a, *peers_b):
        pl.semaphore_signal(barrier, inc=1, device_id={"net": peer}, device_id_type=MESH)

    pending = []

    def send(message, source, target, peer):
        copy = pltpu.make_async_remote_copy(
            src_ref=source,
            dst_ref=target,
            send_sem=send_sem.at[message],
            recv_sem=recv_sem.at[message],
            device_id={"net": peer},
            device_id_type=MESH,
        )
        copy.start()
        pending.append(copy)
        return copy

    for copy in loads:
        copy.wait()

    irow[...] = jnp.full(irow.shape, -1.0, F32)
    irow[0:1, :slots] = from_ref[...].reshape(1, slots).astype(F32)
    irow[1:2, :slots] = to_ref[...].reshape(1, slots).astype(F32)
    irow[2:3, :buses] = bound_ref[...].astype(F32)
    irow[3:4, :gens] = gbus_ref[...].astype(F32)
    frow[...] = jnp.zeros(frow.shape, F32)
    frow[0:1, :slots] = g_ref[...].reshape(1, slots)
    frow[1:2, :slots] = b_ref[...].reshape(1, slots)
    frow[2:3, :gens] = gcur_ref[...]
    from_row, to_row = irow[0:1, :], irow[1:2, :]
    lane_i = lax.broadcasted_iota(jnp.int32, (8, wide), 1)
    lane = lane_i.astype(F32)
    plain = irow[0:8, :wide]
    rolled = pltpu.roll(plain, LANES - ghost, 1)
    upper = (lane_i >= LANES) & (lane_i < LANES + ghost)
    place = jnp.where(lane_i < ghost, plain, jnp.where(upper, rolled, -2.0))[2:3]
    entry = jnp.where(lane_i < ghost, lane, jnp.where(upper, lane - (LANES - ghost), -1e6))[0:1]

    def column(row):
        return jnp.transpose(jnp.broadcast_to(row, (LANES, row.shape[1])))

    def hot(mask):
        return jnp.where(mask, 1.0, 0.0).astype(BF16)

    lanes_of = lambda row, t: row[:, t * LANES : (t + 1) * LANES]

    def index_tables(k, place, from_row, to_row):
        place_col, from_col, to_col = column(place), column(from_row), column(to_row)
        for t in range(span // LANES):
            gather_tab[k, :, t * LANES : (t + 1) * LANES] = hot(place_col == lanes_of(from_row, t))
            gather_tab[k, :, span + t * LANES : span + (t + 1) * LANES] = hot(place_col == lanes_of(to_row, t))
        for t in range(2):
            cols = slice(t * LANES, (t + 1) * LANES)
            scatter_tab[k, 0:span, cols] = hot(from_col == lanes_of(place, t))
            scatter_tab[k, span:, cols] = hot(to_col == lanes_of(place, t))
        return place_col, to_col

    place_col, to_col = index_tables(OWN, place, from_row, to_row)
    irow[4:5, :wide] = place
    cross_tab = jnp.concatenate([hot(to_col == lanes_of(entry, t) + buses) for t in range(2)], axis=1)
    bus_row = lane[0:1]
    bus_col = lax.broadcasted_iota(jnp.int32, (wide, LANES), 0).astype(F32)
    to_place = jnp.concatenate([hot(bus_col == lanes_of(place, t)) for t in range(2)], axis=1)
    to_bus = jnp.concatenate([hot(place_col == lanes_of(bus_row, t)) for t in range(2)], axis=1)

    vin[...] = jnp.zeros(vin.shape, F32)
    vin[0:scen, :buses] = vm_ref[...]
    vin[scen : 2 * scen, :buses] = va_ref[...]
    vin[2 * scen : 3 * scen, :buses] = grad_ref[0]
    vin[3 * scen : 4 * scen, :buses] = grad_ref[1]
    placed = select_dot(vin[...], to_place, 3)
    vm, va, start = placed[0:scen], placed[scen : 2 * scen], placed[2 * scen :]

    slot = lax.broadcasted_iota(jnp.int32, (1, slots), 1)
    live = jnp.where(slot < count_ref[...].reshape(1, 1), 1.0, 0.0)
    pad = jnp.zeros((scen, span - slots), F32)
    weight_p = jnp.concatenate([live * dual_ref[0] / slack_ref[0], pad], axis=1)
    weight_q = jnp.concatenate([live * dual_ref[1] / slack_ref[1], pad], axis=1)
    conduct, suscept = frow[0:1, :], frow[1:2, :]
    stacked = jnp.concatenate([weight_p, weight_q, frow[0:8, :]], axis=0)
    crossing = select_dot(stacked, cross_tab, 3)
    payload = jnp.concatenate([vm, va, crossing], axis=0)
    split = lambda v: (v[:, :LANES], v[:, LANES:])
    join = lambda a, b: jnp.concatenate([a, b], axis=1)
    for half, part in enumerate(split(payload)):
        a_out[half] = part

    pl.semaphore_wait(barrier, 4 + (group - 1) + (outer - 1))
    a_near = [send(0, a_out.at[0], a_in.at[1, 0], prev), send(1, a_out.at[1], a_in.at[0, 1], nxt)]

    def local_blocks(k, volts, weight_p, weight_q, conduct, suscept):
        ends = select_dot(volts, gather_tab[k], 3)
        sine, cosine = sine_cosine(ends[scen:, :span] - ends[scen:, span:])
        hff, htt, hft = branch_blocks(
            ends[:scen, :span], ends[:scen, span:], sine, cosine, conduct, suscept, weight_p, weight_q
        )
        for e in range(4):
            blocks[k, e] = hft[e]
        return hff, htt

    local = jnp.where((to_row >= 0.0) & (to_row < float(buses)), 1.0, 0.0)
    weight_p, weight_q = weight_p * local, weight_q * local
    hff, htt = local_blocks(OWN, placed[0 : 2 * scen], weight_p, weight_q, conduct, suscept)
    both = jnp.concatenate([join(a, b) for a, b in zip(hff, htt)], axis=0)
    diag = select_dot(both, scatter_tab[OWN], 3)
    gen = column(irow[3:4, :LANES])
    curve = column(frow[2:3, :LANES])
    gen_sum = join(
        *(jnp.sum(jnp.where(gen == lanes_of(place, t), curve, 0.0), axis=0, keepdims=True) for t in range(2))
    )
    low, high = vm - volt_low, volt_high - vm
    base_vv = barrier_weight / (low * low) + barrier_weight / (high * high) + gen_sum
    base_aa = angle_reg + gen_sum
    own = jnp.concatenate(
        [diag[0:scen] + base_vv, diag[scen : 2 * scen], diag[2 * scen :] + base_aa, start], axis=0
    )
    for half, part in enumerate(split(own)):
        b_out[half] = part
    b_near = [send(2, b_out.at[0], b_in.at[1, 0], prev), send(3, b_out.at[1], b_in.at[0, 1], nxt)]

    w_out[0:scen] = weight_p
    w_out[scen : 2 * scen] = weight_q
    w_out[2 * scen : 2 * scen + 8] = irow[...]
    w_out[2 * scen + 8 :] = frow[...]
    rows = pl.ds(0, 3 * scen)
    far = [
        send(4, w_out, w_in.at[1], prev),
        send(5, w_out, w_in.at[0], nxt),
        send(6, a_out.at[1], a_in.at[1, 1], prev),
        send(7, a_out.at[0], a_in.at[0, 0], nxt),
        send(8, a_out.at[0], f_in.at[1], prev2),
        send(9, a_out.at[1], f_in.at[0], nxt2),
        send(10, b_out.at[1, rows], b_in.at[1, 1, rows], prev),
        send(11, b_out.at[0, rows], b_in.at[0, 0, rows], nxt),
    ]

    def coupling(here, there):
        vm, va, p, q = (here[k * scen : (k + 1) * scen] for k in range(4))
        there_vm, there_va, there_p, there_q = (there[k * scen : (k + 1) * scen] for k in range(4))
        g, b = here[4 * scen : 4 * scen + 1], here[4 * scen + 1 : 4 * scen + 2]
        there_g, there_b = there[4 * scen : 4 * scen + 1], there[4 * scen + 1 : 4 * scen + 2]
        sine, cosine = sine_cosine(va - there_va)
        off, reach, (o00, o01, o10, o11) = branch_blocks(vm, there_vm, sine, cosine, g, b, p, q)
        root, on, (i00, i01, i10, i11) = branch_blocks(there_vm, vm, -sine, cosine, there_g, there_b, there_p, there_q)
        return (off, on), (reach, root), (o00 + i00, o01 + i10, o10 + i01, o11 + i11)

    def inverse_of(fields, parts):
        first, second = parts
        d00, d01, d11 = (fields[k * scen : (k + 1) * scen] + first[k] + second[k] for k in range(3))
        inverse = 1.0 / (d00 * d11 - d01 * d01)
        return d11 * inverse, -d01 * inverse, d00 * inverse

    def applied(fields, v):
        b00, b01, b11 = fields
        return jnp.concatenate([b00 * v[:scen] + b01 * v[scen:], b01 * v[:scen] + b11 * v[scen:]], axis=0)

    def coupled(c, v):
        v0, v1 = v[:scen], v[scen:]
        return jnp.concatenate([c[0] * v0 + c[1] * v1, c[2] * v0 + c[3] * v1], axis=0)

    for copy in a_near:
        copy.wait_recv()
    here_parts, there_parts, border = coupling(payload, join(a_in[0, 1], a_in[1, 0]))
    border_back = (border[0], border[2], border[1], border[3])
    diag_inverse = inverse_of(own, here_parts)

    for copy in b_near:
        copy.wait_recv()
    beyond = join(b_in[0, 1], b_in[1, 0])
    facing_inverse = inverse_of(beyond, there_parts)
    facing = applied(facing_inverse, beyond[3 * scen :])

    def inside_product(k, v):
        ends = select_dot(v, gather_tab[k], 2)
        f0, f1, t0, t1 = ends[:scen, :span], ends[scen:, :span], ends[:scen, span:], ends[scen:, span:]
        h00, h01, h10, h11 = (blocks[k, e] for e in range(4))
        terms = jnp.concatenate(
            [
                join(h00 * t0 + h01 * t1, h00 * f0 + h10 * f1),
                join(h10 * t0 + h11 * t1, h01 * f0 + h11 * f1),
            ],
            axis=0,
        )
        return select_dot(terms, scatter_tab[k], 2)

    s, u = [start], [applied(diag_inverse, start)]
    s.append(inside_product(OWN, u[0]) + coupled(border, facing))
    u.append(applied(diag_inverse, s[1]))
    for half, part in enumerate(split(u[1])):
        x_out[half] = part
    vectors = [
        send(12, x_out, x_in.at[1], prev),
        send(13, x_out, x_in.at[0], nxt),
        send(14, x_out.at[0], y_in.at[1], prev2),
        send(15, x_out.at[1], y_in.at[0], nxt2),
    ]

    for copy in far:
        copy.wait_recv()
    inside = inside_product(OWN, u[1])
    outer_border, side_inverse = [], []
    for k in range(2):
        index, value = w_in[k, 2 * scen : 2 * scen + 8], w_in[k, 2 * scen + 8 :]
        index_tables(k, index[4:5, :wide], index[0:1], index[1:2])
        volts = join(a_in[k, 0, : 2 * scen], a_in[k, 1, : 2 * scen])
        local_blocks(k, volts, w_in[k, :scen], w_in[k, scen : 2 * scen], value[0:1], value[1:2])
        parts, _, fields = coupling(a_in[k, k], f_in[k])
        outer_border.append(fields)
        outside = inverse_of(b_in[k, k, : 3 * scen], parts)
        near = [split(f)[k] for f in facing_inverse]
        side_inverse.append([join(f, g) if k else join(g, f) for f, g in zip(near, outside)])

    for copy in vectors:
        copy.wait_recv()
    side = [join(x_in[k, 0], x_in[k, 1]) for k in range(2)]
    for j in (2, 3):
        facing = join(split(side[0])[1], split(side[1])[0])
        s.append(inside + coupled(border, facing))
        back = split(coupled(border_back, u[-1]))
        for k in range(2):
            near, outside = back[k], coupled(outer_border[k], y_in[k]) if j == 2 else jnp.zeros_like(back[k])
            product = inside_product(k, side[k]) + (join(near, outside) if k else join(outside, near))
            side[k] = applied(side_inverse[k], product)
        u.append(applied(diag_inverse, s[-1]))
        inside = inside_product(OWN, u[-1])
    facing = join(split(side[0])[1], split(side[1])[0])
    s.append(inside + coupled(border, facing))

    def all_sum(tile):
        red_a[pl.ds(member, 1)] = tile[None]
        copies = []
        for d, peer in enumerate(peers_a):
            copy = pltpu.make_async_remote_copy(
                src_ref=red_a.at[member],
                dst_ref=red_a.at[member],
                send_sem=a_send.at[d],
                recv_sem=a_recv.at[d],
                device_id={"net": peer},
                device_id_type=MESH,
            )
            copy.start()
            copies.append(copy)
        for copy in copies:
            copy.wait_recv()
        pending.extend(copies)
        total = red_a[0]
        for k in range(1, group):
            total = total + red_a[k]
        red_b[pl.ds(block, 1)] = total[None]
        copies = []
        for d, peer in enumerate(peers_b):
            copy = pltpu.make_async_remote_copy(
                src_ref=red_b.at[block],
                dst_ref=red_b.at[block],
                send_sem=b_send.at[d],
                recv_sem=b_recv.at[d],
                device_id={"net": peer},
                device_id_type=MESH,
            )
            copy.start()
            copies.append(copy)
        for copy in copies:
            copy.wait_recv()
        pending.extend(copies)
        total = red_b[0]
        for k in range(1, outer):
            total = total + red_b[k]
        return total

    parts = [inner(u[k // 2], s[k - k // 2]) for k in range(2 * ITERS)]
    total = all_sum(jnp.concatenate([pack(parts[:4]), pack(parts[4:])], axis=0))
    moments = [total[k // 4 : k // 4 + 1] for k in range(2 * ITERS)]
    moments = [pltpu.roll(m, LANES - 32 * (k % 4), 1) if k % 4 else m for k, m in enumerate(moments)]
    gram = {(i, j): moments[i + j] + moments[i + j + 1] for i in range(ITERS) for j in range(i, ITERS)}
    w = unpack(galerkin(gram, moments[ITERS:], ITERS))
    w = [jnp.concatenate([jnp.concatenate([c, c], axis=1)] * 2, axis=0) for c in w]
    step = (1.0 + w[0]) * u[0] + (w[1] - 1.0) * u[1] + (1.0 + w[2]) * u[2] + (w[3] - 1.0) * u[3]
    residual = (1.0 - w[3]) * s[4] - (w[2] + w[3]) * s[3] - (w[1] + w[2]) * s[2] - (w[0] + w[1]) * s[1] - w[0] * s[0]
    out = select_dot(jnp.concatenate([step, residual], axis=0), to_bus, 3)
    for c in range(2):
        x_ref[c] = out[c * scen : (c + 1) * scen, :buses]
        r_ref[c] = out[(2 + c) * scen : (3 + c) * scen, :buses]

    for copy in pending:
        copy.wait_send()


def body(
    n,
    volt_mag,
    volt_ang,
    gradient,
    branch_from,
    branch_to,
    branch_count,
    boundary,
    conductance,
    susceptance,
    duals,
    slacks,
    gen_bus,
    gen_curvature,
):
    buses, scen = volt_mag.shape
    slots = branch_from.shape[0]
    span = -(-slots // LANES) * LANES
    group = 16 if n % 16 == 0 and n > 16 else 4 if n % 4 == 0 else 1
    outer = n // group
    row = lambda a: a.reshape(1, -1)
    rows = 4 * scen + 8
    dma = lambda *shape: pltpu.SemaphoreType.DMA(shape)
    operands = (
        volt_mag.T,
        volt_ang.T,
        gradient.transpose(1, 2, 0),
        branch_from,
        branch_to,
        branch_count,
        row(boundary),
        conductance,
        susceptance,
        duals.transpose(0, 2, 1),
        slacks.transpose(0, 2, 1),
        row(gen_bus),
        row(gen_curvature),
    )
    both = pl.pallas_call(
        functools.partial(kernel, n, group),
        out_shape=pltpu.VMEM((2, 2, scen, buses), F32),
        in_specs=[pl.BlockSpec(memory_space=pltpu.HBM)] * 13,
        out_specs=pl.BlockSpec(memory_space=pltpu.VMEM),
        scratch_shapes=[
            *(pltpu.VMEM(a.shape, a.dtype) for a in operands),
            dma(13),
            pltpu.VMEM((8, span), F32),
            pltpu.VMEM((8, span), F32),
            pltpu.VMEM((4 * scen, 2 * LANES), F32),
            pltpu.VMEM((3, 2 * LANES, 2 * span), BF16),
            pltpu.VMEM((3, 2 * span, 2 * LANES), BF16),
            pltpu.VMEM((3, 4, scen, span), F32),
            pltpu.VMEM((2, rows, LANES), F32),
            pltpu.VMEM((2, 2, rows, LANES), F32),
            pltpu.VMEM((2, rows, LANES), F32),
            pltpu.VMEM((2, 5 * scen, LANES), F32),
            pltpu.VMEM((2, 2, 5 * scen, LANES), F32),
            pltpu.VMEM((2 * scen + 16, span), F32),
            pltpu.VMEM((2, 2 * scen + 16, span), F32),
            pltpu.VMEM((2, 2 * scen, LANES), F32),
            pltpu.VMEM((2, 2, 2 * scen, LANES), F32),
            pltpu.VMEM((2, 2 * scen, LANES), F32),
            pltpu.VMEM((group, 2, LANES), F32),
            pltpu.VMEM((outer, 2, LANES), F32),
            dma(16),
            dma(16),
            dma(group),
            dma(group),
            dma(outer),
            dma(outer),
        ],
        compiler_params=pltpu.CompilerParams(
            collective_id=0, has_side_effects=True, vmem_limit_bytes=62 * 1024 * 1024
        ),
        name="newton",
    )(*operands)
    return both[0].transpose(2, 0, 1), both[1].transpose(2, 0, 1)


def solution(mesh):
    placed = (
        P("net", "scen"),
        P("net", "scen"),
        P("net", None, "scen"),
        P("net"),
        P("net"),
        P("net"),
        P("net"),
        P("net"),
        P("net"),
        P(None, "net", "scen"),
        P(None, "net", "scen"),
        P("net"),
        P("net"),
    )
    return jax.shard_map(
        functools.partial(body, mesh.shape["net"]),
        mesh=mesh,
        in_specs=placed,
        out_specs=(P("net", None, "scen"), P("net", None, "scen")),
        check_vma=False,
    )
```

```python
import functools

import jax
import jax.numpy as jnp
from jax import lax
from jax.experimental import pallas as pl
from jax.experimental.pallas import tpu as pltpu
from jax.sharding import PartitionSpec as P

MESH = pl.DeviceIdType.MESH
F32, BF16 = jnp.float32, jnp.bfloat16
ITERS = 4
LANES = 128
OWN = 2

barrier_weight = 0.01
volt_low = 0.9
volt_high = 1.1
angle_reg = 0.5


def sine_cosine(angle):
    square = angle * angle
    sine = 1.0 / 6227020800.0
    for term in (-1.0 / 39916800.0, 1.0 / 362880.0, -1.0 / 5040.0, 1.0 / 120.0, -1.0 / 6.0, 1.0):
        sine = sine * square + term
    cosine = -1.0 / 87178291200.0
    for term in (1.0 / 479001600.0, -1.0 / 3628800.0, 1.0 / 40320.0, -1.0 / 720.0, 1.0 / 24.0, -0.5, 1.0):
        cosine = cosine * square + term
    return sine * angle, cosine


def branch_blocks(mag_from, mag_to, sine, cosine, conduct, suscept, weight_p, weight_q):
    along = conduct * cosine + suscept * sine
    across = conduct * sine - suscept * cosine
    cross = mag_from * mag_to
    jp = (2.0 * conduct * mag_from - mag_to * along, cross * across, -mag_from * along, -cross * across)
    jq = (-2.0 * suscept * mag_from - mag_to * across, -cross * along, -mag_from * across, cross * along)
    wp = [weight_p * j for j in jp]
    wq = [weight_q * j for j in jq]

    def entry(i, j):
        return wp[i] * jp[j] + wq[i] * jq[j]

    return (
        (entry(0, 0), entry(0, 1), entry(1, 1)),
        (entry(2, 2), entry(2, 3), entry(3, 3)),
        (entry(0, 2), entry(0, 3), entry(1, 2), entry(1, 3)),
    )


def pieces(values, terms):
    out = []
    for _ in range(terms - 1):
        head = values.astype(BF16)
        out.append(head)
        values = values - head.astype(F32)
    return jnp.concatenate(out + [values.astype(BF16)], axis=0)


def select_dot(values, table, terms):
    rows = values.shape[0]
    out = jnp.dot(pieces(values, terms), table, preferred_element_type=F32)
    total = out[(terms - 1) * rows :]
    for k in range(terms - 2, -1, -1):
        total = total + out[k * rows : (k + 1) * rows]
    return total


def inner(left, right):
    product = left * right
    half = product.shape[0] // 2
    product = product[:half] + product[half:]
    return product[:, :LANES] + product[:, LANES:]


def pack(parts):
    return jnp.sum(jnp.transpose(jnp.concatenate(parts, axis=0)), axis=0, keepdims=True)


def unpack(rows):
    lane = lax.broadcasted_iota(jnp.int32, (1, LANES), 1)
    joined = rows[0]
    for k in range(1, len(rows)):
        joined = jnp.where(lane < 32 * k, joined, pltpu.roll(rows[k], 32 * k, 1))
    columns = jnp.transpose(jnp.broadcast_to(joined, (LANES, LANES)))
    return [columns[32 * k : 32 * k + 32] for k in range(len(rows))]


def galerkin(gram, rhs, n):
    a = {(i, j): gram[(min(i, j), max(i, j))] for i in range(n) for j in range(n)}
    rhs = list(rhs)
    low, inv = {}, {}
    for k in range(n):
        live = a[(k, k)] > 1e-7 * gram[(k, k)]
        inv[k] = jnp.where(live, 1.0 / jnp.where(live, a[(k, k)], 1.0), 0.0)
        for i in range(k + 1, n):
            low[(i, k)] = a[(i, k)] * inv[k]
            for j in range(k + 1, i + 1):
                a[(i, j)] = a[(i, j)] - low[(i, k)] * a[(j, k)]
                a[(j, i)] = a[(i, j)]
            rhs[i] = rhs[i] - low[(i, k)] * rhs[k]
    out = [None] * n
    for k in reversed(range(n)):
        value = rhs[k] * inv[k]
        for i in range(k + 1, n):
            value = value - low[(i, k)] * out[i]
        out[k] = value
    return out


def partners(n):
    return (-1, 1, -2, 2, -16, 16) if n > 32 else (-1, 1, -2, 2)


def kernel(
    n,
    group,
    *refs,
):
    inputs, o_ref, loaded, rest = refs[:13], refs[13], refs[14:27], refs[27:]
    x_ref, r_ref = o_ref.at[0], o_ref.at[1]
    load_sem = rest[0]
    me = lax.axis_index("net")
    neighbours = [lax.rem(me + n + d, n) for d in partners(n)]
    for peer in neighbours:
        pl.semaphore_signal(pltpu.get_barrier_semaphore(), inc=1, device_id={"net": peer}, device_id_type=MESH)
    loads = []
    for k, (source, target) in enumerate(zip(inputs, loaded)):
        copy = pltpu.make_async_copy(source, target, load_sem.at[k])
        copy.start()
        loads.append(copy)
    solve(n, group, loads, *loaded, x_ref, r_ref, *rest[1:])


def solve(
    n,
    group,
    loads,
    vm_ref,
    va_ref,
    grad_ref,
    from_ref,
    to_ref,
    count_ref,
    bound_ref,
    g_ref,
    b_ref,
    dual_ref,
    slack_ref,
    gbus_ref,
    gcur_ref,
    x_ref,
    r_ref,
    irow,
    frow,
    vin,
    gather_tab,
    scatter_tab,
    blocks,
    a_out,
    a_in,
    f_in,
    b_out,
    b_in,
    w_out,
    w_in,
    x_out,
    x_in,
    y_in,
    red_a,
    red_b,
    send_sem,
    recv_sem,
    a_send,
    a_recv,
    b_send,
    b_recv,
    known_sem,
):
    scen, buses = vm_ref.shape
    slots = from_ref.shape[-1]
    ghost = buses // 2
    wide = 2 * LANES
    span = gather_tab.shape[2] // 2
    gens = gbus_ref.shape[1]
    outer = n // group
    me = lax.axis_index("net")
    prev, nxt, prev2, nxt2 = [lax.rem(me + n + d, n) for d in (-1, 1, -2, 2)]
    member = lax.rem(me, group)
    block = lax.div(me, group)
    peers_a = [block * group + lax.rem(member + d, group) for d in range(1, group)]
    peers_b = [lax.rem(block + d, outer) * group + member for d in range(1, outer)]

    barrier = pltpu.get_barrier_semaphore()
    spans = [[d for d in step if d < n // 2] for step in ((2, 16), (4, 32), (8,))]

    def tell(step):
        for d in spans[step]:
            for at in (n - d, d):
                pl.semaphore_signal(
                    known_sem.at[step], inc=1, device_id={"net": lax.rem(me + at, n)}, device_id_type=MESH
                )

    def told(step):
        if spans[step]:
            pl.semaphore_wait(known_sem.at[step], 2 * len(spans[step]))

    core = lax.rem(me, 2)
    mate = me + 1 - 2 * core
    beyond_mate = lax.rem(me + n + 2 - 4 * core, n)
    pending = []

    def send(message, source, target, peer):
        copy = pltpu.make_async_remote_copy(
            src_ref=source,
            dst_ref=target,
            send_sem=send_sem.at[message],
            recv_sem=recv_sem.at[message],
            device_id={"net": peer},
            device_id_type=MESH,
        )
        copy.start()
        pending.append(copy)
        return copy

    for copy in loads:
        copy.wait()

    irow[...] = jnp.full(irow.shape, -1.0, F32)
    irow[0:1, :slots] = from_ref[...].reshape(1, slots).astype(F32)
    irow[1:2, :slots] = to_ref[...].reshape(1, slots).astype(F32)
    irow[2:3, :buses] = bound_ref[...].astype(F32)
    irow[3:4, :gens] = gbus_ref[...].astype(F32)
    frow[...] = jnp.zeros(frow.shape, F32)
    frow[0:1, :slots] = g_ref[...].reshape(1, slots)
    frow[1:2, :slots] = b_ref[...].reshape(1, slots)
    frow[2:3, :gens] = gcur_ref[...]
    from_row, to_row = irow[0:1, :], irow[1:2, :]
    lane_i = lax.broadcasted_iota(jnp.int32, (8, wide), 1)
    lane = lane_i.astype(F32)
    plain = irow[0:8, :wide]
    rolled = pltpu.roll(plain, LANES - ghost, 1)
    upper = (lane_i >= LANES) & (lane_i < LANES + ghost)
    place = jnp.where(lane_i < ghost, plain, jnp.where(upper, rolled, -2.0))[2:3]
    entry = jnp.where(lane_i < ghost, lane, jnp.where(upper, lane - (LANES - ghost), -1e6))[0:1]

    def column(row):
        return jnp.transpose(jnp.broadcast_to(row, (LANES, row.shape[1])))

    def hot(mask):
        return jnp.where(mask, 1.0, 0.0).astype(BF16)

    lanes_of = lambda row, t: row[:, t * LANES : (t + 1) * LANES]

    def index_tables(k, place, from_row, to_row):
        place_col, from_col, to_col = column(place), column(from_row), column(to_row)
        for t in range(span // LANES):
            gather_tab[k, :, t * LANES : (t + 1) * LANES] = hot(place_col == lanes_of(from_row, t))
            gather_tab[k, :, span + t * LANES : span + (t + 1) * LANES] = hot(place_col == lanes_of(to_row, t))
        for t in range(2):
            cols = slice(t * LANES, (t + 1) * LANES)
            scatter_tab[k, 0:span, cols] = hot(from_col == lanes_of(place, t))
            scatter_tab[k, span:, cols] = hot(to_col == lanes_of(place, t))
        return place_col, to_col

    place_col, to_col = index_tables(OWN, place, from_row, to_row)
    irow[4:5, :wide] = place
    cross_tab = jnp.concatenate([hot(to_col == lanes_of(entry, t) + buses) for t in range(2)], axis=1)
    bus_row = lane[0:1]
    bus_col = lax.broadcasted_iota(jnp.int32, (wide, LANES), 0).astype(F32)
    to_place = jnp.concatenate([hot(bus_col == lanes_of(place, t)) for t in range(2)], axis=1)
    to_bus = jnp.concatenate([hot(place_col == lanes_of(bus_row, t)) for t in range(2)], axis=1)

    vin[...] = jnp.zeros(vin.shape, F32)
    vin[0:scen, :buses] = vm_ref[...]
    vin[scen : 2 * scen, :buses] = va_ref[...]
    vin[2 * scen : 3 * scen, :buses] = grad_ref[0]
    vin[3 * scen : 4 * scen, :buses] = grad_ref[1]
    placed = select_dot(vin[...], to_place, 3)
    vm, va, start = placed[0:scen], placed[scen : 2 * scen], placed[2 * scen :]

    slot = lax.broadcasted_iota(jnp.int32, (1, slots), 1)
    live = jnp.where(slot < count_ref[...].reshape(1, 1), 1.0, 0.0)
    pad = jnp.zeros((scen, span - slots), F32)
    weight_p = jnp.concatenate([live * dual_ref[0] / slack_ref[0], pad], axis=1)
    weight_q = jnp.concatenate([live * dual_ref[1] / slack_ref[1], pad], axis=1)
    conduct, suscept = frow[0:1, :], frow[1:2, :]
    stacked = jnp.concatenate([weight_p, weight_q, frow[0:8, :]], axis=0)
    crossing = select_dot(stacked, cross_tab, 3)
    payload = jnp.concatenate([vm, va, crossing], axis=0)
    split = lambda v: (v[:, :LANES], v[:, LANES:])
    join = lambda a, b: jnp.concatenate([a, b], axis=1)
    for half, part in enumerate(split(payload)):
        a_out[half] = part

    pl.semaphore_wait(barrier, len(partners(n)))
    a_near = [send(0, a_out.at[0], a_in.at[1, 0], prev), send(1, a_out.at[1], a_in.at[0, 1], nxt)]

    def local_blocks(k, volts, weight_p, weight_q, conduct, suscept):
        ends = select_dot(volts, gather_tab[k], 3)
        sine, cosine = sine_cosine(ends[scen:, :span] - ends[scen:, span:])
        hff, htt, hft = branch_blocks(
            ends[:scen, :span], ends[:scen, span:], sine, cosine, conduct, suscept, weight_p, weight_q
        )
        for e in range(4):
            blocks[k, e] = hft[e]
        return hff, htt

    local = jnp.where((to_row >= 0.0) & (to_row < float(buses)), 1.0, 0.0)
    weight_p, weight_q = weight_p * local, weight_q * local
    hff, htt = local_blocks(OWN, placed[0 : 2 * scen], weight_p, weight_q, conduct, suscept)
    both = jnp.concatenate([join(a, b) for a, b in zip(hff, htt)], axis=0)
    diag = select_dot(both, scatter_tab[OWN], 3)
    gen = column(irow[3:4, :LANES])
    curve = column(frow[2:3, :LANES])
    gen_sum = join(
        *(jnp.sum(jnp.where(gen == lanes_of(place, t), curve, 0.0), axis=0, keepdims=True) for t in range(2))
    )
    low, high = vm - volt_low, volt_high - vm
    base_vv = barrier_weight / (low * low) + barrier_weight / (high * high) + gen_sum
    base_aa = angle_reg + gen_sum
    own = jnp.concatenate(
        [diag[0:scen] + base_vv, diag[scen : 2 * scen], diag[2 * scen :] + base_aa, start], axis=0
    )
    for half, part in enumerate(split(own)):
        b_out[half] = part
    b_near = [send(2, b_out.at[0], b_in.at[1, 0], prev), send(3, b_out.at[1], b_in.at[0, 1], nxt)]

    tell(0)

    w_out[0:scen] = weight_p
    w_out[scen : 2 * scen] = weight_q
    irow[5:7] = frow[0:2]
    w_out[2 * scen :] = irow[...]
    rows = pl.ds(0, 3 * scen)
    far = [
        send(4, w_out, w_in.at[1], prev),
        send(5, w_out, w_in.at[0], nxt),
        send(6, a_out.at[1], a_in.at[1, 1], prev),
        send(7, a_out.at[0], a_in.at[0, 0], nxt),
        send(8, a_out.at[1 - core], f_in.at[core], beyond_mate),
        send(10, b_out.at[1, rows], b_in.at[1, 1, rows], prev),
        send(11, b_out.at[0, rows], b_in.at[0, 0, rows], nxt),
    ]

    def coupling(here, there):
        vm, va, p, q = (here[k * scen : (k + 1) * scen] for k in range(4))
        there_vm, there_va, there_p, there_q = (there[k * scen : (k + 1) * scen] for k in range(4))
        g, b = here[4 * scen : 4 * scen + 1], here[4 * scen + 1 : 4 * scen + 2]
        there_g, there_b = there[4 * scen : 4 * scen + 1], there[4 * scen + 1 : 4 * scen + 2]
        sine, cosine = sine_cosine(va - there_va)
        off, reach, (o00, o01, o10, o11) = branch_blocks(vm, there_vm, sine, cosine, g, b, p, q)
        root, on, (i00, i01, i10, i11) = branch_blocks(there_vm, vm, -sine, cosine, there_g, there_b, there_p, there_q)
        return (off, on), (reach, root), (o00 + i00, o01 + i10, o10 + i01, o11 + i11)

    def inverse_of(fields, parts):
        first, second = parts
        d00, d01, d11 = (fields[k * scen : (k + 1) * scen] + first[k] + second[k] for k in range(3))
        inverse = 1.0 / (d00 * d11 - d01 * d01)
        return d11 * inverse, -d01 * inverse, d00 * inverse

    def applied(fields, v):
        b00, b01, b11 = fields
        return jnp.concatenate([b00 * v[:scen] + b01 * v[scen:], b01 * v[:scen] + b11 * v[scen:]], axis=0)

    def coupled(c, v):
        v0, v1 = v[:scen], v[scen:]
        return jnp.concatenate([c[0] * v0 + c[1] * v1, c[2] * v0 + c[3] * v1], axis=0)

    for copy in a_near:
        copy.wait_recv()
    told(0)
    tell(1)
    far.append(send(9, a_in.at[core, 1 - core], f_in.at[core], mate))
    here_parts, there_parts, border = coupling(payload, join(a_in[0, 1], a_in[1, 0]))
    border_back = (border[0], border[2], border[1], border[3])
    diag_inverse = inverse_of(own, here_parts)

    for copy in b_near:
        copy.wait_recv()
    beyond = join(b_in[0, 1], b_in[1, 0])
    facing_inverse = inverse_of(beyond, there_parts)
    facing = applied(facing_inverse, beyond[3 * scen :])

    def inside_product(k, v):
        ends = select_dot(v, gather_tab[k], 2)
        f0, f1, t0, t1 = ends[:scen, :span], ends[scen:, :span], ends[:scen, span:], ends[scen:, span:]
        h00, h01, h10, h11 = (blocks[k, e] for e in range(4))
        terms = jnp.concatenate(
            [
                join(h00 * t0 + h01 * t1, h00 * f0 + h10 * f1),
                join(h10 * t0 + h11 * t1, h01 * f0 + h11 * f1),
            ],
            axis=0,
        )
        return select_dot(terms, scatter_tab[k], 2)

    s, u = [start], [applied(diag_inverse, start)]
    s.append(inside_product(OWN, u[0]) + coupled(border, facing))
    u.append(applied(diag_inverse, s[1]))
    for half, part in enumerate(split(u[1])):
        x_out[half] = part
    vectors = [
        send(12, x_out, x_in.at[1], prev),
        send(13, x_out, x_in.at[0], nxt),
        send(14, x_out.at[0], y_in.at[1], prev2),
        send(15, x_out.at[1], y_in.at[0], nxt2),
    ]

    told(1)
    tell(2)

    for copy in far:
        copy.wait_recv()
    inside = inside_product(OWN, u[1])
    outer_border, side_inverse = [], []
    for k in range(2):
        index = w_in[k, 2 * scen :]
        index_tables(k, index[4:5, :wide], index[0:1], index[1:2])
        volts = join(a_in[k, 0, : 2 * scen], a_in[k, 1, : 2 * scen])
        local_blocks(k, volts, w_in[k, :scen], w_in[k, scen : 2 * scen], index[5:6], index[6:7])
        parts, _, fields = coupling(a_in[k, k], f_in[k])
        outer_border.append(fields)
        outside = inverse_of(b_in[k, k, : 3 * scen], parts)
        near = [split(f)[k] for f in facing_inverse]
        side_inverse.append([join(f, g) if k else join(g, f) for f, g in zip(near, outside)])

    for copy in vectors:
        copy.wait_recv()
    side = [join(x_in[k, 0], x_in[k, 1]) for k in range(2)]
    for j in (2, 3):
        facing = join(split(side[0])[1], split(side[1])[0])
        s.append(inside + coupled(border, facing))
        back = split(coupled(border_back, u[-1]))
        for k in range(2):
            near, outside = back[k], coupled(outer_border[k], y_in[k]) if j == 2 else jnp.zeros_like(back[k])
            product = inside_product(k, side[k]) + (join(near, outside) if k else join(outside, near))
            side[k] = applied(side_inverse[k], product)
        u.append(applied(diag_inverse, s[-1]))
        inside = inside_product(OWN, u[-1])
    facing = join(split(side[0])[1], split(side[1])[0])
    s.append(inside + coupled(border, facing))

    def all_sum(tile):
        red_a[pl.ds(member, 1)] = tile[None]
        copies = []
        for d, peer in enumerate(peers_a):
            copy = pltpu.make_async_remote_copy(
                src_ref=red_a.at[member],
                dst_ref=red_a.at[member],
                send_sem=a_send.at[d],
                recv_sem=a_recv.at[d],
                device_id={"net": peer},
                device_id_type=MESH,
            )
            copy.start()
            copies.append(copy)
        for copy in copies:
            copy.wait_recv()
        pending.extend(copies)
        total = red_a[0]
        for k in range(1, group):
            total = total + red_a[k]
        red_b[pl.ds(block, 1)] = total[None]
        copies = []
        for d, peer in enumerate(peers_b):
            copy = pltpu.make_async_remote_copy(
                src_ref=red_b.at[block],
                dst_ref=red_b.at[block],
                send_sem=b_send.at[d],
                recv_sem=b_recv.at[d],
                device_id={"net": peer},
                device_id_type=MESH,
            )
            copy.start()
            copies.append(copy)
        for copy in copies:
            copy.wait_recv()
        pending.extend(copies)
        total = red_b[0]
        for k in range(1, outer):
            total = total + red_b[k]
        return total

    told(2)
    parts = [inner(u[k // 2], s[k - k // 2]) for k in range(2 * ITERS)]
    total = all_sum(jnp.concatenate([pack(parts[:4]), pack(parts[4:])], axis=0))
    moments = [total[k // 4 : k // 4 + 1] for k in range(2 * ITERS)]
    moments = [pltpu.roll(m, LANES - 32 * (k % 4), 1) if k % 4 else m for k, m in enumerate(moments)]
    gram = {(i, j): moments[i + j] + moments[i + j + 1] for i in range(ITERS) for j in range(i, ITERS)}
    w = unpack(galerkin(gram, moments[ITERS:], ITERS))
    w = [jnp.concatenate([jnp.concatenate([c, c], axis=1)] * 2, axis=0) for c in w]
    step = (1.0 + w[0]) * u[0] + (w[1] - 1.0) * u[1] + (1.0 + w[2]) * u[2] + (w[3] - 1.0) * u[3]
    residual = (1.0 - w[3]) * s[4] - (w[2] + w[3]) * s[3] - (w[1] + w[2]) * s[2] - (w[0] + w[1]) * s[1] - w[0] * s[0]
    out = select_dot(jnp.concatenate([step, residual], axis=0), to_bus, 3)
    for c in range(2):
        x_ref[c] = out[c * scen : (c + 1) * scen, :buses]
        r_ref[c] = out[(2 + c) * scen : (3 + c) * scen, :buses]

    for copy in pending:
        copy.wait_send()


def body(
    n,
    volt_mag,
    volt_ang,
    gradient,
    branch_from,
    branch_to,
    branch_count,
    boundary,
    conductance,
    susceptance,
    duals,
    slacks,
    gen_bus,
    gen_curvature,
):
    buses, scen = volt_mag.shape
    slots = branch_from.shape[0]
    span = -(-slots // LANES) * LANES
    group = 16 if n % 16 == 0 and n > 16 else 4 if n % 4 == 0 else 1
    outer = n // group
    row = lambda a: a.reshape(1, -1)
    rows = 4 * scen + 8
    dma = lambda *shape: pltpu.SemaphoreType.DMA(shape)
    operands = (
        volt_mag.T,
        volt_ang.T,
        gradient.transpose(1, 2, 0),
        branch_from,
        branch_to,
        branch_count,
        row(boundary),
        conductance,
        susceptance,
        duals.transpose(0, 2, 1),
        slacks.transpose(0, 2, 1),
        row(gen_bus),
        row(gen_curvature),
    )
    both = pl.pallas_call(
        functools.partial(kernel, n, group),
        out_shape=pltpu.VMEM((2, 2, scen, buses), F32),
        in_specs=[pl.BlockSpec(memory_space=pltpu.HBM)] * 13,
        out_specs=pl.BlockSpec(memory_space=pltpu.VMEM),
        scratch_shapes=[
            *(pltpu.VMEM(a.shape, a.dtype) for a in operands),
            dma(13),
            pltpu.VMEM((8, span), F32),
            pltpu.VMEM((8, span), F32),
            pltpu.VMEM((4 * scen, 2 * LANES), F32),
            pltpu.VMEM((3, 2 * LANES, 2 * span), BF16),
            pltpu.VMEM((3, 2 * span, 2 * LANES), BF16),
            pltpu.VMEM((3, 4, scen, span), F32),
            pltpu.VMEM((2, rows, LANES), F32),
            pltpu.VMEM((2, 2, rows, LANES), F32),
            pltpu.VMEM((2, rows, LANES), F32),
            pltpu.VMEM((2, 5 * scen, LANES), F32),
            pltpu.VMEM((2, 2, 5 * scen, LANES), F32),
            pltpu.VMEM((2 * scen + 8, span), F32),
            pltpu.VMEM((2, 2 * scen + 8, span), F32),
            pltpu.VMEM((2, 2 * scen, LANES), F32),
            pltpu.VMEM((2, 2, 2 * scen, LANES), F32),
            pltpu.VMEM((2, 2 * scen, LANES), F32),
            pltpu.VMEM((group, 2, LANES), F32),
            pltpu.VMEM((outer, 2, LANES), F32),
            dma(16),
            dma(16),
            dma(group),
            dma(group),
            dma(outer),
            dma(outer),
            pltpu.SemaphoreType.REGULAR((3,)),
        ],
        compiler_params=pltpu.CompilerParams(
            collective_id=0, has_side_effects=True, vmem_limit_bytes=62 * 1024 * 1024
        ),
        name="newton",
    )(*operands)
    return both[0].transpose(2, 0, 1), both[1].transpose(2, 0, 1)


def solution(mesh):
    placed = (
        P("net", "scen"),
        P("net", "scen"),
        P("net", None, "scen"),
        P("net"),
        P("net"),
        P("net"),
        P("net"),
        P("net"),
        P("net"),
        P(None, "net", "scen"),
        P(None, "net", "scen"),
        P("net"),
        P("net"),
    )
    return jax.shard_map(
        functools.partial(body, mesh.shape["net"]),
        mesh=mesh,
        in_specs=placed,
        out_specs=(P("net", None, "scen"), P("net", None, "scen")),
        check_vma=False,
    )
```

```python
import functools

import jax
import jax.numpy as jnp
from jax import lax
from jax.experimental import pallas as pl
from jax.experimental.pallas import tpu as pltpu
from jax.sharding import PartitionSpec as P

MESH = pl.DeviceIdType.MESH
F32, BF16 = jnp.float32, jnp.bfloat16
ITERS = 4
LANES = 128
OWN = 2

barrier_weight = 0.01
volt_low = 0.9
volt_high = 1.1
angle_reg = 0.5


def sine_cosine(angle):
    square = angle * angle
    sine = 1.0 / 6227020800.0
    for term in (-1.0 / 39916800.0, 1.0 / 362880.0, -1.0 / 5040.0, 1.0 / 120.0, -1.0 / 6.0, 1.0):
        sine = sine * square + term
    cosine = -1.0 / 87178291200.0
    for term in (1.0 / 479001600.0, -1.0 / 3628800.0, 1.0 / 40320.0, -1.0 / 720.0, 1.0 / 24.0, -0.5, 1.0):
        cosine = cosine * square + term
    return sine * angle, cosine


def branch_blocks(mag_from, mag_to, sine, cosine, conduct, suscept, weight_p, weight_q):
    along = conduct * cosine + suscept * sine
    across = conduct * sine - suscept * cosine
    cross = mag_from * mag_to
    jp = (2.0 * conduct * mag_from - mag_to * along, cross * across, -mag_from * along, -cross * across)
    jq = (-2.0 * suscept * mag_from - mag_to * across, -cross * along, -mag_from * across, cross * along)
    wp = [weight_p * j for j in jp]
    wq = [weight_q * j for j in jq]

    def entry(i, j):
        return wp[i] * jp[j] + wq[i] * jq[j]

    return (
        (entry(0, 0), entry(0, 1), entry(1, 1)),
        (entry(2, 2), entry(2, 3), entry(3, 3)),
        (entry(0, 2), entry(0, 3), entry(1, 2), entry(1, 3)),
    )


def pieces(values, terms):
    out = []
    for _ in range(terms - 1):
        head = values.astype(BF16)
        out.append(head)
        values = values - head.astype(F32)
    return jnp.concatenate(out + [values.astype(BF16)], axis=0)


def select_dot(values, table, terms):
    rows = values.shape[0]
    out = jnp.dot(pieces(values, terms), table, preferred_element_type=F32)
    total = out[(terms - 1) * rows :]
    for k in range(terms - 2, -1, -1):
        total = total + out[k * rows : (k + 1) * rows]
    return total


def inner(left, right):
    product = left * right
    half = product.shape[0] // 2
    product = product[:half] + product[half:]
    return product[:, :LANES] + product[:, LANES:]


def pack(parts):
    return jnp.sum(jnp.transpose(jnp.concatenate(parts, axis=0)), axis=0, keepdims=True)


def unpack(rows):
    lane = lax.broadcasted_iota(jnp.int32, (1, LANES), 1)
    joined = rows[0]
    for k in range(1, len(rows)):
        joined = jnp.where(lane < 32 * k, joined, pltpu.roll(rows[k], 32 * k, 1))
    columns = jnp.transpose(jnp.broadcast_to(joined, (LANES, LANES)))
    return [columns[32 * k : 32 * k + 32] for k in range(len(rows))]


def galerkin(gram, rhs, n):
    a = {(i, j): gram[(min(i, j), max(i, j))] for i in range(n) for j in range(n)}
    rhs = list(rhs)
    low, inv = {}, {}
    for k in range(n):
        live = a[(k, k)] > 1e-7 * gram[(k, k)]
        inv[k] = jnp.where(live, 1.0 / jnp.where(live, a[(k, k)], 1.0), 0.0)
        for i in range(k + 1, n):
            low[(i, k)] = a[(i, k)] * inv[k]
            for j in range(k + 1, i + 1):
                a[(i, j)] = a[(i, j)] - low[(i, k)] * a[(j, k)]
                a[(j, i)] = a[(i, j)]
            rhs[i] = rhs[i] - low[(i, k)] * rhs[k]
    out = [None] * n
    for k in reversed(range(n)):
        value = rhs[k] * inv[k]
        for i in range(k + 1, n):
            value = value - low[(i, k)] * out[i]
        out[k] = value
    return out


def partners(n):
    return (-1, 1, -2, 2, -16, 16) if n > 32 else (-1, 1, -2, 2)


def kernel(
    n,
    group,
    *refs,
):
    inputs, o_ref, loaded, rest = refs[:13], refs[13], refs[14:27], refs[27:]
    x_ref, r_ref = o_ref.at[0], o_ref.at[1]
    load_sem = rest[0]
    me = lax.axis_index("net")
    neighbours = [lax.rem(me + n + d, n) for d in partners(n)]
    for peer in neighbours:
        pl.semaphore_signal(pltpu.get_barrier_semaphore(), inc=1, device_id={"net": peer}, device_id_type=MESH)
    loads = []
    for k, (source, target) in enumerate(zip(inputs, loaded)):
        copy = pltpu.make_async_copy(source, target, load_sem.at[k])
        copy.start()
        loads.append(copy)
    solve(n, group, loads, *loaded, x_ref, r_ref, *rest[1:])


def solve(
    n,
    group,
    loads,
    vm_ref,
    va_ref,
    grad_ref,
    from_ref,
    to_ref,
    count_ref,
    bound_ref,
    g_ref,
    b_ref,
    dual_ref,
    slack_ref,
    gbus_ref,
    gcur_ref,
    x_ref,
    r_ref,
    irow,
    frow,
    vin,
    gather_tab,
    scatter_tab,
    blocks,
    a_out,
    a_in,
    f_in,
    b_out,
    b_in,
    w_out,
    w_in,
    x_out,
    x_in,
    y_in,
    red_a,
    red_b,
    send_sem,
    recv_sem,
    a_send,
    a_recv,
    b_send,
    b_recv,
    known_sem,
):
    scen, buses = vm_ref.shape
    slots = from_ref.shape[-1]
    ghost = buses // 2
    wide = 2 * LANES
    span = gather_tab.shape[2] // 2
    gens = gbus_ref.shape[1]
    outer = n // group
    me = lax.axis_index("net")
    prev, nxt, prev2, nxt2 = [lax.rem(me + n + d, n) for d in (-1, 1, -2, 2)]
    member = lax.rem(me, group)
    block = lax.div(me, group)
    peers_a = [block * group + lax.rem(member + d, group) for d in range(1, group)]
    peers_b = [lax.rem(block + d, outer) * group + member for d in range(1, outer)]

    barrier = pltpu.get_barrier_semaphore()
    spans = [[d for d in step if d < n // 2] for step in ((2, 16), (4, 32), (8,))]

    def tell(step):
        for d in spans[step]:
            for at in (n - d, d):
                pl.semaphore_signal(
                    known_sem.at[step], inc=1, device_id={"net": lax.rem(me + at, n)}, device_id_type=MESH
                )

    def told(step):
        if spans[step]:
            pl.semaphore_wait(known_sem.at[step], 2 * len(spans[step]))

    core = lax.rem(me, 2)
    mate = me + 1 - 2 * core
    beyond_mate = lax.rem(me + n + 2 - 4 * core, n)
    pending = []

    def send(message, source, target, peer):
        copy = pltpu.make_async_remote_copy(
            src_ref=source,
            dst_ref=target,
            send_sem=send_sem.at[message],
            recv_sem=recv_sem.at[message],
            device_id={"net": peer},
            device_id_type=MESH,
        )
        copy.start()
        pending.append(copy)
        return copy

    for copy in loads:
        copy.wait()

    irow[...] = jnp.full(irow.shape, -1.0, F32)
    irow[0:1, :slots] = from_ref[...].reshape(1, slots).astype(F32)
    irow[1:2, :slots] = to_ref[...].reshape(1, slots).astype(F32)
    irow[2:3, :buses] = bound_ref[...].astype(F32)
    irow[3:4, :gens] = gbus_ref[...].astype(F32)
    frow[...] = jnp.zeros(frow.shape, F32)
    frow[0:1, :slots] = g_ref[...].reshape(1, slots)
    frow[1:2, :slots] = b_ref[...].reshape(1, slots)
    frow[2:3, :gens] = gcur_ref[...]
    from_row, to_row = irow[0:1, :], irow[1:2, :]
    lane_i = lax.broadcasted_iota(jnp.int32, (8, wide), 1)
    lane = lane_i.astype(F32)
    plain = irow[0:8, :wide]
    rolled = pltpu.roll(plain, LANES - ghost, 1)
    upper = (lane_i >= LANES) & (lane_i < LANES + ghost)
    place = jnp.where(lane_i < ghost, plain, jnp.where(upper, rolled, -2.0))[2:3]
    entry = jnp.where(lane_i < ghost, lane, jnp.where(upper, lane - (LANES - ghost), -1e6))[0:1]

    def column(row):
        return jnp.transpose(jnp.broadcast_to(row, (LANES, row.shape[1])))

    def hot(mask):
        return jnp.where(mask, 1.0, 0.0).astype(BF16)

    lanes_of = lambda row, t: row[:, t * LANES : (t + 1) * LANES]

    def index_tables(k, place, from_row, to_row):
        place_col, from_col, to_col = column(place), column(from_row), column(to_row)
        for t in range(span // LANES):
            gather_tab[k, :, t * LANES : (t + 1) * LANES] = hot(place_col == lanes_of(from_row, t))
            gather_tab[k, :, span + t * LANES : span + (t + 1) * LANES] = hot(place_col == lanes_of(to_row, t))
        for t in range(2):
            cols = slice(t * LANES, (t + 1) * LANES)
            scatter_tab[k, 0:span, cols] = hot(from_col == lanes_of(place, t))
            scatter_tab[k, span:, cols] = hot(to_col == lanes_of(place, t))
        return place_col, to_col

    place_col, to_col = index_tables(OWN, place, from_row, to_row)
    irow[4:5, :wide] = place
    cross_tab = jnp.concatenate([hot(to_col == lanes_of(entry, t) + buses) for t in range(2)], axis=1)
    bus_row = lane[0:1]
    bus_col = lax.broadcasted_iota(jnp.int32, (wide, LANES), 0).astype(F32)
    to_place = jnp.concatenate([hot(bus_col == lanes_of(place, t)) for t in range(2)], axis=1)
    to_bus = jnp.concatenate([hot(place_col == lanes_of(bus_row, t)) for t in range(2)], axis=1)

    vin[...] = jnp.zeros(vin.shape, F32)
    vin[0:scen, :buses] = vm_ref[...]
    vin[scen : 2 * scen, :buses] = va_ref[...]
    vin[2 * scen : 3 * scen, :buses] = grad_ref[0]
    vin[3 * scen : 4 * scen, :buses] = grad_ref[1]
    placed = select_dot(vin[...], to_place, 3)
    vm, va, start = placed[0:scen], placed[scen : 2 * scen], placed[2 * scen :]

    slot = lax.broadcasted_iota(jnp.int32, (1, slots), 1)
    live = jnp.where(slot < count_ref[...].reshape(1, 1), 1.0, 0.0)
    pad = jnp.zeros((scen, span - slots), F32)
    weight_p = jnp.concatenate([live * dual_ref[0] / slack_ref[0], pad], axis=1)
    weight_q = jnp.concatenate([live * dual_ref[1] / slack_ref[1], pad], axis=1)
    conduct, suscept = frow[0:1, :], frow[1:2, :]
    stacked = jnp.concatenate([weight_p, weight_q, frow[0:8, :]], axis=0)
    crossing = select_dot(stacked, cross_tab, 3)
    payload = jnp.concatenate([vm, va, crossing], axis=0)
    split = lambda v: (v[:, :LANES], v[:, LANES:])
    join = lambda a, b: jnp.concatenate([a, b], axis=1)
    for half, part in enumerate(split(payload)):
        a_out[half] = part

    pl.semaphore_wait(barrier, len(partners(n)))
    a_near = [send(0, a_out.at[0], a_in.at[1, 0], prev), send(1, a_out.at[1], a_in.at[0, 1], nxt)]

    def local_blocks(k, volts, weight_p, weight_q, conduct, suscept):
        ends = select_dot(volts, gather_tab[k], 3)
        sine, cosine = sine_cosine(ends[scen:, :span] - ends[scen:, span:])
        hff, htt, hft = branch_blocks(
            ends[:scen, :span], ends[:scen, span:], sine, cosine, conduct, suscept, weight_p, weight_q
        )
        for e in range(4):
            blocks[k, e] = hft[e]
        return hff, htt

    local = jnp.where((to_row >= 0.0) & (to_row < float(buses)), 1.0, 0.0)
    weight_p, weight_q = weight_p * local, weight_q * local
    hff, htt = local_blocks(OWN, placed[0 : 2 * scen], weight_p, weight_q, conduct, suscept)
    both = jnp.concatenate([join(a, b) for a, b in zip(hff, htt)], axis=0)
    diag = select_dot(both, scatter_tab[OWN], 3)
    gen = column(irow[3:4, :LANES])
    curve = column(frow[2:3, :LANES])
    gen_sum = join(
        *(jnp.sum(jnp.where(gen == lanes_of(place, t), curve, 0.0), axis=0, keepdims=True) for t in range(2))
    )
    low, high = vm - volt_low, volt_high - vm
    base_vv = barrier_weight / (low * low) + barrier_weight / (high * high) + gen_sum
    base_aa = angle_reg + gen_sum
    own = jnp.concatenate(
        [diag[0:scen] + base_vv, diag[scen : 2 * scen], diag[2 * scen :] + base_aa, start], axis=0
    )
    for half, part in enumerate(split(own)):
        b_out[half] = part
    b_near = [send(2, b_out.at[0], b_in.at[1, 0], prev), send(3, b_out.at[1], b_in.at[0, 1], nxt)]

    tell(0)

    w_out[0:scen] = weight_p
    w_out[scen : 2 * scen] = weight_q
    irow[5:7] = frow[0:2]
    w_out[2 * scen :] = irow[...]
    rows = pl.ds(0, 3 * scen)
    far = [
        send(4, w_out, w_in.at[1], prev),
        send(5, w_out, w_in.at[0], nxt),
        send(6, a_out.at[1], a_in.at[1, 1], prev),
        send(7, a_out.at[0], a_in.at[0, 0], nxt),
        send(8, a_out.at[1 - core], f_in.at[core], beyond_mate),
        send(10, b_out.at[1, rows], b_in.at[1, 1, rows], prev),
        send(11, b_out.at[0, rows], b_in.at[0, 0, rows], nxt),
    ]

    def coupling(here, there):
        vm, va, p, q = (here[k * scen : (k + 1) * scen] for k in range(4))
        there_vm, there_va, there_p, there_q = (there[k * scen : (k + 1) * scen] for k in range(4))
        g, b = here[4 * scen : 4 * scen + 1], here[4 * scen + 1 : 4 * scen + 2]
        there_g, there_b = there[4 * scen : 4 * scen + 1], there[4 * scen + 1 : 4 * scen + 2]
        sine, cosine = sine_cosine(va - there_va)
        off, reach, (o00, o01, o10, o11) = branch_blocks(vm, there_vm, sine, cosine, g, b, p, q)
        root, on, (i00, i01, i10, i11) = branch_blocks(there_vm, vm, -sine, cosine, there_g, there_b, there_p, there_q)
        return (off, on), (reach, root), (o00 + i00, o01 + i10, o10 + i01, o11 + i11)

    def inverse_of(fields, parts):
        first, second = parts
        d00, d01, d11 = (fields[k * scen : (k + 1) * scen] + first[k] + second[k] for k in range(3))
        inverse = 1.0 / (d00 * d11 - d01 * d01)
        return d11 * inverse, -d01 * inverse, d00 * inverse

    def applied(fields, v):
        b00, b01, b11 = fields
        return jnp.concatenate([b00 * v[:scen] + b01 * v[scen:], b01 * v[:scen] + b11 * v[scen:]], axis=0)

    def coupled(c, v):
        v0, v1 = v[:scen], v[scen:]
        return jnp.concatenate([c[0] * v0 + c[1] * v1, c[2] * v0 + c[3] * v1], axis=0)

    for copy in a_near:
        copy.wait_recv()
    told(0)
    tell(1)
    far.append(send(9, a_in.at[core, 1 - core], f_in.at[core], mate))
    here_parts, there_parts, border = coupling(payload, join(a_in[0, 1], a_in[1, 0]))
    border_back = (border[0], border[2], border[1], border[3])
    diag_inverse = inverse_of(own, here_parts)

    for copy in b_near:
        copy.wait_recv()
    beyond = join(b_in[0, 1], b_in[1, 0])
    facing_inverse = inverse_of(beyond, there_parts)
    facing = applied(facing_inverse, beyond[3 * scen :])

    def inside_product(k, v, cols=slice(0, wide)):
        ends = select_dot(v, gather_tab[k], 2)
        f0, f1, t0, t1 = ends[:scen, :span], ends[scen:, :span], ends[:scen, span:], ends[scen:, span:]
        h00, h01, h10, h11 = (blocks[k, e] for e in range(4))
        terms = jnp.concatenate(
            [
                join(h00 * t0 + h01 * t1, h00 * f0 + h10 * f1),
                join(h10 * t0 + h11 * t1, h01 * f0 + h11 * f1),
            ],
            axis=0,
        )
        return select_dot(terms, scatter_tab[k, :, cols], 2)

    s, u = [start], [applied(diag_inverse, start)]
    s.append(inside_product(OWN, u[0]) + coupled(border, facing))
    u.append(applied(diag_inverse, s[1]))
    for half, part in enumerate(split(u[1])):
        x_out[half] = part
    vectors = [
        send(12, x_out, x_in.at[1], prev),
        send(13, x_out, x_in.at[0], nxt),
        send(14, x_out.at[0], y_in.at[1], prev2),
        send(15, x_out.at[1], y_in.at[0], nxt2),
    ]

    told(1)
    tell(2)

    sums = [inner(u[k // 2], s[k - k // 2]) for k in range(3)]

    for copy in far:
        copy.wait_recv()
    inside = inside_product(OWN, u[1])
    outer_border, side_inverse = [], []
    for k in range(2):
        index = w_in[k, 2 * scen :]
        index_tables(k, index[4:5, :wide], index[0:1], index[1:2])
        volts = join(a_in[k, 0, : 2 * scen], a_in[k, 1, : 2 * scen])
        local_blocks(k, volts, w_in[k, :scen], w_in[k, scen : 2 * scen], index[5:6], index[6:7])
        parts, _, fields = coupling(a_in[k, k], f_in[k])
        outer_border.append(fields)
        outside = inverse_of(b_in[k, k, : 3 * scen], parts)
        near = [split(f)[k] for f in facing_inverse]
        side_inverse.append([join(f, g) if k else join(g, f) for f, g in zip(near, outside)])

    for copy in vectors:
        copy.wait_recv()
    side = [join(x_in[k, 0], x_in[k, 1]) for k in range(2)]
    for j in (2, 3):
        facing = join(split(side[0])[1], split(side[1])[0])
        s.append(inside + coupled(border, facing))
        back = split(coupled(border_back, u[-1]))
        for k in range(2):
            if j == 2:
                outside = coupled(outer_border[k], y_in[k])
                product = inside_product(k, side[k]) + (join(back[k], outside) if k else join(outside, back[k]))
                side[k] = applied(side_inverse[k], product)
            else:
                cols = slice(0, LANES) if k else slice(LANES, wide)
                product = inside_product(k, side[k], cols) + back[k]
                side[k] = applied([f[:, cols] for f in side_inverse[k]], product)
        u.append(applied(diag_inverse, s[-1]))
        inside = inside_product(OWN, u[-1])
    s.append(inside + coupled(border, join(*side)))

    def all_sum(tile, meanwhile):
        red_a[pl.ds(member, 1)] = tile[None]
        copies = []
        for d, peer in enumerate(peers_a):
            copy = pltpu.make_async_remote_copy(
                src_ref=red_a.at[member],
                dst_ref=red_a.at[member],
                send_sem=a_send.at[d],
                recv_sem=a_recv.at[d],
                device_id={"net": peer},
                device_id_type=MESH,
            )
            copy.start()
            copies.append(copy)
        ahead = meanwhile()
        for copy in copies:
            copy.wait_recv()
        pending.extend(copies)
        total = red_a[0]
        for k in range(1, group):
            total = total + red_a[k]
        red_b[pl.ds(block, 1)] = total[None]
        copies = []
        for d, peer in enumerate(peers_b):
            copy = pltpu.make_async_remote_copy(
                src_ref=red_b.at[block],
                dst_ref=red_b.at[block],
                send_sem=b_send.at[d],
                recv_sem=b_recv.at[d],
                device_id={"net": peer},
                device_id_type=MESH,
            )
            copy.start()
            copies.append(copy)
        for copy in copies:
            copy.wait_recv()
        pending.extend(copies)
        total = red_b[0]
        for k in range(1, outer):
            total = total + red_b[k]
        return total, ahead

    told(2)
    sums += [inner(u[k // 2], s[k - k // 2]) for k in range(3, 2 * ITERS)]
    def bus_order():
        return [select_dot(v, to_bus, 3) for v in u], [select_dot(v, to_bus, 3) for v in s]

    total, (u, s) = all_sum(jnp.concatenate([pack(sums[:4]), pack(sums[4:])], axis=0), bus_order)
    moments = [total[k // 4 : k // 4 + 1] for k in range(2 * ITERS)]
    moments = [pltpu.roll(m, LANES - 32 * (k % 4), 1) if k % 4 else m for k, m in enumerate(moments)]
    gram = {(i, j): moments[i + j] + moments[i + j + 1] for i in range(ITERS) for j in range(i, ITERS)}
    w = unpack(galerkin(gram, moments[ITERS:], ITERS))
    w = [jnp.concatenate([jnp.concatenate([c, c], axis=1)] * 2, axis=0) for c in w]
    step = (1.0 + w[0]) * u[0] + (w[1] - 1.0) * u[1] + (1.0 + w[2]) * u[2] + (w[3] - 1.0) * u[3]
    residual = (1.0 - w[3]) * s[4] - (w[2] + w[3]) * s[3] - (w[1] + w[2]) * s[2] - (w[0] + w[1]) * s[1] - w[0] * s[0]
    for c in range(2):
        x_ref[c] = step[c * scen : (c + 1) * scen, :buses]
        r_ref[c] = residual[c * scen : (c + 1) * scen, :buses]

    for copy in pending:
        copy.wait_send()


def body(
    n,
    volt_mag,
    volt_ang,
    gradient,
    branch_from,
    branch_to,
    branch_count,
    boundary,
    conductance,
    susceptance,
    duals,
    slacks,
    gen_bus,
    gen_curvature,
):
    buses, scen = volt_mag.shape
    slots = branch_from.shape[0]
    span = -(-slots // LANES) * LANES
    group = 16 if n % 16 == 0 and n > 16 else 4 if n % 4 == 0 else 1
    outer = n // group
    row = lambda a: a.reshape(1, -1)
    rows = 4 * scen + 8
    dma = lambda *shape: pltpu.SemaphoreType.DMA(shape)
    operands = (
        volt_mag.T,
        volt_ang.T,
        gradient.transpose(1, 2, 0),
        branch_from,
        branch_to,
        branch_count,
        row(boundary),
        conductance,
        susceptance,
        duals.transpose(0, 2, 1),
        slacks.transpose(0, 2, 1),
        row(gen_bus),
        row(gen_curvature),
    )
    both = pl.pallas_call(
        functools.partial(kernel, n, group),
        out_shape=pltpu.VMEM((2, 2, scen, buses), F32),
        in_specs=[pl.BlockSpec(memory_space=pltpu.HBM)] * 13,
        out_specs=pl.BlockSpec(memory_space=pltpu.VMEM),
        scratch_shapes=[
            *(pltpu.VMEM(a.shape, a.dtype) for a in operands),
            dma(13),
            pltpu.VMEM((8, span), F32),
            pltpu.VMEM((8, span), F32),
            pltpu.VMEM((4 * scen, 2 * LANES), F32),
            pltpu.VMEM((3, 2 * LANES, 2 * span), BF16),
            pltpu.VMEM((3, 2 * span, 2 * LANES), BF16),
            pltpu.VMEM((3, 4, scen, span), F32),
            pltpu.VMEM((2, rows, LANES), F32),
            pltpu.VMEM((2, 2, rows, LANES), F32),
            pltpu.VMEM((2, rows, LANES), F32),
            pltpu.VMEM((2, 5 * scen, LANES), F32),
            pltpu.VMEM((2, 2, 5 * scen, LANES), F32),
            pltpu.VMEM((2 * scen + 8, span), F32),
            pltpu.VMEM((2, 2 * scen + 8, span), F32),
            pltpu.VMEM((2, 2 * scen, LANES), F32),
            pltpu.VMEM((2, 2, 2 * scen, LANES), F32),
            pltpu.VMEM((2, 2 * scen, LANES), F32),
            pltpu.VMEM((group, 2, LANES), F32),
            pltpu.VMEM((outer, 2, LANES), F32),
            dma(16),
            dma(16),
            dma(group),
            dma(group),
            dma(outer),
            dma(outer),
            pltpu.SemaphoreType.REGULAR((3,)),
        ],
        compiler_params=pltpu.CompilerParams(
            collective_id=0, has_side_effects=True, vmem_limit_bytes=62 * 1024 * 1024
        ),
        name="newton",
    )(*operands)
    return both[0].transpose(2, 0, 1), both[1].transpose(2, 0, 1)


def solution(mesh):
    placed = (
        P("net", "scen"),
        P("net", "scen"),
        P("net", None, "scen"),
        P("net"),
        P("net"),
        P("net"),
        P("net"),
        P("net"),
        P("net"),
        P(None, "net", "scen"),
        P(None, "net", "scen"),
        P("net"),
        P("net"),
    )
    return jax.shard_map(
        functools.partial(body, mesh.shape["net"]),
        mesh=mesh,
        in_specs=placed,
        out_specs=(P("net", None, "scen"), P("net", None, "scen")),
        check_vma=False,
    )
```

```python
import functools

import jax
import jax.numpy as jnp
from jax import lax
from jax.experimental import pallas as pl
from jax.experimental.pallas import tpu as pltpu
from jax.sharding import PartitionSpec as P

MESH = pl.DeviceIdType.MESH
F32, BF16 = jnp.float32, jnp.bfloat16
ITERS = 4
LANES = 128
OWN = 2

barrier_weight = 0.01
volt_low = 0.9
volt_high = 1.1
angle_reg = 0.5


def sine_cosine(angle):
    square = angle * angle
    sine = 1.0 / 6227020800.0
    for term in (-1.0 / 39916800.0, 1.0 / 362880.0, -1.0 / 5040.0, 1.0 / 120.0, -1.0 / 6.0, 1.0):
        sine = sine * square + term
    cosine = -1.0 / 87178291200.0
    for term in (1.0 / 479001600.0, -1.0 / 3628800.0, 1.0 / 40320.0, -1.0 / 720.0, 1.0 / 24.0, -0.5, 1.0):
        cosine = cosine * square + term
    return sine * angle, cosine


def branch_blocks(mag_from, mag_to, sine, cosine, conduct, suscept, weight_p, weight_q):
    along = conduct * cosine + suscept * sine
    across = conduct * sine - suscept * cosine
    cross = mag_from * mag_to
    jp = (2.0 * conduct * mag_from - mag_to * along, cross * across, -mag_from * along, -cross * across)
    jq = (-2.0 * suscept * mag_from - mag_to * across, -cross * along, -mag_from * across, cross * along)
    wp = [weight_p * j for j in jp]
    wq = [weight_q * j for j in jq]

    def entry(i, j):
        return wp[i] * jp[j] + wq[i] * jq[j]

    return (
        (entry(0, 0), entry(0, 1), entry(1, 1)),
        (entry(2, 2), entry(2, 3), entry(3, 3)),
        (entry(0, 2), entry(0, 3), entry(1, 2), entry(1, 3)),
    )


def pieces(values, terms):
    out = []
    for _ in range(terms - 1):
        head = values.astype(BF16)
        out.append(head)
        values = values - head.astype(F32)
    return jnp.concatenate(out + [values.astype(BF16)], axis=0)


def select_dot(values, table, terms):
    rows = values.shape[0]
    out = jnp.dot(pieces(values, terms), table, preferred_element_type=F32)
    total = out[(terms - 1) * rows :]
    for k in range(terms - 2, -1, -1):
        total = total + out[k * rows : (k + 1) * rows]
    return total


def inner(left, right):
    product = left * right
    half = product.shape[0] // 2
    product = product[:half] + product[half:]
    return product[:, :LANES] + product[:, LANES:]


def pack(parts):
    return jnp.sum(jnp.transpose(jnp.concatenate(parts, axis=0)), axis=0, keepdims=True)


def unpack(rows):
    lane = lax.broadcasted_iota(jnp.int32, (1, LANES), 1)
    joined = rows[0]
    for k in range(1, len(rows)):
        joined = jnp.where(lane < 32 * k, joined, pltpu.roll(rows[k], 32 * k, 1))
    columns = jnp.transpose(jnp.broadcast_to(joined, (LANES, LANES)))
    return [columns[32 * k : 32 * k + 32] for k in range(len(rows))]


def galerkin(gram, rhs, n):
    a = {(i, j): gram[(min(i, j), max(i, j))] for i in range(n) for j in range(n)}
    rhs = list(rhs)
    low, inv = {}, {}
    for k in range(n):
        live = a[(k, k)] > 1e-7 * gram[(k, k)]
        inv[k] = jnp.where(live, 1.0 / jnp.where(live, a[(k, k)], 1.0), 0.0)
        for i in range(k + 1, n):
            low[(i, k)] = a[(i, k)] * inv[k]
            for j in range(k + 1, i + 1):
                a[(i, j)] = a[(i, j)] - low[(i, k)] * a[(j, k)]
                a[(j, i)] = a[(i, j)]
            rhs[i] = rhs[i] - low[(i, k)] * rhs[k]
    out = [None] * n
    for k in reversed(range(n)):
        value = rhs[k] * inv[k]
        for i in range(k + 1, n):
            value = value - low[(i, k)] * out[i]
        out[k] = value
    return out


def partners(n):
    return (-1, 1, -2, 2, -16, 16) if n > 32 else (-1, 1, -2, 2)


def kernel(
    n,
    group,
    *refs,
):
    inputs, o_ref, loaded, rest = refs[:13], refs[13], refs[14:27], refs[27:]
    x_ref, r_ref = o_ref.at[0], o_ref.at[1]
    load_sem = rest[0]
    me = lax.axis_index("net")
    neighbours = [lax.rem(me + n + d, n) for d in partners(n)]
    for peer in neighbours:
        pl.semaphore_signal(pltpu.get_barrier_semaphore(), inc=1, device_id={"net": peer}, device_id_type=MESH)
    loads = []
    for k, (source, target) in enumerate(zip(inputs, loaded)):
        copy = pltpu.make_async_copy(source, target, load_sem.at[k])
        copy.start()
        loads.append(copy)
    solve(n, group, loads, *loaded, x_ref, r_ref, *rest[1:])


def solve(
    n,
    group,
    loads,
    vm_ref,
    va_ref,
    grad_ref,
    from_ref,
    to_ref,
    count_ref,
    bound_ref,
    g_ref,
    b_ref,
    dual_ref,
    slack_ref,
    gbus_ref,
    gcur_ref,
    x_ref,
    r_ref,
    irow,
    frow,
    vin,
    gather_tab,
    scatter_tab,
    blocks,
    a_out,
    a_in,
    f_in,
    b_out,
    b_in,
    w_out,
    w_in,
    x_out,
    x_in,
    y_in,
    red_a,
    red_b,
    send_sem,
    recv_sem,
    a_send,
    a_recv,
    b_send,
    b_recv,
    known_sem,
):
    scen, buses = vm_ref.shape
    slots = from_ref.shape[-1]
    ghost = buses // 2
    wide = 2 * LANES
    span = gather_tab.shape[2] // 2
    gens = gbus_ref.shape[1]
    outer = n // group
    me = lax.axis_index("net")
    prev, nxt, prev2, nxt2 = [lax.rem(me + n + d, n) for d in (-1, 1, -2, 2)]
    member = lax.rem(me, group)
    block = lax.div(me, group)
    peers_a = [block * group + lax.rem(member + d, group) for d in range(1, group)]
    peers_b = [lax.rem(block + d, outer) * group + member for d in range(1, outer)]

    barrier = pltpu.get_barrier_semaphore()
    spans = [[d for d in step if d < n // 2] for step in ((2, 16), (4, 32), (8,))]

    def tell(step):
        for d in spans[step]:
            for at in (n - d, d):
                pl.semaphore_signal(
                    known_sem.at[step], inc=1, device_id={"net": lax.rem(me + at, n)}, device_id_type=MESH
                )

    def told(step):
        if spans[step]:
            pl.semaphore_wait(known_sem.at[step], 2 * len(spans[step]))

    core = lax.rem(me, 2)
    mate = me + 1 - 2 * core
    across = lax.rem(me + n - 1 + 2 * core, n)
    beyond_mate = lax.rem(me + n + 2 - 4 * core, n)
    pending = []

    def send(message, source, target, peer):
        copy = pltpu.make_async_remote_copy(
            src_ref=source,
            dst_ref=target,
            send_sem=send_sem.at[message],
            recv_sem=recv_sem.at[message],
            device_id={"net": peer},
            device_id_type=MESH,
        )
        copy.start()
        pending.append(copy)
        return copy

    for copy in loads:
        copy.wait()

    irow[...] = jnp.full(irow.shape, -1.0, F32)
    irow[0:1, :slots] = from_ref[...].reshape(1, slots).astype(F32)
    irow[1:2, :slots] = to_ref[...].reshape(1, slots).astype(F32)
    irow[2:3, :buses] = bound_ref[...].astype(F32)
    irow[3:4, :gens] = gbus_ref[...].astype(F32)
    frow[...] = jnp.zeros(frow.shape, F32)
    frow[0:1, :slots] = g_ref[...].reshape(1, slots)
    frow[1:2, :slots] = b_ref[...].reshape(1, slots)
    frow[2:3, :gens] = gcur_ref[...]
    from_row, to_row = irow[0:1, :], irow[1:2, :]
    lane_i = lax.broadcasted_iota(jnp.int32, (8, wide), 1)
    lane = lane_i.astype(F32)
    plain = irow[0:8, :wide]
    rolled = pltpu.roll(plain, LANES - ghost, 1)
    upper = (lane_i >= LANES) & (lane_i < LANES + ghost)
    place = jnp.where(lane_i < ghost, plain, jnp.where(upper, rolled, -2.0))[2:3]
    entry = jnp.where(lane_i < ghost, lane, jnp.where(upper, lane - (LANES - ghost), -1e6))[0:1]

    def column(row):
        return jnp.transpose(jnp.broadcast_to(row, (LANES, row.shape[1])))

    def hot(mask):
        return jnp.where(mask, 1.0, 0.0).astype(BF16)

    lanes_of = lambda row, t: row[:, t * LANES : (t + 1) * LANES]

    def index_tables(k, place, from_row, to_row):
        place_col, from_col, to_col = column(place), column(from_row), column(to_row)
        for t in range(span // LANES):
            gather_tab[k, :, t * LANES : (t + 1) * LANES] = hot(place_col == lanes_of(from_row, t))
            gather_tab[k, :, span + t * LANES : span + (t + 1) * LANES] = hot(place_col == lanes_of(to_row, t))
        for t in range(2):
            cols = slice(t * LANES, (t + 1) * LANES)
            scatter_tab[k, 0:span, cols] = hot(from_col == lanes_of(place, t))
            scatter_tab[k, span:, cols] = hot(to_col == lanes_of(place, t))
        return place_col, to_col

    place_col, to_col = index_tables(OWN, place, from_row, to_row)
    irow[4:5, :wide] = place
    cross_tab = jnp.concatenate([hot(to_col == lanes_of(entry, t) + buses) for t in range(2)], axis=1)
    bus_row = lane[0:1]
    bus_col = lax.broadcasted_iota(jnp.int32, (wide, LANES), 0).astype(F32)
    to_place = jnp.concatenate([hot(bus_col == lanes_of(place, t)) for t in range(2)], axis=1)
    to_bus = jnp.concatenate([hot(place_col == lanes_of(bus_row, t)) for t in range(2)], axis=1)

    vin[...] = jnp.zeros(vin.shape, F32)
    vin[0:scen, :buses] = vm_ref[...]
    vin[scen : 2 * scen, :buses] = va_ref[...]
    vin[2 * scen : 3 * scen, :buses] = grad_ref[0]
    vin[3 * scen : 4 * scen, :buses] = grad_ref[1]
    placed = select_dot(vin[...], to_place, 3)
    vm, va, start = placed[0:scen], placed[scen : 2 * scen], placed[2 * scen :]

    slot = lax.broadcasted_iota(jnp.int32, (1, slots), 1)
    live = jnp.where(slot < count_ref[...].reshape(1, 1), 1.0, 0.0)
    pad = jnp.zeros((scen, span - slots), F32)
    weight_p = jnp.concatenate([live * dual_ref[0] / slack_ref[0], pad], axis=1)
    weight_q = jnp.concatenate([live * dual_ref[1] / slack_ref[1], pad], axis=1)
    conduct, suscept = frow[0:1, :], frow[1:2, :]
    stacked = jnp.concatenate([weight_p, weight_q, frow[0:8, :]], axis=0)
    crossing = select_dot(stacked, cross_tab, 3)
    payload = jnp.concatenate([vm, va, crossing], axis=0)
    split = lambda v: (v[:, :LANES], v[:, LANES:])
    join = lambda a, b: jnp.concatenate([a, b], axis=1)
    for half, part in enumerate(split(payload)):
        a_out[half] = part

    pl.semaphore_wait(barrier, len(partners(n)))
    a_near = [
        send(0, a_out.at[core], a_in.at[1 - core, core], across),
        send(1, a_out.at[1 - core], a_in.at[core, 1 - core], mate),
    ]

    def local_blocks(k, volts, weight_p, weight_q, conduct, suscept):
        ends = select_dot(volts, gather_tab[k], 3)
        sine, cosine = sine_cosine(ends[scen:, :span] - ends[scen:, span:])
        hff, htt, hft = branch_blocks(
            ends[:scen, :span], ends[:scen, span:], sine, cosine, conduct, suscept, weight_p, weight_q
        )
        for e in range(4):
            blocks[k, e] = hft[e]
        return hff, htt

    local = jnp.where((to_row >= 0.0) & (to_row < float(buses)), 1.0, 0.0)
    weight_p, weight_q = weight_p * local, weight_q * local
    hff, htt = local_blocks(OWN, placed[0 : 2 * scen], weight_p, weight_q, conduct, suscept)
    both = jnp.concatenate([join(a, b) for a, b in zip(hff, htt)], axis=0)
    diag = select_dot(both, scatter_tab[OWN], 3)
    gen = column(irow[3:4, :LANES])
    curve = column(frow[2:3, :LANES])
    gen_sum = join(
        *(jnp.sum(jnp.where(gen == lanes_of(place, t), curve, 0.0), axis=0, keepdims=True) for t in range(2))
    )
    low, high = vm - volt_low, volt_high - vm
    base_vv = barrier_weight / (low * low) + barrier_weight / (high * high) + gen_sum
    base_aa = angle_reg + gen_sum
    own = jnp.concatenate(
        [diag[0:scen] + base_vv, diag[scen : 2 * scen], diag[2 * scen :] + base_aa, start], axis=0
    )
    for half, part in enumerate(split(own)):
        b_out[half] = part
    b_near = [
        send(2, b_out.at[core], b_in.at[1 - core, core], across),
        send(3, b_out.at[1 - core], b_in.at[core, 1 - core], mate),
    ]

    tell(0)

    w_out[0:scen] = weight_p
    w_out[scen : 2 * scen] = weight_q
    irow[5:7] = frow[0:2]
    w_out[2 * scen :] = irow[...]
    rows = pl.ds(0, 3 * scen)
    far = [
        send(4, w_out, w_in.at[1], prev),
        send(5, w_out, w_in.at[0], nxt),
        send(6, a_out.at[1], a_in.at[1, 1], prev),
        send(7, a_out.at[0], a_in.at[0, 0], nxt),
        send(8, a_out.at[1 - core], f_in.at[core], beyond_mate),
        send(10, b_out.at[1, rows], b_in.at[1, 1, rows], prev),
        send(11, b_out.at[0, rows], b_in.at[0, 0, rows], nxt),
    ]

    def coupling(here, there):
        vm, va, p, q = (here[k * scen : (k + 1) * scen] for k in range(4))
        there_vm, there_va, there_p, there_q = (there[k * scen : (k + 1) * scen] for k in range(4))
        g, b = here[4 * scen : 4 * scen + 1], here[4 * scen + 1 : 4 * scen + 2]
        there_g, there_b = there[4 * scen : 4 * scen + 1], there[4 * scen + 1 : 4 * scen + 2]
        sine, cosine = sine_cosine(va - there_va)
        off, reach, (o00, o01, o10, o11) = branch_blocks(vm, there_vm, sine, cosine, g, b, p, q)
        root, on, (i00, i01, i10, i11) = branch_blocks(there_vm, vm, -sine, cosine, there_g, there_b, there_p, there_q)
        return (off, on), (reach, root), (o00 + i00, o01 + i10, o10 + i01, o11 + i11)

    def inverse_of(fields, parts):
        first, second = parts
        d00, d01, d11 = (fields[k * scen : (k + 1) * scen] + first[k] + second[k] for k in range(3))
        inverse = 1.0 / (d00 * d11 - d01 * d01)
        return d11 * inverse, -d01 * inverse, d00 * inverse

    def applied(fields, v):
        b00, b01, b11 = fields
        return jnp.concatenate([b00 * v[:scen] + b01 * v[scen:], b01 * v[:scen] + b11 * v[scen:]], axis=0)

    def coupled(c, v):
        v0, v1 = v[:scen], v[scen:]
        return jnp.concatenate([c[0] * v0 + c[1] * v1, c[2] * v0 + c[3] * v1], axis=0)

    told(0)
    tell(1)
    for copy in a_near:
        copy.wait_recv()
    far.append(send(9, a_in.at[core, 1 - core], f_in.at[core], mate))
    here_parts, there_parts, border = coupling(payload, join(a_in[0, 1], a_in[1, 0]))
    border_back = (border[0], border[2], border[1], border[3])
    diag_inverse = inverse_of(own, here_parts)

    for copy in b_near:
        copy.wait_recv()
    beyond = join(b_in[0, 1], b_in[1, 0])
    facing_inverse = inverse_of(beyond, there_parts)
    facing = applied(facing_inverse, beyond[3 * scen :])

    def inside_product(k, v, cols=slice(0, wide)):
        ends = select_dot(v, gather_tab[k], 2)
        f0, f1, t0, t1 = ends[:scen, :span], ends[scen:, :span], ends[:scen, span:], ends[scen:, span:]
        h00, h01, h10, h11 = (blocks[k, e] for e in range(4))
        terms = jnp.concatenate(
            [
                join(h00 * t0 + h01 * t1, h00 * f0 + h10 * f1),
                join(h10 * t0 + h11 * t1, h01 * f0 + h11 * f1),
            ],
            axis=0,
        )
        return select_dot(terms, scatter_tab[k, :, cols], 2)

    s, u = [start], [applied(diag_inverse, start)]
    s.append(inside_product(OWN, u[0]) + coupled(border, facing))
    u.append(applied(diag_inverse, s[1]))
    for half, part in enumerate(split(u[1])):
        x_out[half] = part
    vectors = [
        send(12, x_out, x_in.at[1 - core], across),
        send(14, x_out.at[0], y_in.at[1], prev2),
        send(15, x_out.at[1], y_in.at[0], nxt2),
        send(13, x_out, x_in.at[core], mate),
    ]

    told(1)
    tell(2)

    sums = [inner(u[k // 2], s[k - k // 2]) for k in range(3)]

    for copy in far:
        copy.wait_recv()
    inside = inside_product(OWN, u[1])
    outer_border, side_inverse = [], []
    for k in range(2):
        index = w_in[k, 2 * scen :]
        index_tables(k, index[4:5, :wide], index[0:1], index[1:2])
        volts = join(a_in[k, 0, : 2 * scen], a_in[k, 1, : 2 * scen])
        local_blocks(k, volts, w_in[k, :scen], w_in[k, scen : 2 * scen], index[5:6], index[6:7])
        parts, _, fields = coupling(a_in[k, k], f_in[k])
        outer_border.append(fields)
        outside = inverse_of(b_in[k, k, : 3 * scen], parts)
        near = [split(f)[k] for f in facing_inverse]
        side_inverse.append([join(f, g) if k else join(g, f) for f, g in zip(near, outside)])

    for copy in vectors:
        copy.wait_recv()
    side = [join(x_in[k, 0], x_in[k, 1]) for k in range(2)]
    for j in (2, 3):
        facing = join(split(side[0])[1], split(side[1])[0])
        s.append(inside + coupled(border, facing))
        back = split(coupled(border_back, u[-1]))
        for k in range(2):
            if j == 2:
                outside = coupled(outer_border[k], y_in[k])
                product = inside_product(k, side[k]) + (join(back[k], outside) if k else join(outside, back[k]))
                side[k] = applied(side_inverse[k], product)
            else:
                cols = slice(0, LANES) if k else slice(LANES, wide)
                product = inside_product(k, side[k], cols) + back[k]
                side[k] = applied([f[:, cols] for f in side_inverse[k]], product)
        u.append(applied(diag_inverse, s[-1]))
        inside = inside_product(OWN, u[-1])
    s.append(inside + coupled(border, join(*side)))

    def all_sum(tile, meanwhile):
        red_a[pl.ds(member, 1)] = tile[None]
        copies = []
        for d, peer in enumerate(peers_a):
            copy = pltpu.make_async_remote_copy(
                src_ref=red_a.at[member],
                dst_ref=red_a.at[member],
                send_sem=a_send.at[d],
                recv_sem=a_recv.at[d],
                device_id={"net": peer},
                device_id_type=MESH,
            )
            copy.start()
            copies.append(copy)
        ahead = meanwhile()
        for copy in copies:
            copy.wait_recv()
        pending.extend(copies)
        total = red_a[0]
        for k in range(1, group):
            total = total + red_a[k]
        red_b[pl.ds(block, 1)] = total[None]
        copies = []
        for d, peer in enumerate(peers_b):
            copy = pltpu.make_async_remote_copy(
                src_ref=red_b.at[block],
                dst_ref=red_b.at[block],
                send_sem=b_send.at[d],
                recv_sem=b_recv.at[d],
                device_id={"net": peer},
                device_id_type=MESH,
            )
            copy.start()
            copies.append(copy)
        for copy in copies:
            copy.wait_recv()
        pending.extend(copies)
        total = red_b[0]
        for k in range(1, outer):
            total = total + red_b[k]
        return total, ahead

    told(2)
    sums += [inner(u[k // 2], s[k - k // 2]) for k in range(3, 2 * ITERS)]
    def bus_order():
        return [select_dot(v, to_bus, 3) for v in u], [select_dot(v, to_bus, 3) for v in s]

    total, (u, s) = all_sum(jnp.concatenate([pack(sums[:4]), pack(sums[4:])], axis=0), bus_order)
    moments = [total[k // 4 : k // 4 + 1] for k in range(2 * ITERS)]
    moments = [pltpu.roll(m, LANES - 32 * (k % 4), 1) if k % 4 else m for k, m in enumerate(moments)]
    gram = {(i, j): moments[i + j] + moments[i + j + 1] for i in range(ITERS) for j in range(i, ITERS)}
    w = unpack(galerkin(gram, moments[ITERS:], ITERS))
    w = [jnp.concatenate([jnp.concatenate([c, c], axis=1)] * 2, axis=0) for c in w]
    step = (1.0 + w[0]) * u[0] + (w[1] - 1.0) * u[1] + (1.0 + w[2]) * u[2] + (w[3] - 1.0) * u[3]
    residual = (1.0 - w[3]) * s[4] - (w[2] + w[3]) * s[3] - (w[1] + w[2]) * s[2] - (w[0] + w[1]) * s[1] - w[0] * s[0]
    for c in range(2):
        x_ref[c] = step[c * scen : (c + 1) * scen, :buses]
        r_ref[c] = residual[c * scen : (c + 1) * scen, :buses]

    for copy in pending:
        copy.wait_send()


def body(
    n,
    volt_mag,
    volt_ang,
    gradient,
    branch_from,
    branch_to,
    branch_count,
    boundary,
    conductance,
    susceptance,
    duals,
    slacks,
    gen_bus,
    gen_curvature,
):
    buses, scen = volt_mag.shape
    slots = branch_from.shape[0]
    span = -(-slots // LANES) * LANES
    group = 16 if n % 16 == 0 and n > 16 else 4 if n % 4 == 0 else 1
    outer = n // group
    row = lambda a: a.reshape(1, -1)
    rows = 4 * scen + 8
    dma = lambda *shape: pltpu.SemaphoreType.DMA(shape)
    operands = (
        volt_mag.T,
        volt_ang.T,
        gradient.transpose(1, 2, 0),
        branch_from,
        branch_to,
        branch_count,
        row(boundary),
        conductance,
        susceptance,
        duals.transpose(0, 2, 1),
        slacks.transpose(0, 2, 1),
        row(gen_bus),
        row(gen_curvature),
    )
    both = pl.pallas_call(
        functools.partial(kernel, n, group),
        out_shape=pltpu.VMEM((2, 2, scen, buses), F32),
        in_specs=[pl.BlockSpec(memory_space=pltpu.HBM)] * 13,
        out_specs=pl.BlockSpec(memory_space=pltpu.VMEM),
        scratch_shapes=[
            *(pltpu.VMEM(a.shape, a.dtype) for a in operands),
            dma(13),
            pltpu.VMEM((8, span), F32),
            pltpu.VMEM((8, span), F32),
            pltpu.VMEM((4 * scen, 2 * LANES), F32),
            pltpu.VMEM((3, 2 * LANES, 2 * span), BF16),
            pltpu.VMEM((3, 2 * span, 2 * LANES), BF16),
            pltpu.VMEM((3, 4, scen, span), F32),
            pltpu.VMEM((2, rows, LANES), F32),
            pltpu.VMEM((2, 2, rows, LANES), F32),
            pltpu.VMEM((2, rows, LANES), F32),
            pltpu.VMEM((2, 5 * scen, LANES), F32),
            pltpu.VMEM((2, 2, 5 * scen, LANES), F32),
            pltpu.VMEM((2 * scen + 8, span), F32),
            pltpu.VMEM((2, 2 * scen + 8, span), F32),
            pltpu.VMEM((2, 2 * scen, LANES), F32),
            pltpu.VMEM((2, 2, 2 * scen, LANES), F32),
            pltpu.VMEM((2, 2 * scen, LANES), F32),
            pltpu.VMEM((group, 2, LANES), F32),
            pltpu.VMEM((outer, 2, LANES), F32),
            dma(16),
            dma(16),
            dma(group),
            dma(group),
            dma(outer),
            dma(outer),
            pltpu.SemaphoreType.REGULAR((3,)),
        ],
        compiler_params=pltpu.CompilerParams(
            collective_id=0, has_side_effects=True, vmem_limit_bytes=62 * 1024 * 1024
        ),
        name="newton",
    )(*operands)
    return both[0].transpose(2, 0, 1), both[1].transpose(2, 0, 1)


def solution(mesh):
    placed = (
        P("net", "scen"),
        P("net", "scen"),
        P("net", None, "scen"),
        P("net"),
        P("net"),
        P("net"),
        P("net"),
        P("net"),
        P("net"),
        P(None, "net", "scen"),
        P(None, "net", "scen"),
        P("net"),
        P("net"),
    )
    return jax.shard_map(
        functools.partial(body, mesh.shape["net"]),
        mesh=mesh,
        in_specs=placed,
        out_specs=(P("net", None, "scen"), P("net", None, "scen")),
        check_vma=False,
    )
```

```python
import functools

import jax
import jax.numpy as jnp
from jax import lax
from jax.experimental import pallas as pl
from jax.experimental.pallas import tpu as pltpu
from jax.sharding import PartitionSpec as P

MESH = pl.DeviceIdType.MESH
F32, BF16 = jnp.float32, jnp.bfloat16
ITERS = 4
LANES = 128
OWN = 2

barrier_weight = 0.01
volt_low = 0.9
volt_high = 1.1
angle_reg = 0.5


def sine_cosine(angle):
    square = angle * angle
    sine = 1.0 / 6227020800.0
    for term in (-1.0 / 39916800.0, 1.0 / 362880.0, -1.0 / 5040.0, 1.0 / 120.0, -1.0 / 6.0, 1.0):
        sine = sine * square + term
    cosine = -1.0 / 87178291200.0
    for term in (1.0 / 479001600.0, -1.0 / 3628800.0, 1.0 / 40320.0, -1.0 / 720.0, 1.0 / 24.0, -0.5, 1.0):
        cosine = cosine * square + term
    return sine * angle, cosine


def branch_blocks(mag_from, mag_to, sine, cosine, conduct, suscept, weight_p, weight_q):
    along = conduct * cosine + suscept * sine
    across = conduct * sine - suscept * cosine
    cross = mag_from * mag_to
    jp = (2.0 * conduct * mag_from - mag_to * along, cross * across, -mag_from * along, -cross * across)
    jq = (-2.0 * suscept * mag_from - mag_to * across, -cross * along, -mag_from * across, cross * along)
    wp = [weight_p * j for j in jp]
    wq = [weight_q * j for j in jq]

    def entry(i, j):
        return wp[i] * jp[j] + wq[i] * jq[j]

    return (
        (entry(0, 0), entry(0, 1), entry(1, 1)),
        (entry(2, 2), entry(2, 3), entry(3, 3)),
        (entry(0, 2), entry(0, 3), entry(1, 2), entry(1, 3)),
    )


def pieces(values, terms):
    out = []
    for _ in range(terms - 1):
        head = values.astype(BF16)
        out.append(head)
        values = values - head.astype(F32)
    return jnp.concatenate(out + [values.astype(BF16)], axis=0)


def select_dot(values, table, terms):
    rows = values.shape[0]
    out = jnp.dot(pieces(values, terms), table, preferred_element_type=F32)
    total = out[(terms - 1) * rows :]
    for k in range(terms - 2, -1, -1):
        total = total + out[k * rows : (k + 1) * rows]
    return total


def inner(left, right):
    product = left * right
    half = product.shape[0] // 2
    product = product[:half] + product[half:]
    return product[:, :LANES] + product[:, LANES:]


def pack(parts):
    return jnp.sum(jnp.transpose(jnp.concatenate(parts, axis=0)), axis=0, keepdims=True)


def unpack(rows):
    lane = lax.broadcasted_iota(jnp.int32, (1, LANES), 1)
    joined = rows[0]
    for k in range(1, len(rows)):
        joined = jnp.where(lane < 32 * k, joined, pltpu.roll(rows[k], 32 * k, 1))
    columns = jnp.transpose(jnp.broadcast_to(joined, (LANES, LANES)))
    return [columns[32 * k : 32 * k + 32] for k in range(len(rows))]


def galerkin(gram, rhs, n):
    a = {(i, j): gram[(min(i, j), max(i, j))] for i in range(n) for j in range(n)}
    rhs = list(rhs)
    low, inv = {}, {}
    for k in range(n):
        live = a[(k, k)] > 1e-7 * gram[(k, k)]
        inv[k] = jnp.where(live, 1.0 / jnp.where(live, a[(k, k)], 1.0), 0.0)
        for i in range(k + 1, n):
            low[(i, k)] = a[(i, k)] * inv[k]
            for j in range(k + 1, i + 1):
                a[(i, j)] = a[(i, j)] - low[(i, k)] * a[(j, k)]
                a[(j, i)] = a[(i, j)]
            rhs[i] = rhs[i] - low[(i, k)] * rhs[k]
    out = [None] * n
    for k in reversed(range(n)):
        value = rhs[k] * inv[k]
        for i in range(k + 1, n):
            value = value - low[(i, k)] * out[i]
        out[k] = value
    return out


def partners(n):
    return (-1, 1, -2, 2, -16, 16) if n > 32 else (-1, 1, -2, 2)


def kernel(
    n,
    group,
    *refs,
):
    inputs, o_ref, loaded, rest = refs[:13], refs[13], refs[14:27], refs[27:]
    x_ref, r_ref = o_ref.at[0], o_ref.at[1]
    load_sem = rest[0]
    me = lax.axis_index("net")
    neighbours = [lax.rem(me + n + d, n) for d in partners(n)]
    for peer in neighbours:
        pl.semaphore_signal(pltpu.get_barrier_semaphore(), inc=1, device_id={"net": peer}, device_id_type=MESH)
    loads = []
    for k, (source, target) in enumerate(zip(inputs, loaded)):
        copy = pltpu.make_async_copy(source, target, load_sem.at[k])
        copy.start()
        loads.append(copy)
    solve(n, group, loads, *loaded, x_ref, r_ref, *rest[1:])


def solve(
    n,
    group,
    loads,
    vm_ref,
    va_ref,
    grad_ref,
    from_ref,
    to_ref,
    count_ref,
    bound_ref,
    g_ref,
    b_ref,
    dual_ref,
    slack_ref,
    gbus_ref,
    gcur_ref,
    x_ref,
    r_ref,
    irow,
    frow,
    vin,
    gather_tab,
    scatter_tab,
    blocks,
    a_out,
    a_in,
    f_in,
    b_out,
    b_in,
    w_out,
    w_in,
    x_out,
    x_in,
    y_in,
    red_a,
    red_b,
    send_sem,
    recv_sem,
    a_send,
    a_recv,
    b_send,
    b_recv,
    known_sem,
):
    scen, buses = vm_ref.shape
    slots = from_ref.shape[-1]
    ghost = buses // 2
    wide = 2 * LANES
    span = gather_tab.shape[2] // 2
    gens = gbus_ref.shape[1]
    outer = n // group
    me = lax.axis_index("net")
    prev, nxt, prev2, nxt2 = [lax.rem(me + n + d, n) for d in (-1, 1, -2, 2)]
    member = lax.rem(me, group)
    block = lax.div(me, group)
    peers_a = [block * group + lax.rem(member + d, group) for d in range(1, group)]
    peers_b = [lax.rem(block + d, outer) * group + member for d in range(1, outer)]

    barrier = pltpu.get_barrier_semaphore()
    spans = [[d for d in step if d < n // 2] for step in ((2, 16), (4, 32), (8,))]

    def tell(step):
        for d in spans[step]:
            for at in (n - d, d):
                pl.semaphore_signal(
                    known_sem.at[step], inc=1, device_id={"net": lax.rem(me + at, n)}, device_id_type=MESH
                )

    def told(step):
        if spans[step]:
            pl.semaphore_wait(known_sem.at[step], 2 * len(spans[step]))

    core = lax.rem(me, 2)
    mate = me + 1 - 2 * core
    across = lax.rem(me + n - 1 + 2 * core, n)
    beyond_mate = lax.rem(me + n + 2 - 4 * core, n)
    pending = []

    def send(message, source, target, peer):
        copy = pltpu.make_async_remote_copy(
            src_ref=source,
            dst_ref=target,
            send_sem=send_sem.at[message],
            recv_sem=recv_sem.at[message],
            device_id={"net": peer},
            device_id_type=MESH,
        )
        copy.start()
        pending.append(copy)
        return copy

    for copy in loads:
        copy.wait()

    irow[...] = jnp.full(irow.shape, -1.0, F32)
    irow[0:1, :slots] = from_ref[...].reshape(1, slots).astype(F32)
    irow[1:2, :slots] = to_ref[...].reshape(1, slots).astype(F32)
    irow[2:3, :buses] = bound_ref[...].astype(F32)
    irow[3:4, :gens] = gbus_ref[...].astype(F32)
    frow[...] = jnp.zeros(frow.shape, F32)
    frow[0:1, :slots] = g_ref[...].reshape(1, slots)
    frow[1:2, :slots] = b_ref[...].reshape(1, slots)
    frow[2:3, :gens] = gcur_ref[...]
    from_row, to_row = irow[0:1, :], irow[1:2, :]
    lane_i = lax.broadcasted_iota(jnp.int32, (8, wide), 1)
    lane = lane_i.astype(F32)
    plain = irow[0:8, :wide]
    rolled = pltpu.roll(plain, LANES - ghost, 1)
    upper = (lane_i >= LANES) & (lane_i < LANES + ghost)
    place = jnp.where(lane_i < ghost, plain, jnp.where(upper, rolled, -2.0))[2:3]
    entry = jnp.where(lane_i < ghost, lane, jnp.where(upper, lane - (LANES - ghost), -1e6))[0:1]

    def column(row):
        return jnp.transpose(jnp.broadcast_to(row, (LANES, row.shape[1])))

    def hot(mask):
        return jnp.where(mask, 1.0, 0.0).astype(BF16)

    lanes_of = lambda row, t: row[:, t * LANES : (t + 1) * LANES]

    def index_tables(k, place, from_row, to_row):
        place_col, from_col, to_col = column(place), column(from_row), column(to_row)
        for t in range(span // LANES):
            gather_tab[k, :, t * LANES : (t + 1) * LANES] = hot(place_col == lanes_of(from_row, t))
            gather_tab[k, :, span + t * LANES : span + (t + 1) * LANES] = hot(place_col == lanes_of(to_row, t))
        for t in range(2):
            cols = slice(t * LANES, (t + 1) * LANES)
            scatter_tab[k, 0:span, cols] = hot(from_col == lanes_of(place, t))
            scatter_tab[k, span:, cols] = hot(to_col == lanes_of(place, t))
        return place_col, to_col

    place_col, to_col = index_tables(OWN, place, from_row, to_row)
    irow[4:5, :wide] = place
    cross_tab = jnp.concatenate([hot(to_col == lanes_of(entry, t) + buses) for t in range(2)], axis=1)
    bus_row = lane[0:1]
    bus_col = lax.broadcasted_iota(jnp.int32, (wide, LANES), 0).astype(F32)
    to_place = jnp.concatenate([hot(bus_col == lanes_of(place, t)) for t in range(2)], axis=1)
    to_bus = jnp.concatenate([hot(place_col == lanes_of(bus_row, t)) for t in range(2)], axis=1)

    vin[...] = jnp.zeros(vin.shape, F32)
    vin[0:scen, :buses] = vm_ref[...]
    vin[scen : 2 * scen, :buses] = va_ref[...]
    vin[2 * scen : 3 * scen, :buses] = grad_ref[0]
    vin[3 * scen : 4 * scen, :buses] = grad_ref[1]
    placed = select_dot(vin[...], to_place, 3)
    vm, va, start = placed[0:scen], placed[scen : 2 * scen], placed[2 * scen :]

    slot = lax.broadcasted_iota(jnp.int32, (1, slots), 1)
    live = jnp.where(slot < count_ref[...].reshape(1, 1), 1.0, 0.0)
    pad = jnp.zeros((scen, span - slots), F32)
    weight_p = jnp.concatenate([live * dual_ref[0] / slack_ref[0], pad], axis=1)
    weight_q = jnp.concatenate([live * dual_ref[1] / slack_ref[1], pad], axis=1)
    conduct, suscept = frow[0:1, :], frow[1:2, :]
    stacked = jnp.concatenate([weight_p, weight_q, frow[0:8, :]], axis=0)
    crossing = select_dot(stacked, cross_tab, 3)
    payload = jnp.concatenate([vm, va, crossing], axis=0)
    split = lambda v: (v[:, :LANES], v[:, LANES:])
    join = lambda a, b: jnp.concatenate([a, b], axis=1)
    for half, part in enumerate(split(payload)):
        a_out[half] = part

    pl.semaphore_wait(barrier, len(partners(n)))
    a_near = [
        send(0, a_out.at[core], a_in.at[1 - core, core], across),
        send(1, a_out.at[1 - core], a_in.at[core, 1 - core], mate),
    ]
    tell(0)

    def local_blocks(k, volts, weight_p, weight_q, conduct, suscept):
        ends = select_dot(volts, gather_tab[k], 3)
        sine, cosine = sine_cosine(ends[scen:, :span] - ends[scen:, span:])
        hff, htt, hft = branch_blocks(
            ends[:scen, :span], ends[:scen, span:], sine, cosine, conduct, suscept, weight_p, weight_q
        )
        for e in range(4):
            blocks[k, e] = hft[e]
        return hff, htt

    local = jnp.where((to_row >= 0.0) & (to_row < float(buses)), 1.0, 0.0)
    weight_p, weight_q = weight_p * local, weight_q * local
    hff, htt = local_blocks(OWN, placed[0 : 2 * scen], weight_p, weight_q, conduct, suscept)
    both = jnp.concatenate([join(a, b) for a, b in zip(hff, htt)], axis=0)
    diag = select_dot(both, scatter_tab[OWN], 3)
    gen = column(irow[3:4, :LANES])
    curve = column(frow[2:3, :LANES])
    gen_sum = join(
        *(jnp.sum(jnp.where(gen == lanes_of(place, t), curve, 0.0), axis=0, keepdims=True) for t in range(2))
    )
    low, high = vm - volt_low, volt_high - vm
    base_vv = barrier_weight / (low * low) + barrier_weight / (high * high) + gen_sum
    base_aa = angle_reg + gen_sum
    own = jnp.concatenate(
        [diag[0:scen] + base_vv, diag[scen : 2 * scen], diag[2 * scen :] + base_aa, start], axis=0
    )
    for half, part in enumerate(split(own)):
        b_out[half] = part
    b_near = [
        send(2, b_out.at[core], b_in.at[1 - core, core], across),
        send(3, b_out.at[1 - core], b_in.at[core, 1 - core], mate),
    ]

    w_out[0:scen] = weight_p
    w_out[scen : 2 * scen] = weight_q
    irow[5:7] = frow[0:2]
    w_out[2 * scen :] = irow[...]
    rows = pl.ds(0, 3 * scen)
    far = [
        send(8, a_out.at[1 - core], f_in.at[core], beyond_mate),
        send(4, w_out, w_in.at[1], prev),
        send(5, w_out, w_in.at[0], nxt),
        send(6, a_out.at[1], a_in.at[1, 1], prev),
        send(7, a_out.at[0], a_in.at[0, 0], nxt),
        send(10, b_out.at[1, rows], b_in.at[1, 1, rows], prev),
        send(11, b_out.at[0, rows], b_in.at[0, 0, rows], nxt),
    ]

    def coupling(here, there):
        vm, va, p, q = (here[k * scen : (k + 1) * scen] for k in range(4))
        there_vm, there_va, there_p, there_q = (there[k * scen : (k + 1) * scen] for k in range(4))
        g, b = here[4 * scen : 4 * scen + 1], here[4 * scen + 1 : 4 * scen + 2]
        there_g, there_b = there[4 * scen : 4 * scen + 1], there[4 * scen + 1 : 4 * scen + 2]
        sine, cosine = sine_cosine(va - there_va)
        off, reach, (o00, o01, o10, o11) = branch_blocks(vm, there_vm, sine, cosine, g, b, p, q)
        root, on, (i00, i01, i10, i11) = branch_blocks(there_vm, vm, -sine, cosine, there_g, there_b, there_p, there_q)
        return (off, on), (reach, root), (o00 + i00, o01 + i10, o10 + i01, o11 + i11)

    def inverse_of(fields, parts):
        first, second = parts
        d00, d01, d11 = (fields[k * scen : (k + 1) * scen] + first[k] + second[k] for k in range(3))
        inverse = 1.0 / (d00 * d11 - d01 * d01)
        return d11 * inverse, -d01 * inverse, d00 * inverse

    def applied(fields, v):
        b00, b01, b11 = fields
        return jnp.concatenate([b00 * v[:scen] + b01 * v[scen:], b01 * v[:scen] + b11 * v[scen:]], axis=0)

    def coupled(c, v):
        v0, v1 = v[:scen], v[scen:]
        return jnp.concatenate([c[0] * v0 + c[1] * v1, c[2] * v0 + c[3] * v1], axis=0)

    told(0)
    tell(1)
    for copy in a_near:
        copy.wait_recv()
    far.append(send(9, a_in.at[core, 1 - core], f_in.at[core], mate))
    here_parts, there_parts, border = coupling(payload, join(a_in[0, 1], a_in[1, 0]))
    border_back = (border[0], border[2], border[1], border[3])
    diag_inverse = inverse_of(own, here_parts)

    for copy in b_near:
        copy.wait_recv()
    beyond = join(b_in[0, 1], b_in[1, 0])
    facing_inverse = inverse_of(beyond, there_parts)
    facing = applied(facing_inverse, beyond[3 * scen :])

    def inside_product(k, v, cols=slice(0, wide)):
        ends = select_dot(v, gather_tab[k], 2)
        f0, f1, t0, t1 = ends[:scen, :span], ends[scen:, :span], ends[:scen, span:], ends[scen:, span:]
        h00, h01, h10, h11 = (blocks[k, e] for e in range(4))
        terms = jnp.concatenate(
            [
                join(h00 * t0 + h01 * t1, h00 * f0 + h10 * f1),
                join(h10 * t0 + h11 * t1, h01 * f0 + h11 * f1),
            ],
            axis=0,
        )
        return select_dot(terms, scatter_tab[k, :, cols], 2)

    s, u = [start], [applied(diag_inverse, start)]
    s.append(inside_product(OWN, u[0]) + coupled(border, facing))
    u.append(applied(diag_inverse, s[1]))
    for half, part in enumerate(split(u[1])):
        x_out[half] = part
    vectors = [
        send(12, x_out, x_in.at[1 - core], across),
        send(14, x_out.at[0], y_in.at[1], prev2),
        send(15, x_out.at[1], y_in.at[0], nxt2),
        send(13, x_out, x_in.at[core], mate),
    ]

    told(1)
    tell(2)

    sums = [inner(u[k // 2], s[k - k // 2]) for k in range(3)]

    for copy in far:
        copy.wait_recv()
    inside = inside_product(OWN, u[1])
    outer_border, side_inverse = [], []
    for k in range(2):
        index = w_in[k, 2 * scen :]
        index_tables(k, index[4:5, :wide], index[0:1], index[1:2])
        volts = join(a_in[k, 0, : 2 * scen], a_in[k, 1, : 2 * scen])
        local_blocks(k, volts, w_in[k, :scen], w_in[k, scen : 2 * scen], index[5:6], index[6:7])
        parts, _, fields = coupling(a_in[k, k], f_in[k])
        outer_border.append(fields)
        outside = inverse_of(b_in[k, k, : 3 * scen], parts)
        near = [split(f)[k] for f in facing_inverse]
        side_inverse.append([join(f, g) if k else join(g, f) for f, g in zip(near, outside)])

    for copy in vectors:
        copy.wait_recv()
    side = [join(x_in[k, 0], x_in[k, 1]) for k in range(2)]
    for j in (2, 3):
        facing = join(split(side[0])[1], split(side[1])[0])
        s.append(inside + coupled(border, facing))
        back = split(coupled(border_back, u[-1]))
        for k in range(2):
            if j == 2:
                outside = coupled(outer_border[k], y_in[k])
                product = inside_product(k, side[k]) + (join(back[k], outside) if k else join(outside, back[k]))
                side[k] = applied(side_inverse[k], product)
            else:
                cols = slice(0, LANES) if k else slice(LANES, wide)
                product = inside_product(k, side[k], cols) + back[k]
                side[k] = applied([f[:, cols] for f in side_inverse[k]], product)
        u.append(applied(diag_inverse, s[-1]))
        inside = inside_product(OWN, u[-1])
    s.append(inside + coupled(border, join(*side)))

    def all_sum(tile, meanwhile):
        red_a[pl.ds(member, 1)] = tile[None]
        copies = []
        for d, peer in enumerate(peers_a):
            copy = pltpu.make_async_remote_copy(
                src_ref=red_a.at[member],
                dst_ref=red_a.at[member],
                send_sem=a_send.at[d],
                recv_sem=a_recv.at[d],
                device_id={"net": peer},
                device_id_type=MESH,
            )
            copy.start()
            copies.append(copy)
        ahead = meanwhile()
        for copy in copies:
            copy.wait_recv()
        pending.extend(copies)
        total = red_a[0]
        for k in range(1, group):
            total = total + red_a[k]
        red_b[pl.ds(block, 1)] = total[None]
        copies = []
        for d, peer in enumerate(peers_b):
            copy = pltpu.make_async_remote_copy(
                src_ref=red_b.at[block],
                dst_ref=red_b.at[block],
                send_sem=b_send.at[d],
                recv_sem=b_recv.at[d],
                device_id={"net": peer},
                device_id_type=MESH,
            )
            copy.start()
            copies.append(copy)
        for copy in copies:
            copy.wait_recv()
        pending.extend(copies)
        total = red_b[0]
        for k in range(1, outer):
            total = total + red_b[k]
        return total, ahead

    told(2)
    sums += [inner(u[k // 2], s[k - k // 2]) for k in range(3, 2 * ITERS)]
    def bus_order():
        return [select_dot(v, to_bus, 3) for v in u], [select_dot(v, to_bus, 3) for v in s]

    total, (u, s) = all_sum(jnp.concatenate([pack(sums[:4]), pack(sums[4:])], axis=0), bus_order)
    moments = [total[k // 4 : k // 4 + 1] for k in range(2 * ITERS)]
    moments = [pltpu.roll(m, LANES - 32 * (k % 4), 1) if k % 4 else m for k, m in enumerate(moments)]
    gram = {(i, j): moments[i + j] + moments[i + j + 1] for i in range(ITERS) for j in range(i, ITERS)}
    w = unpack(galerkin(gram, moments[ITERS:], ITERS))
    w = [jnp.concatenate([jnp.concatenate([c, c], axis=1)] * 2, axis=0) for c in w]
    step = (1.0 + w[0]) * u[0] + (w[1] - 1.0) * u[1] + (1.0 + w[2]) * u[2] + (w[3] - 1.0) * u[3]
    residual = (1.0 - w[3]) * s[4] - (w[2] + w[3]) * s[3] - (w[1] + w[2]) * s[2] - (w[0] + w[1]) * s[1] - w[0] * s[0]
    for c in range(2):
        x_ref[c] = step[c * scen : (c + 1) * scen, :buses]
        r_ref[c] = residual[c * scen : (c + 1) * scen, :buses]

    for copy in pending:
        copy.wait_send()


def body(
    n,
    volt_mag,
    volt_ang,
    gradient,
    branch_from,
    branch_to,
    branch_count,
    boundary,
    conductance,
    susceptance,
    duals,
    slacks,
    gen_bus,
    gen_curvature,
):
    buses, scen = volt_mag.shape
    slots = branch_from.shape[0]
    span = -(-slots // LANES) * LANES
    group = 16 if n % 16 == 0 and n > 16 else 4 if n % 4 == 0 else 1
    outer = n // group
    row = lambda a: a.reshape(1, -1)
    rows = 4 * scen + 8
    dma = lambda *shape: pltpu.SemaphoreType.DMA(shape)
    operands = (
        volt_mag.T,
        volt_ang.T,
        gradient.transpose(1, 2, 0),
        branch_from,
        branch_to,
        branch_count,
        row(boundary),
        conductance,
        susceptance,
        duals.transpose(0, 2, 1),
        slacks.transpose(0, 2, 1),
        row(gen_bus),
        row(gen_curvature),
    )
    both = pl.pallas_call(
        functools.partial(kernel, n, group),
        out_shape=pltpu.VMEM((2, 2, scen, buses), F32),
        in_specs=[pl.BlockSpec(memory_space=pltpu.HBM)] * 13,
        out_specs=pl.BlockSpec(memory_space=pltpu.VMEM),
        scratch_shapes=[
            *(pltpu.VMEM(a.shape, a.dtype) for a in operands),
            dma(13),
            pltpu.VMEM((8, span), F32),
            pltpu.VMEM((8, span), F32),
            pltpu.VMEM((4 * scen, 2 * LANES), F32),
            pltpu.VMEM((3, 2 * LANES, 2 * span), BF16),
            pltpu.VMEM((3, 2 * span, 2 * LANES), BF16),
            pltpu.VMEM((3, 4, scen, span), F32),
            pltpu.VMEM((2, rows, LANES), F32),
            pltpu.VMEM((2, 2, rows, LANES), F32),
            pltpu.VMEM((2, rows, LANES), F32),
            pltpu.VMEM((2, 5 * scen, LANES), F32),
            pltpu.VMEM((2, 2, 5 * scen, LANES), F32),
            pltpu.VMEM((2 * scen + 8, span), F32),
            pltpu.VMEM((2, 2 * scen + 8, span), F32),
            pltpu.VMEM((2, 2 * scen, LANES), F32),
            pltpu.VMEM((2, 2, 2 * scen, LANES), F32),
            pltpu.VMEM((2, 2 * scen, LANES), F32),
            pltpu.VMEM((group, 2, LANES), F32),
            pltpu.VMEM((outer, 2, LANES), F32),
            dma(16),
            dma(16),
            dma(group),
            dma(group),
            dma(outer),
            dma(outer),
            pltpu.SemaphoreType.REGULAR((3,)),
        ],
        compiler_params=pltpu.CompilerParams(
            collective_id=0, has_side_effects=True, vmem_limit_bytes=62 * 1024 * 1024
        ),
        name="newton",
    )(*operands)
    return both[0].transpose(2, 0, 1), both[1].transpose(2, 0, 1)


def solution(mesh):
    placed = (
        P("net", "scen"),
        P("net", "scen"),
        P("net", None, "scen"),
        P("net"),
        P("net"),
        P("net"),
        P("net"),
        P("net"),
        P("net"),
        P(None, "net", "scen"),
        P(None, "net", "scen"),
        P("net"),
        P("net"),
    )
    return jax.shard_map(
        functools.partial(body, mesh.shape["net"]),
        mesh=mesh,
        in_specs=placed,
        out_specs=(P("net", None, "scen"), P("net", None, "scen")),
        check_vma=False,
    )
```
